512 devices in a mesh: dp: 8 (over y, x_lo), ctx: 64 (over z, x_hi, core).
Axes of the slice: x: 4 (x_hi: 2, x_lo: 2; x = x_hi * 2 + x_lo), y: 4, z: 16, core: 2. Of those that a mesh axis runs over, the one named last changes fastest.
Arguments:
- events: bfloat16 [8, 16384, 1024], P('dp', 'ctx'), may hold values from -6 to 6
- w_query: bfloat16 [1024, 512], replicated, may hold values from -0.1875 to 0.1875
- w_key: bfloat16 [1024, 512], replicated, may hold values from -0.1875 to 0.1875
- values: bfloat16 [8, 16384, 512], P('dp', 'ctx'), may hold values from -6 to 6
- grad_out: bfloat16 [8, 16384, 512], P('dp', 'ctx'), may hold values from -6 to 6
- lengths: int32 [8, 32], P('dp'), may hold values from 1 to 768, 16384 in all within a row
- stream_shift: int32 [8], P('dp'), may hold values from 0 to 16383
- block_keep: int32 [8, 128], P('dp'), may hold values 0 or 1
Outputs:
- attended: bfloat16 [8, 16384, 512], P('dp', 'ctx')
- grad_values: bfloat16 [8, 16384, 512], P('dp', 'ctx')
- grad_wq: bfloat16 [1024, 512], P('ctx')
- grad_wk: bfloat16 [1024, 512], P('ctx')
The draws below stay inside these ranges and needn't reach their ends.
Inputs may be any that keep to these rules, and one draw needn't show every extreme that they name: The lengths of a stream sum to 16384; the longest is exactly 768.
All inputs are finite; a program needn't handle non-finite values. No bound on the sum of `block_keep` on one device may be relied on, other than what follows from the above.
Results may differ from the reference program's by a relative error of at most 0.011.
Values may be sent and summed in bfloat16 or wider, within the bound.
A program may use at most 64 MiB of HBM per device.

```python
import math
import jax
import jax.numpy as jnp
import numpy as np
from jax import lax

D = 1024
HEADS = 4
HD = 128
ROWS_DEV = 256
SPAN = 3
BLOCK = 128
STREAMS = 8
L = 16384
USERS = 32
MAXLEN = 768
NBLK = 128


def touch_ends(result, key, low, high):
    extent = result.shape
    index_at = [jax.random.randint(jax.random.fold_in(key, axis), (), 0, extent[axis]) for axis in range(len(extent))]
    result = result.at[tuple(index_at)].set(low)
    longest = extent.index(max(extent))
    index_at[longest] = (index_at[longest] + 1) % extent[longest]
    return result.at[tuple(index_at)].set(high)


def levels(key, extent, cuts, smallest, top_value):
    def one(dim, blocks):
        draws = jax.random.uniform(jax.random.fold_in(jax.random.fold_in(key, 6), dim), (blocks,), jnp.float32, smallest / len(cuts), top_value / len(cuts))
        return jnp.repeat(jnp.exp(draws), extent[dim] // blocks).reshape((-1,) + (1,) * (len(extent) - dim - 1))

    level = one(*cuts[0])
    for cut in cuts[1:]:
        level = level * one(*cut)
    return level


def split_up(amount, total, most, slope):
    weights = [(1 << 20) // math.isqrt(standing ** slope) + 1 for standing in range(2, amount + 1)]
    surplus, counts = total - most - (amount - 1), [1] * (amount - 1)
    while surplus > 0:
        free = [i for i in range(amount - 1) if counts[i] < most]
        pool, left = sum([weights[i] for i in free]), surplus
        for i in free:
            more = min(most - counts[i], max(1, left * weights[i] // pool), surplus)
            counts[i] = counts[i] + more
            surplus = surplus - more
    return np.array([most] + counts)


def uneven_parts(key, amount, total, limit, lean):
    if amount == 2:
        one = jax.random.randint(key, (), max(1, total - limit), min(limit, total - 1) + 1)
        return jnp.stack([one, total - one])
    sizes = jnp.asarray(split_up(amount, total, limit, lean), jnp.int32)
    twos = (amount - 1) // 2
    giver, taker = sizes[1:1 + 2 * twos:2], sizes[2:2 + 2 * twos:2]
    room = jnp.minimum(giver - 1, limit - taker)
    moved = jax.random.randint(jax.random.fold_in(key, 1), (twos,), 0, 1 << 20) % (room + 1)
    sizes = sizes.at[1:1 + 2 * twos:2].set(giver - moved).at[2:2 + 2 * twos:2].set(taker + moved)
    return sizes[jax.random.permutation(jax.random.fold_in(key, 2), amount)]


def bell_draw(own_key, dims, deviation, most, pieces=(), held_as=jnp.bfloat16):
    result = jax.random.normal(own_key, dims, jnp.float32) * deviation
    if len(pieces) > 0:
        result = levels(own_key, dims, pieces, -0.22, 0.18) * result
    return jnp.clip(result, min=-most, max=most).astype(held_as)


def setup_inputs(seed: int = 0) -> dict:
    keys = jax.random.split(jax.random.key(seed), 9)
    events = bell_draw(keys[0], (STREAMS, L, D), 1.0, 6.0, ((0, 8), (1, 64)))
    w_query = bell_draw(keys[1], (D, HEADS * HD), D ** -0.5, 0.1875)
    w_key = bell_draw(keys[2], (D, HEADS * HD), D ** -0.5, 0.1875)
    values = bell_draw(keys[3], (STREAMS, L, HEADS * HD), 1.0, 6.0, ((0, 8), (1, 64)))
    grad_out = bell_draw(keys[4], (STREAMS, L, HEADS * HD), 1.0, 6.0, ((0, 8), (1, 64)))
    lengths = jax.vmap(lambda own: uneven_parts(own, USERS, L, MAXLEN, 1))(jax.random.split(keys[5], STREAMS)).reshape((STREAMS, USERS)).astype(jnp.int32)
    stream_shift = touch_ends(jax.random.randint(keys[6], (STREAMS,), 0, L), jax.random.fold_in(keys[6], 1), 0, L - 1).astype(jnp.int32)
    block_keep = touch_ends((jax.random.randint(keys[7], (STREAMS, NBLK), 0, 4) < 3).astype(jnp.int32), jax.random.fold_in(keys[7], 1), 0, 1)
    return {"events": events, "w_query": w_query, "w_key": w_key, "values": values, "grad_out": grad_out, "lengths": lengths, "stream_shift": stream_shift, "block_keep": block_keep}


def tile_terms(query, grad, key, value, valid, scale, alpha):
    q32 = query.astype(jnp.float32)
    k32 = key.astype(jnp.float32)
    v32 = value.astype(jnp.float32)
    g32 = grad.astype(jnp.float32)
    z = jnp.einsum("bqhd,bkhd->bhqk", q32, k32) * alpha
    sig = jax.nn.sigmoid(z)
    weight = valid[:, None, :, :].astype(jnp.float32) * scale
    att = (z * sig * weight).astype(jnp.bfloat16)
    a32 = att.astype(jnp.float32)
    out = jnp.einsum("bhqk,bkhd->bqhd", a32, v32)
    dprod = jnp.einsum("bqhd,bkhd->bhqk", g32, v32)
    dsc = (dprod * sig * (1.0 + z * (1.0 - sig)) * weight * alpha).astype(jnp.bfloat16)
    d32 = dsc.astype(jnp.float32)
    dquery = jnp.einsum("bhqk,bkhd->bqhd", d32, k32)
    dkey = jnp.einsum("bhqk,bqhd->bkhd", d32, q32)
    dvalue = jnp.einsum("bhqk,bqhd->bkhd", a32, g32)
    return out, dquery, dkey, dvalue


def reference(events, w_query, w_key, values, grad_out, lengths, stream_shift, block_keep):
    alpha = 1.0 / (HD ** 0.5)
    scale = 1.0 / (MAXLEN ** 0.5)

    def one_stream(packed):
        x, vals, grads, lens, shift, keep = packed
        total = x.shape[0]
        nblocks = total // ROWS_DEV
        query = jnp.dot(x, w_query, preferred_element_type=jnp.float32).astype(jnp.bfloat16)
        key = jnp.dot(x, w_key, preferred_element_type=jnp.float32).astype(jnp.bfloat16)
        q4 = query.reshape(nblocks, ROWS_DEV, HEADS, HD)
        k4 = key.reshape(nblocks, ROWS_DEV, HEADS, HD)
        v4 = vals.reshape(nblocks, ROWS_DEV, HEADS, HD)
        g4 = grads.reshape(nblocks, ROWS_DEV, HEADS, HD)
        stored = jnp.arange(total, dtype=jnp.int32)
        pos = jnp.remainder(stored - shift, total).astype(jnp.int32)
        ends = jnp.cumsum(lens).astype(jnp.int32)
        user = jnp.sum((pos[:, None] >= ends[None, :]).astype(jnp.int32), axis=1).astype(jnp.int32)
        kept = keep[(pos // BLOCK).astype(jnp.int32)] > 0
        pos = pos.reshape(nblocks, ROWS_DEV)
        user = user.reshape(nblocks, ROWS_DEV)
        kept = kept.reshape(nblocks, ROWS_DEV)
        out = jnp.zeros((nblocks, ROWS_DEV, HEADS, HD), jnp.float32)
        dq = jnp.zeros_like(out)
        dk = jnp.zeros_like(out)
        dv = jnp.zeros_like(out)
        for step in range(SPAN + 1):
            kr = jnp.roll(k4, step, axis=0)
            vr = jnp.roll(v4, step, axis=0)
            posk = jnp.roll(pos, step, axis=0)
            userk = jnp.roll(user, step, axis=0)
            keptk = jnp.roll(kept, step, axis=0)
            valid = (user[:, :, None] == userk[:, None, :]) & (posk[:, None, :] <= pos[:, :, None]) & keptk[:, None, :]
            o, a, b, c = tile_terms(q4, g4, kr, vr, valid, scale, alpha)
            out = out + o
            dq = dq + a
            dk = dk + jnp.roll(b, -step, axis=0)
            dv = dv + jnp.roll(c, -step, axis=0)
        dq_b = dq.reshape(total, HEADS * HD).astype(jnp.bfloat16)
        dk_b = dk.reshape(total, HEADS * HD).astype(jnp.bfloat16)
        gq = jnp.dot(x.T, dq_b, preferred_element_type=jnp.float32)
        gk = jnp.dot(x.T, dk_b, preferred_element_type=jnp.float32)
        return (out.reshape(total, HEADS * HD).astype(jnp.bfloat16),
                dv.reshape(total, HEADS * HD).astype(jnp.bfloat16), gq, gk)

    attended, grad_values, gq, gk = lax.map(one_stream, (events, values, grad_out, lengths, stream_shift, block_keep))
    grad_wq = jnp.sum(gq, axis=0).astype(jnp.bfloat16)
    grad_wk = jnp.sum(gk, axis=0).astype(jnp.bfloat16)
    return (attended, grad_values, grad_wq, grad_wk)
```

```python
import jax
import jax.numpy as jnp
from jax import lax
from jax.sharding import PartitionSpec as P

HD = 128
SPAN = 3
BLOCK = 128
MAXLEN = 768


def shifted(value, axis, steps):
    count = lax.axis_size(axis)
    pairs = [(source, (source + steps) % count) for source in range(count)]
    return lax.ppermute(value, axis, pairs)


def scores(query, key, valid, scale, alpha):
    z = jnp.einsum("qhd,khd->hqk", query, key, preferred_element_type=jnp.float32) * alpha
    sig = jax.nn.sigmoid(z)
    weight = valid[None, :, :].astype(jnp.float32) * scale
    return z, sig, weight


def forward_terms(query, grad, key, value, valid, scale, alpha):
    z, sig, weight = scores(query, key, valid, scale, alpha)
    att = (z * sig * weight).astype(jnp.bfloat16)
    out = jnp.einsum("hqk,khd->qhd", att, value, preferred_element_type=jnp.float32)
    dprod = jnp.einsum("qhd,khd->hqk", grad, value, preferred_element_type=jnp.float32)
    dsc = (dprod * sig * (1.0 + z * (1.0 - sig)) * weight * alpha).astype(jnp.bfloat16)
    dquery = jnp.einsum("hqk,khd->qhd", dsc, key, preferred_element_type=jnp.float32)
    return out, dquery, att, dsc


def backward_terms(query, grad, key, value, valid, scale, alpha):
    z, sig, weight = scores(query, key, valid, scale, alpha)
    att = (z * sig * weight).astype(jnp.bfloat16)
    dprod = jnp.einsum("qhd,khd->hqk", grad, value, preferred_element_type=jnp.float32)
    dsc = (dprod * sig * (1.0 + z * (1.0 - sig)) * weight * alpha).astype(jnp.bfloat16)
    dkey = jnp.einsum("hqk,qhd->khd", dsc, query, preferred_element_type=jnp.float32)
    dvalue = jnp.einsum("hqk,qhd->khd", att, grad, preferred_element_type=jnp.float32)
    return dkey, dvalue


def body(events, w_query, w_key, values, grad_out, lengths, stream_shift, block_keep):
    rows = events.shape[1]
    features = w_query.shape[1]
    nheads = features // HD
    alpha = 1.0 / HD**0.5
    scale = 1.0 / MAXLEN**0.5
    local = events[0]
    queries = jnp.dot(local, w_query, preferred_element_type=jnp.float32).astype(jnp.bfloat16)
    keys = jnp.dot(local, w_key, preferred_element_type=jnp.float32).astype(jnp.bfloat16)
    cycle_size = lax.axis_size("ctx")
    myself = lax.axis_index("ctx")
    total = rows * cycle_size
    ends = jnp.cumsum(lengths[0])
    offset = stream_shift[0]
    keep = block_keep[0]
    blocks_all = jnp.arange(keep.shape[0], dtype=jnp.int32)
    within = jnp.arange(rows, dtype=jnp.int32)

    def describe(anchor):
        anchor = jnp.remainder(anchor, cycle_size)
        position = jnp.remainder(anchor * rows + within - offset, total)
        owner = jnp.sum((position[:, None] >= ends[None, :]).astype(jnp.int32), axis=1)
        which = position // BLOCK
        kept = (
            jnp.sum(jnp.where(which[:, None] == blocks_all[None, :], keep[None, :], 0), axis=1) > 0
        )
        return (position, owner, kept)

    def mask(qinfo, kinfo):
        return (
            (qinfo[1][:, None] == kinfo[1][None, :])
            & (kinfo[0][None, :] <= qinfo[0][:, None])
            & kinfo[2][None, :]
        )

    def split(packed):
        return (
            packed[:, :features].reshape(rows, nheads, HD),
            packed[:, features:].reshape(rows, nheads, HD),
        )

    kv = jnp.concatenate([keys, values[0]], axis=1)
    qg = jnp.concatenate([queries, grad_out[0]], axis=1)
    kv_from = [None] + [shifted(kv, "ctx", step) for step in range(1, SPAN + 1)]
    qg_from = [None] + [shifted(qg, "ctx", -step) for step in range(1, SPAN + 1)]

    q_me, g_me = split(qg)
    k_me, v_me = split(kv)
    info_me = describe(myself)
    out_acc, dq_acc, att0, dsc0 = forward_terms(
        q_me, g_me, k_me, v_me, mask(info_me, info_me), scale, alpha
    )
    dk_acc = jnp.einsum("hqk,qhd->khd", dsc0, q_me, preferred_element_type=jnp.float32)
    dv_acc = jnp.einsum("hqk,qhd->khd", att0, g_me, preferred_element_type=jnp.float32)
    for step in range(1, SPAN + 1):
        k_s, v_s = split(kv_from[step])
        o, a, _, _ = forward_terms(
            q_me, g_me, k_s, v_s, mask(info_me, describe(myself - step)), scale, alpha
        )
        out_acc = out_acc + o
        dq_acc = dq_acc + a
        q_s, g_s = split(qg_from[step])
        b, c = backward_terms(
            q_s, g_s, k_me, v_me, mask(describe(myself + step), info_me), scale, alpha
        )
        dk_acc = dk_acc + b
        dv_acc = dv_acc + c
    attended = out_acc.reshape(1, rows, features).astype(jnp.bfloat16)
    grad_values = dv_acc.reshape(1, rows, features).astype(jnp.bfloat16)
    dq_b = dq_acc.reshape(rows, features).astype(jnp.bfloat16)
    dk_b = dk_acc.reshape(rows, features).astype(jnp.bfloat16)
    joined = jnp.concatenate([dq_b, dk_b], axis=1)
    terms = jnp.einsum("rd,rf->df", local, joined, preferred_element_type=jnp.float32)
    mine = lax.psum_scatter(terms, "ctx", scatter_dimension=0, tiled=True)
    mine = lax.psum(mine, "dp")
    grad_wq = mine[:, :features].astype(jnp.bfloat16)
    grad_wk = mine[:, features:].astype(jnp.bfloat16)
    return (attended, grad_values, grad_wq, grad_wk)


def solution(mesh):
    placed = (
        P("dp", "ctx", None),
        P(),
        P(),
        P("dp", "ctx", None),
        P("dp", "ctx", None),
        P("dp", None),
        P("dp"),
        P("dp", None),
    )
    return jax.shard_map(
        body,
        mesh=mesh,
        in_specs=placed,
        out_specs=(P("dp", "ctx", None), P("dp", "ctx", None), P("ctx", None), P("ctx", None)),
        check_vma=False,
    )
```

```python
import jax
import jax.numpy as jnp
from jax import lax
from jax.sharding import PartitionSpec as P

HD = 128
SPAN = 3
BLOCK = 128
MAXLEN = 768


def shifted(value, axis, steps):
    count = lax.axis_size(axis)
    pairs = [(source, (source + steps) % count) for source in range(count)]
    return lax.ppermute(value, axis, pairs)


def exchange(value, axis, mask):
    count = lax.axis_size(axis)
    return lax.ppermute(value, axis, [(source, source ^ mask) for source in range(count)])


def pick(value, bit, axis):
    return (
        lax.dynamic_index_in_dim(value, bit, axis, keepdims=False),
        lax.dynamic_index_in_dim(value, 1 - bit, axis, keepdims=False),
    )


def reduce_rows(local, partner_events, joined, myself, cycle_size):
    width = local.shape[1]
    share = width // cycle_size
    core = myself % 2
    partner_joined = exchange(joined, "ctx", 1)
    both_events = jnp.concatenate([local, partner_events], axis=0)
    both_joined = jnp.concatenate([joined, partner_joined], axis=0)
    halves = both_events.reshape(both_events.shape[0], width // (2 * share), 2, share)
    kept = lax.dynamic_index_in_dim(halves, core, 2, keepdims=False).reshape(both_events.shape[0], width // 2)
    acc = jnp.dot(kept.T, both_joined, preferred_element_type=jnp.float32)
    acc = acc.reshape(width // (2 * share), share, joined.shape[1])
    mask = 2
    while mask < cycle_size:
        acc = acc.reshape(acc.shape[0] // 2, 2, share, joined.shape[1])
        keep_part, send_part = pick(acc, (myself // mask) % 2, 1)
        acc = keep_part + exchange(send_part, "ctx", mask)
        mask *= 2
    acc = acc.reshape(share, joined.shape[1])
    mask = 1
    while mask < lax.axis_size("dp"):
        acc = acc + exchange(acc, "dp", mask)
        mask *= 2
    return acc


def scores(query, key, valid, scale, alpha):
    z = jnp.einsum("qhd,khd->hqk", query, key, preferred_element_type=jnp.float32) * alpha
    sig = jax.nn.sigmoid(z)
    weight = valid[None, :, :].astype(jnp.float32) * scale
    return z, sig, weight


def forward_terms(query, grad, key, value, valid, scale, alpha):
    z, sig, weight = scores(query, key, valid, scale, alpha)
    att = (z * sig * weight).astype(jnp.bfloat16)
    out = jnp.einsum("hqk,khd->qhd", att, value, preferred_element_type=jnp.float32)
    dprod = jnp.einsum("qhd,khd->hqk", grad, value, preferred_element_type=jnp.float32)
    dsc = (dprod * sig * (1.0 + z * (1.0 - sig)) * weight * alpha).astype(jnp.bfloat16)
    dquery = jnp.einsum("hqk,khd->qhd", dsc, key, preferred_element_type=jnp.float32)
    return out, dquery, att, dsc


def backward_terms(query, grad, key, value, valid, scale, alpha):
    z, sig, weight = scores(query, key, valid, scale, alpha)
    att = (z * sig * weight).astype(jnp.bfloat16)
    dprod = jnp.einsum("qhd,khd->hqk", grad, value, preferred_element_type=jnp.float32)
    dsc = (dprod * sig * (1.0 + z * (1.0 - sig)) * weight * alpha).astype(jnp.bfloat16)
    dkey = jnp.einsum("hqk,qhd->khd", dsc, query, preferred_element_type=jnp.float32)
    dvalue = jnp.einsum("hqk,qhd->khd", att, grad, preferred_element_type=jnp.float32)
    return dkey, dvalue


def body(events, w_query, w_key, values, grad_out, lengths, stream_shift, block_keep):
    rows = events.shape[1]
    features = w_query.shape[1]
    nheads = features // HD
    alpha = 1.0 / HD**0.5
    scale = 1.0 / MAXLEN**0.5
    local = events[0]
    queries = jnp.dot(local, w_query, preferred_element_type=jnp.float32).astype(jnp.bfloat16)
    keys = jnp.dot(local, w_key, preferred_element_type=jnp.float32).astype(jnp.bfloat16)
    cycle_size = lax.axis_size("ctx")
    myself = lax.axis_index("ctx")
    total = rows * cycle_size
    ends = jnp.cumsum(lengths[0])
    offset = stream_shift[0]
    keep = block_keep[0]
    blocks_all = jnp.arange(keep.shape[0], dtype=jnp.int32)
    within = jnp.arange(rows, dtype=jnp.int32)

    def describe(anchor):
        anchor = jnp.remainder(anchor, cycle_size)
        position = jnp.remainder(anchor * rows + within - offset, total)
        owner = jnp.sum((position[:, None] >= ends[None, :]).astype(jnp.int32), axis=1)
        which = position // BLOCK
        kept = (
            jnp.sum(jnp.where(which[:, None] == blocks_all[None, :], keep[None, :], 0), axis=1) > 0
        )
        return (position, owner, kept)

    def mask(qinfo, kinfo):
        return (
            (qinfo[1][:, None] == kinfo[1][None, :])
            & (kinfo[0][None, :] <= qinfo[0][:, None])
            & kinfo[2][None, :]
        )

    def split(packed):
        return (
            packed[:, :features].reshape(rows, nheads, HD),
            packed[:, features:].reshape(rows, nheads, HD),
        )

    partner_events = exchange(local, "ctx", 1)
    kv = jnp.concatenate([keys, values[0]], axis=1)
    qg = jnp.concatenate([queries, grad_out[0]], axis=1)
    kv_from = [None] + [shifted(kv, "ctx", step) for step in range(1, SPAN + 1)]
    qg_from = [None] + [shifted(qg, "ctx", -step) for step in range(1, SPAN + 1)]

    q_me, g_me = split(qg)
    k_me, v_me = split(kv)
    info_me = describe(myself)
    out_acc, dq_acc, att0, dsc0 = forward_terms(
        q_me, g_me, k_me, v_me, mask(info_me, info_me), scale, alpha
    )
    dk_acc = jnp.einsum("hqk,qhd->khd", dsc0, q_me, preferred_element_type=jnp.float32)
    dv_acc = jnp.einsum("hqk,qhd->khd", att0, g_me, preferred_element_type=jnp.float32)
    for step in range(1, SPAN + 1):
        k_s, v_s = split(kv_from[step])
        o, a, _, _ = forward_terms(
            q_me, g_me, k_s, v_s, mask(info_me, describe(myself - step)), scale, alpha
        )
        out_acc = out_acc + o
        dq_acc = dq_acc + a
        q_s, g_s = split(qg_from[step])
        b, c = backward_terms(
            q_s, g_s, k_me, v_me, mask(describe(myself + step), info_me), scale, alpha
        )
        dk_acc = dk_acc + b
        dv_acc = dv_acc + c
    attended = out_acc.reshape(1, rows, features).astype(jnp.bfloat16)
    grad_values = dv_acc.reshape(1, rows, features).astype(jnp.bfloat16)
    dq_b = dq_acc.reshape(rows, features).astype(jnp.bfloat16)
    dk_b = dk_acc.reshape(rows, features).astype(jnp.bfloat16)
    joined = jnp.concatenate([dq_b, dk_b], axis=1)
    mine = reduce_rows(local, partner_events, joined, myself, cycle_size)
    grad_wq = mine[:, :features].astype(jnp.bfloat16)
    grad_wk = mine[:, features:].astype(jnp.bfloat16)
    return (attended, grad_values, grad_wq, grad_wk)


def solution(mesh):
    placed = (
        P("dp", "ctx", None),
        P(),
        P(),
        P("dp", "ctx", None),
        P("dp", "ctx", None),
        P("dp", None),
        P("dp"),
        P("dp", None),
    )
    return jax.shard_map(
        body,
        mesh=mesh,
        in_specs=placed,
        out_specs=(P("dp", "ctx", None), P("dp", "ctx", None), P("ctx", None), P("ctx", None)),
        check_vma=False,
    )
```

```python
import jax
import jax.numpy as jnp
from jax import lax
from jax.sharding import PartitionSpec as P

HD = 128
SPAN = 3
BLOCK = 128
MAXLEN = 768


def shifted(value, axis, steps):
    count = lax.axis_size(axis)
    pairs = [(source, (source + steps) % count) for source in range(count)]
    return lax.ppermute(value, axis, pairs)


def exchange(value, axis, mask):
    count = lax.axis_size(axis)
    return lax.ppermute(value, axis, [(source, source ^ mask) for source in range(count)])


def pick(value, bit, axis):
    return (
        lax.dynamic_index_in_dim(value, bit, axis, keepdims=False),
        lax.dynamic_index_in_dim(value, 1 - bit, axis, keepdims=False),
    )


def reduce_rows(local, partner_events, joined, myself, cycle_size):
    width = local.shape[1]
    share = width // cycle_size
    core = myself % 2
    partner_joined = exchange(joined, "ctx", 1)
    both_events = jnp.concatenate([local, partner_events], axis=0)
    both_joined = jnp.concatenate([joined, partner_joined], axis=0)
    halves = both_events.reshape(both_events.shape[0], width // (2 * share), 2, share)
    kept = lax.dynamic_index_in_dim(halves, core, 2, keepdims=False).reshape(both_events.shape[0], width // 2)
    acc = jnp.dot(kept.T, both_joined, preferred_element_type=jnp.float32)
    acc = acc.reshape(width // (2 * share), share, joined.shape[1])
    mask = 2
    while mask < cycle_size:
        acc = acc.reshape(acc.shape[0] // 2, 2, share, joined.shape[1])
        keep_part, send_part = pick(acc, (myself // mask) % 2, 1)
        acc = keep_part + exchange(send_part.astype(jnp.bfloat16), "ctx", mask).astype(jnp.float32)
        mask *= 2
    acc = acc.reshape(share, joined.shape[1])
    mask = 1
    while mask < lax.axis_size("dp"):
        acc = acc + exchange(acc, "dp", mask)
        mask *= 2
    return acc


def scores(query, key, valid, scale, alpha):
    z = jnp.einsum("qhd,khd->hqk", query, key, preferred_element_type=jnp.float32) * alpha
    sig = jax.nn.sigmoid(z)
    weight = valid[None, :, :].astype(jnp.float32) * scale
    return z, sig, weight


def forward_terms(query, grad, key, value, valid, scale, alpha):
    z, sig, weight = scores(query, key, valid, scale, alpha)
    att = (z * sig * weight).astype(jnp.bfloat16)
    out = jnp.einsum("hqk,khd->qhd", att, value, preferred_element_type=jnp.float32)
    dprod = jnp.einsum("qhd,khd->hqk", grad, value, preferred_element_type=jnp.float32)
    dsc = (dprod * sig * (1.0 + z * (1.0 - sig)) * weight * alpha).astype(jnp.bfloat16)
    dquery = jnp.einsum("hqk,khd->qhd", dsc, key, preferred_element_type=jnp.float32)
    return out, dquery, att, dsc


def backward_terms(query, grad, key, value, valid, scale, alpha):
    z, sig, weight = scores(query, key, valid, scale, alpha)
    att = (z * sig * weight).astype(jnp.bfloat16)
    dprod = jnp.einsum("qhd,khd->hqk", grad, value, preferred_element_type=jnp.float32)
    dsc = (dprod * sig * (1.0 + z * (1.0 - sig)) * weight * alpha).astype(jnp.bfloat16)
    dkey = jnp.einsum("hqk,qhd->khd", dsc, query, preferred_element_type=jnp.float32)
    dvalue = jnp.einsum("hqk,qhd->khd", att, grad, preferred_element_type=jnp.float32)
    return dkey, dvalue


def body(events, w_query, w_key, values, grad_out, lengths, stream_shift, block_keep):
    rows = events.shape[1]
    features = w_query.shape[1]
    nheads = features // HD
    alpha = 1.0 / HD**0.5
    scale = 1.0 / MAXLEN**0.5
    local = events[0]
    queries = jnp.dot(local, w_query, preferred_element_type=jnp.float32).astype(jnp.bfloat16)
    keys = jnp.dot(local, w_key, preferred_element_type=jnp.float32).astype(jnp.bfloat16)
    cycle_size = lax.axis_size("ctx")
    myself = lax.axis_index("ctx")
    total = rows * cycle_size
    ends = jnp.cumsum(lengths[0])
    offset = stream_shift[0]
    keep = block_keep[0]
    blocks_all = jnp.arange(keep.shape[0], dtype=jnp.int32)
    within = jnp.arange(rows, dtype=jnp.int32)

    def describe(anchor):
        anchor = jnp.remainder(anchor, cycle_size)
        position = jnp.remainder(anchor * rows + within - offset, total)
        owner = jnp.sum((position[:, None] >= ends[None, :]).astype(jnp.int32), axis=1)
        which = position // BLOCK
        kept = (
            jnp.sum(jnp.where(which[:, None] == blocks_all[None, :], keep[None, :], 0), axis=1) > 0
        )
        return (position, owner, kept)

    def mask(qinfo, kinfo):
        return (
            (qinfo[1][:, None] == kinfo[1][None, :])
            & (kinfo[0][None, :] <= qinfo[0][:, None])
            & kinfo[2][None, :]
        )

    def split(packed):
        return (
            packed[:, :features].reshape(rows, nheads, HD),
            packed[:, features:].reshape(rows, nheads, HD),
        )

    partner_events = exchange(local, "ctx", 1)
    kv = jnp.concatenate([keys, values[0]], axis=1)
    qg = jnp.concatenate([queries, grad_out[0]], axis=1)
    kv_from = [None] + [shifted(kv, "ctx", step) for step in range(1, SPAN + 1)]
    qg_from = [None] + [shifted(qg, "ctx", -step) for step in range(1, SPAN + 1)]

    q_me, g_me = split(qg)
    k_me, v_me = split(kv)
    info_me = describe(myself)
    out_acc, dq_acc, att0, dsc0 = forward_terms(
        q_me, g_me, k_me, v_me, mask(info_me, info_me), scale, alpha
    )
    dk_acc = jnp.einsum("hqk,qhd->khd", dsc0, q_me, preferred_element_type=jnp.float32)
    dv_acc = jnp.einsum("hqk,qhd->khd", att0, g_me, preferred_element_type=jnp.float32)
    for step in range(1, SPAN + 1):
        k_s, v_s = split(kv_from[step])
        o, a, _, _ = forward_terms(
            q_me, g_me, k_s, v_s, mask(info_me, describe(myself - step)), scale, alpha
        )
        out_acc = out_acc + o
        dq_acc = dq_acc + a
        q_s, g_s = split(qg_from[step])
        b, c = backward_terms(
            q_s, g_s, k_me, v_me, mask(describe(myself + step), info_me), scale, alpha
        )
        dk_acc = dk_acc + b
        dv_acc = dv_acc + c
    attended = out_acc.reshape(1, rows, features).astype(jnp.bfloat16)
    grad_values = dv_acc.reshape(1, rows, features).astype(jnp.bfloat16)
    dq_b = dq_acc.reshape(rows, features).astype(jnp.bfloat16)
    dk_b = dk_acc.reshape(rows, features).astype(jnp.bfloat16)
    joined = jnp.concatenate([dq_b, dk_b], axis=1)
    mine = reduce_rows(local, partner_events, joined, myself, cycle_size)
    grad_wq = mine[:, :features].astype(jnp.bfloat16)
    grad_wk = mine[:, features:].astype(jnp.bfloat16)
    return (attended, grad_values, grad_wq, grad_wk)


def solution(mesh):
    placed = (
        P("dp", "ctx", None),
        P(),
        P(),
        P("dp", "ctx", None),
        P("dp", "ctx", None),
        P("dp", None),
        P("dp"),
        P("dp", None),
    )
    return jax.shard_map(
        body,
        mesh=mesh,
        in_specs=placed,
        out_specs=(P("dp", "ctx", None), P("dp", "ctx", None), P("ctx", None), P("ctx", None)),
        check_vma=False,
    )
```

```python
import jax
import jax.numpy as jnp
from jax import lax
from jax.experimental import pallas as pl
from jax.experimental.pallas import tpu as pltpu
from jax.sharding import PartitionSpec as P
import functools

HD = 128
SPAN = 3
BLOCK = 128
MAXLEN = 768


def shifted(value, axis, steps):
    count = lax.axis_size(axis)
    pairs = [(source, (source + steps) % count) for source in range(count)]
    return lax.ppermute(value, axis, pairs)


def exchange(value, axis, mask):
    count = lax.axis_size(axis)
    return lax.ppermute(value, axis, [(source, source ^ mask) for source in range(count)])


def pick(value, bit, axis):
    return (
        lax.dynamic_index_in_dim(value, bit, axis, keepdims=False),
        lax.dynamic_index_in_dim(value, 1 - bit, axis, keepdims=False),
    )


def reduce_rows(local, partner_events, joined, myself, cycle_size):
    width = local.shape[1]
    share = width // cycle_size
    core = myself % 2
    partner_joined = exchange(joined, "ctx", 1)
    both_events = jnp.concatenate([local, partner_events], axis=0)
    both_joined = jnp.concatenate([joined, partner_joined], axis=0)
    halves = both_events.reshape(both_events.shape[0], width // (2 * share), 2, share)
    kept = lax.dynamic_index_in_dim(halves, core, 2, keepdims=False).reshape(both_events.shape[0], width // 2)
    acc = jnp.dot(kept.T, both_joined, preferred_element_type=jnp.float32)
    acc = acc.reshape(width // (2 * share), share, joined.shape[1])
    mask = 2
    while mask < cycle_size:
        acc = acc.reshape(acc.shape[0] // 2, 2, share, joined.shape[1])
        keep_part, send_part = pick(acc, (myself // mask) % 2, 1)
        acc = keep_part + exchange(send_part.astype(jnp.bfloat16), "ctx", mask).astype(jnp.float32)
        mask *= 2
    acc = acc.reshape(share, joined.shape[1])
    mask = 1
    while mask < lax.axis_size("dp"):
        acc = acc + exchange(acc, "dp", mask)
        mask *= 2
    return acc


def tiles_kernel(span, alpha, scale, infoc, infor, *refs):
    count = 2 * span + 2
    qs = refs[0:count:2]
    gs = refs[1:count:2]
    ks = refs[count:2 * count:2]
    vs = refs[count + 1:2 * count:2]
    out_ref, dq_ref, dk_ref, dv_ref = refs[2 * count:]
    lanes = 2 * span + 1

    def valid(qa, ka):
        qpos = infoc[:, qa:qa + 1]
        quser = infoc[:, lanes + qa:lanes + qa + 1]
        kpos = infor[ka:ka + 1, :]
        kuser = infor[lanes + ka:lanes + ka + 1, :]
        kkept = infor[2 * lanes + ka:2 * lanes + ka + 1, :]
        return (quser == kuser) & (kpos <= qpos) & (kkept > 0)

    def terms(q, g, k, v, ok):
        z = lax.dot_general(q, k, (((1,), (1,)), ((), ())), preferred_element_type=jnp.float32) * alpha
        sig = 1.0 / (1.0 + jnp.exp(-z))
        weight = jnp.where(ok, scale, 0.0)
        att = (z * sig * weight).astype(jnp.bfloat16)
        dprod = lax.dot_general(g, v, (((1,), (1,)), ((), ())), preferred_element_type=jnp.float32)
        dsc = (dprod * sig * (1.0 + z * (1.0 - sig)) * weight * alpha).astype(jnp.bfloat16)
        return att, dsc

    def back(att, dsc, q, g):
        dk = lax.dot_general(dsc, q, (((0,), (0,)), ((), ())), preferred_element_type=jnp.float32)
        dv = lax.dot_general(att, g, (((0,), (0,)), ((), ())), preferred_element_type=jnp.float32)
        return dk, dv

    q0, g0, k0, v0 = qs[0][...], gs[0][...], ks[0][...], vs[0][...]
    att, dsc = terms(q0, g0, k0, v0, valid(span, span))
    out = jnp.dot(att, v0, preferred_element_type=jnp.float32)
    dq = jnp.dot(dsc, k0, preferred_element_type=jnp.float32)
    dk, dv = back(att, dsc, q0, g0)
    for step in range(1, span + 1):
        k, v = ks[step][...], vs[step][...]
        att, dsc = terms(q0, g0, k, v, valid(span, span - step))
        out = out + jnp.dot(att, v, preferred_element_type=jnp.float32)
        dq = dq + jnp.dot(dsc, k, preferred_element_type=jnp.float32)
        q, g = qs[step][...], gs[step][...]
        att, dsc = terms(q, g, k0, v0, valid(span + step, span))
        b, c = back(att, dsc, q, g)
        dk = dk + b
        dv = dv + c
    out_ref[...] = out.astype(out_ref.dtype)
    dq_ref[...] = dq.astype(dq_ref.dtype)
    dk_ref[...] = dk.astype(dk_ref.dtype)
    dv_ref[...] = dv.astype(dv_ref.dtype)


def attention_tiles(qg_list, kv_list, infoc, infor, nheads, alpha, scale):
    rows = qg_list[0].shape[0]
    span = len(qg_list) - 1
    blk = lambda offset: pl.BlockSpec((rows, HD), lambda h: (0, h + offset))
    full = lambda arr: pl.BlockSpec(arr.shape, lambda h: (0, 0))
    operands, specs = [infoc, infor], [full(infoc), full(infor)]
    for group in (qg_list, kv_list):
        for packed in group:
            operands += [packed, packed]
            specs += [blk(0), blk(nheads)]
    shape = jax.ShapeDtypeStruct((rows, nheads * HD), jnp.bfloat16)
    tile = rows * rows * HD * 2
    return pl.pallas_call(
        functools.partial(tiles_kernel, span, alpha, scale),
        grid=(nheads,),
        in_specs=specs,
        out_specs=[blk(0)] * 4,
        out_shape=[shape] * 4,
        cost_estimate=pl.CostEstimate(
            flops=nheads * (2 * span + 1) * 5 * tile,
            transcendentals=nheads * (2 * span + 1) * rows * rows,
            bytes_accessed=(2 * span + 2) * 2 * rows * nheads * HD * 2 * 2 + 4 * rows * nheads * HD * 2,
        ),
    )(*operands)


def scores(query, key, valid, scale, alpha):
    z = jnp.einsum("qhd,khd->hqk", query, key, preferred_element_type=jnp.float32) * alpha
    sig = jax.nn.sigmoid(z)
    weight = valid[None, :, :].astype(jnp.float32) * scale
    return z, sig, weight


def forward_terms(query, grad, key, value, valid, scale, alpha):
    z, sig, weight = scores(query, key, valid, scale, alpha)
    att = (z * sig * weight).astype(jnp.bfloat16)
    out = jnp.einsum("hqk,khd->qhd", att, value, preferred_element_type=jnp.float32)
    dprod = jnp.einsum("qhd,khd->hqk", grad, value, preferred_element_type=jnp.float32)
    dsc = (dprod * sig * (1.0 + z * (1.0 - sig)) * weight * alpha).astype(jnp.bfloat16)
    dquery = jnp.einsum("hqk,khd->qhd", dsc, key, preferred_element_type=jnp.float32)
    return out, dquery, att, dsc


def backward_terms(query, grad, key, value, valid, scale, alpha):
    z, sig, weight = scores(query, key, valid, scale, alpha)
    att = (z * sig * weight).astype(jnp.bfloat16)
    dprod = jnp.einsum("qhd,khd->hqk", grad, value, preferred_element_type=jnp.float32)
    dsc = (dprod * sig * (1.0 + z * (1.0 - sig)) * weight * alpha).astype(jnp.bfloat16)
    dkey = jnp.einsum("hqk,qhd->khd", dsc, query, preferred_element_type=jnp.float32)
    dvalue = jnp.einsum("hqk,qhd->khd", att, grad, preferred_element_type=jnp.float32)
    return dkey, dvalue


def body(events, w_query, w_key, values, grad_out, lengths, stream_shift, block_keep):
    rows = events.shape[1]
    features = w_query.shape[1]
    nheads = features // HD
    alpha = 1.0 / HD**0.5
    scale = 1.0 / MAXLEN**0.5
    local = events[0]
    queries = jnp.dot(local, w_query, preferred_element_type=jnp.float32).astype(jnp.bfloat16)
    keys = jnp.dot(local, w_key, preferred_element_type=jnp.float32).astype(jnp.bfloat16)
    cycle_size = lax.axis_size("ctx")
    myself = lax.axis_index("ctx")
    total = rows * cycle_size
    ends = jnp.cumsum(lengths[0])
    offset = stream_shift[0]
    keep = block_keep[0]
    blocks_all = jnp.arange(keep.shape[0], dtype=jnp.int32)
    within = jnp.arange(rows, dtype=jnp.int32)

    def describe(anchor):
        anchor = jnp.remainder(anchor, cycle_size)
        position = jnp.remainder(anchor * rows + within - offset, total)
        owner = jnp.sum((position[:, None] >= ends[None, :]).astype(jnp.int32), axis=1)
        which = position // BLOCK
        kept = (
            jnp.sum(jnp.where(which[:, None] == blocks_all[None, :], keep[None, :], 0), axis=1) > 0
        )
        return (position, owner, kept)

    def mask(qinfo, kinfo):
        return (
            (qinfo[1][:, None] == kinfo[1][None, :])
            & (kinfo[0][None, :] <= qinfo[0][:, None])
            & kinfo[2][None, :]
        )

    def split(packed):
        return (
            packed[:, :features].reshape(rows, nheads, HD),
            packed[:, features:].reshape(rows, nheads, HD),
        )

    partner_events = exchange(local, "ctx", 1)
    kv = jnp.concatenate([keys, values[0]], axis=1)
    qg = jnp.concatenate([queries, grad_out[0]], axis=1)
    kv_from = [None] + [shifted(kv, "ctx", step) for step in range(1, SPAN + 1)]
    qg_from = [None] + [shifted(qg, "ctx", -step) for step in range(1, SPAN + 1)]

    offsets = range(-SPAN, SPAN + 1)
    described = [describe(myself + offset) for offset in offsets]
    infor = jnp.stack(
        [d[0] for d in described] + [d[1] for d in described] + [d[2].astype(jnp.int32) for d in described]
    ).astype(jnp.int32)
    infoc = infor.T
    out_b, dq_b, dk_b, dv_b = attention_tiles(
        [qg] + qg_from[1:], [kv] + kv_from[1:], infoc, infor, nheads, alpha, scale
    )
    attended = out_b.reshape(1, rows, features)
    grad_values = dv_b.reshape(1, rows, features)
    joined = jnp.concatenate([dq_b, dk_b], axis=1)
    mine = reduce_rows(local, partner_events, joined, myself, cycle_size)
    grad_wq = mine[:, :features].astype(jnp.bfloat16)
    grad_wk = mine[:, features:].astype(jnp.bfloat16)
    return (attended, grad_values, grad_wq, grad_wk)


def solution(mesh):
    placed = (
        P("dp", "ctx", None),
        P(),
        P(),
        P("dp", "ctx", None),
        P("dp", "ctx", None),
        P("dp", None),
        P("dp"),
        P("dp", None),
    )
    return jax.shard_map(
        body,
        mesh=mesh,
        in_specs=placed,
        out_specs=(P("dp", "ctx", None), P("dp", "ctx", None), P("ctx", None), P("ctx", None)),
        check_vma=False,
    )
```

```python
import jax
import jax.numpy as jnp
from jax import lax
from jax.experimental import pallas as pl
from jax.experimental.pallas import tpu as pltpu
from jax.sharding import PartitionSpec as P
import functools

HD = 128
SPAN = 3
BLOCK = 128
MAXLEN = 768


def shifted(value, axis, steps):
    count = lax.axis_size(axis)
    pairs = [(source, (source + steps) % count) for source in range(count)]
    return lax.ppermute(value, axis, pairs)


def exchange(value, axis, mask):
    count = lax.axis_size(axis)
    return lax.ppermute(value, axis, [(source, source ^ mask) for source in range(count)])


def pick(value, bit, axis):
    return (
        lax.dynamic_index_in_dim(value, bit, axis, keepdims=False),
        lax.dynamic_index_in_dim(value, 1 - bit, axis, keepdims=False),
    )


def reduce_rows(local, partner_events, joined, myself, cycle_size):
    width = local.shape[1]
    share = width // cycle_size
    core = myself % 2
    partner_joined = exchange(joined, "ctx", 1)
    both_events = jnp.concatenate([local, partner_events], axis=0)
    both_joined = jnp.concatenate([joined, partner_joined], axis=0)
    halves = both_events.reshape(both_events.shape[0], width // (2 * share), 2, share)
    kept = lax.dynamic_index_in_dim(halves, core, 2, keepdims=False).reshape(both_events.shape[0], width // 2)
    acc = jnp.dot(kept.T, both_joined, preferred_element_type=jnp.float32)
    acc = acc.reshape(width // (2 * share), share, joined.shape[1])
    mask = 2
    while mask < cycle_size:
        acc = acc.reshape(acc.shape[0] // 2, 2, share, joined.shape[1])
        keep_part, send_part = pick(acc, (myself // mask) % 2, 1)
        acc = keep_part + exchange(send_part.astype(jnp.bfloat16), "ctx", mask).astype(jnp.float32)
        mask *= 2
    acc = acc.reshape(share, joined.shape[1])
    mask = 1
    while mask < lax.axis_size("dp"):
        acc = acc + exchange(acc, "dp", mask)
        mask *= 2
    return acc


def tiles_kernel(span, alpha, scale, infoc, infor, *refs):
    count = 2 * span + 2
    qs = refs[0:count:2]
    gs = refs[1:count:2]
    ks = refs[count:2 * count:2]
    vs = refs[count + 1:2 * count:2]
    out_ref, dq_ref, dk_ref, dv_ref = refs[2 * count:]
    lanes = 2 * span + 1

    def valid(qa, ka):
        qpos = infoc[:, qa:qa + 1]
        quser = infoc[:, lanes + qa:lanes + qa + 1]
        kpos = infor[ka:ka + 1, :]
        kuser = infor[lanes + ka:lanes + ka + 1, :]
        kkept = infor[2 * lanes + ka:2 * lanes + ka + 1, :]
        return (quser == kuser) & (kpos <= qpos) & (kkept > 0)

    def terms(q, g, k, v, ok):
        z = lax.dot_general(q, k, (((1,), (1,)), ((), ())), preferred_element_type=jnp.float32) * alpha
        sig = 1.0 / (1.0 + jnp.exp(-z))
        weight = jnp.where(ok, scale, 0.0)
        att = (z * sig * weight).astype(jnp.bfloat16)
        dprod = lax.dot_general(g, v, (((1,), (1,)), ((), ())), preferred_element_type=jnp.float32)
        dsc = (dprod * sig * (1.0 + z * (1.0 - sig)) * weight * alpha).astype(jnp.bfloat16)
        return att, dsc

    def back(att, dsc, q, g):
        dk = lax.dot_general(dsc, q, (((0,), (0,)), ((), ())), preferred_element_type=jnp.float32)
        dv = lax.dot_general(att, g, (((0,), (0,)), ((), ())), preferred_element_type=jnp.float32)
        return dk, dv

    q0, g0, k0, v0 = qs[0][...], gs[0][...], ks[0][...], vs[0][...]
    att, dsc = terms(q0, g0, k0, v0, valid(span, span))
    out = jnp.dot(att, v0, preferred_element_type=jnp.float32)
    dq = jnp.dot(dsc, k0, preferred_element_type=jnp.float32)
    dk, dv = back(att, dsc, q0, g0)
    for step in range(1, span + 1):
        k, v = ks[step][...], vs[step][...]
        att, dsc = terms(q0, g0, k, v, valid(span, span - step))
        out = out + jnp.dot(att, v, preferred_element_type=jnp.float32)
        dq = dq + jnp.dot(dsc, k, preferred_element_type=jnp.float32)
        q, g = qs[step][...], gs[step][...]
        att, dsc = terms(q, g, k0, v0, valid(span + step, span))
        b, c = back(att, dsc, q, g)
        dk = dk + b
        dv = dv + c
    out_ref[...] = out.astype(out_ref.dtype)
    dq_ref[...] = dq.astype(dq_ref.dtype)
    dk_ref[...] = dk.astype(dk_ref.dtype)
    dv_ref[...] = dv.astype(dv_ref.dtype)


def attention_tiles(qg_list, kv_list, infoc, infor, nheads, alpha, scale):
    rows = qg_list[0].shape[0]
    span = len(qg_list) - 1
    blk = lambda offset: pl.BlockSpec((rows, HD), lambda h: (0, h + offset))
    full = lambda arr: pl.BlockSpec(arr.shape, lambda h: (0, 0))
    operands, specs = [infoc, infor], [full(infoc), full(infor)]
    for group in (qg_list, kv_list):
        for packed in group:
            operands += [packed, packed]
            specs += [blk(0), blk(nheads)]
    shape = jax.ShapeDtypeStruct((rows, nheads * HD), jnp.bfloat16)
    tile = rows * rows * HD * 2
    return pl.pallas_call(
        functools.partial(tiles_kernel, span, alpha, scale),
        grid=(nheads,),
        in_specs=specs,
        out_specs=[blk(0)] * 4,
        out_shape=[shape] * 4,
        cost_estimate=pl.CostEstimate(
            flops=nheads * (2 * span + 1) * 5 * tile,
            transcendentals=nheads * (2 * span + 1) * rows * rows,
            bytes_accessed=(2 * span + 2) * 2 * rows * nheads * HD * 2 * 2 + 4 * rows * nheads * HD * 2,
        ),
    )(*operands)


def exchange_kernel(span, kv_ref, qg_ref, ev_ref, out_ref, ev_out, landed, ev_land, send_sem, recv_sem):
    count = lax.axis_size("ctx")
    me = lax.axis_index("ctx")
    group = lax.axis_index("dp")
    barrier = pltpu.get_barrier_semaphore()
    for step in range(1, span + 1):
        for peer in ((me + step) % count, (me + count - step) % count):
            pl.semaphore_signal(barrier, inc=1, device_id=(group, peer), device_id_type=pl.DeviceIdType.MESH)
    pl.semaphore_wait(barrier, 2 * span)
    copies = []
    for step in range(1, span + 1):
        forward = pltpu.make_async_remote_copy(
            src_ref=kv_ref,
            dst_ref=landed.at[step - 1],
            send_sem=send_sem.at[step - 1],
            recv_sem=recv_sem.at[step - 1],
            device_id=(group, (me + step) % count),
            device_id_type=pl.DeviceIdType.MESH,
        )
        backward = pltpu.make_async_remote_copy(
            src_ref=qg_ref,
            dst_ref=landed.at[span + step - 1],
            send_sem=send_sem.at[span + step - 1],
            recv_sem=recv_sem.at[span + step - 1],
            device_id=(group, (me + count - step) % count),
            device_id_type=pl.DeviceIdType.MESH,
        )
        copies += [forward, backward]
    partner = pltpu.make_async_remote_copy(
        src_ref=ev_ref,
        dst_ref=ev_land,
        send_sem=send_sem.at[2 * span],
        recv_sem=recv_sem.at[2 * span],
        device_id=(group, me + 1 - 2 * (me % 2)),
        device_id_type=pl.DeviceIdType.MESH,
    )
    copies.append(partner)
    for copy in copies:
        copy.start()
    for copy in copies:
        copy.wait()
    out_ref[...] = landed[...]
    ev_out[...] = ev_land[...]


def exchange_blocks(kv, qg, events, span):
    rows, width = kv.shape
    vmem = pl.BlockSpec(memory_space=pltpu.VMEM)
    return pl.pallas_call(
        functools.partial(exchange_kernel, span),
        in_specs=[vmem] * 3,
        out_specs=[vmem, vmem],
        out_shape=[
            jax.ShapeDtypeStruct((2 * span, rows, width), kv.dtype),
            jax.ShapeDtypeStruct(events.shape, events.dtype),
        ],
        scratch_shapes=[
            pltpu.VMEM((2 * span, rows, width), kv.dtype),
            pltpu.VMEM(events.shape, events.dtype),
            pltpu.SemaphoreType.DMA((2 * span + 1,)),
            pltpu.SemaphoreType.DMA((2 * span + 1,)),
        ],
        compiler_params=pltpu.CompilerParams(collective_id=0, has_side_effects=True),
    )(kv, qg, events)


def body(events, w_query, w_key, values, grad_out, lengths, stream_shift, block_keep):
    rows = events.shape[1]
    features = w_query.shape[1]
    nheads = features // HD
    alpha = 1.0 / HD**0.5
    scale = 1.0 / MAXLEN**0.5
    local = events[0]
    queries = jnp.dot(local, w_query, preferred_element_type=jnp.float32).astype(jnp.bfloat16)
    keys = jnp.dot(local, w_key, preferred_element_type=jnp.float32).astype(jnp.bfloat16)
    cycle_size = lax.axis_size("ctx")
    myself = lax.axis_index("ctx")
    total = rows * cycle_size
    ends = jnp.cumsum(lengths[0])
    offset = stream_shift[0]
    keep = block_keep[0]
    blocks_all = jnp.arange(keep.shape[0], dtype=jnp.int32)
    within = jnp.arange(rows, dtype=jnp.int32)

    def describe(anchor):
        anchor = jnp.remainder(anchor, cycle_size)
        position = jnp.remainder(anchor * rows + within - offset, total)
        owner = jnp.sum((position[:, None] >= ends[None, :]).astype(jnp.int32), axis=1)
        which = position // BLOCK
        kept = (
            jnp.sum(jnp.where(which[:, None] == blocks_all[None, :], keep[None, :], 0), axis=1) > 0
        )
        return (position, owner, kept)

    kv = jnp.concatenate([keys, values[0]], axis=1)
    qg = jnp.concatenate([queries, grad_out[0]], axis=1)
    landed, partner_events = exchange_blocks(kv, qg, local, SPAN)
    kv_from = [None] + [landed[step - 1] for step in range(1, SPAN + 1)]
    qg_from = [None] + [landed[SPAN + step - 1] for step in range(1, SPAN + 1)]

    offsets = range(-SPAN, SPAN + 1)
    described = [describe(myself + offset) for offset in offsets]
    infor = jnp.stack(
        [d[0] for d in described] + [d[1] for d in described] + [d[2].astype(jnp.int32) for d in described]
    ).astype(jnp.int32)
    infoc = infor.T
    out_b, dq_b, dk_b, dv_b = attention_tiles(
        [qg] + qg_from[1:], [kv] + kv_from[1:], infoc, infor, nheads, alpha, scale
    )
    attended = out_b.reshape(1, rows, features)
    grad_values = dv_b.reshape(1, rows, features)
    joined = jnp.concatenate([dq_b, dk_b], axis=1)
    mine = reduce_rows(local, partner_events, joined, myself, cycle_size)
    grad_wq = mine[:, :features].astype(jnp.bfloat16)
    grad_wk = mine[:, features:].astype(jnp.bfloat16)
    return (attended, grad_values, grad_wq, grad_wk)


def solution(mesh):
    placed = (
        P("dp", "ctx", None),
        P(),
        P(),
        P("dp", "ctx", None),
        P("dp", "ctx", None),
        P("dp", None),
        P("dp"),
        P("dp", None),
    )
    return jax.shard_map(
        body,
        mesh=mesh,
        in_specs=placed,
        out_specs=(P("dp", "ctx", None), P("dp", "ctx", None), P("ctx", None), P("ctx", None)),
        check_vma=False,
    )
```

```python
import jax
import jax.numpy as jnp
from jax import lax
from jax.experimental import pallas as pl
from jax.experimental.pallas import tpu as pltpu
from jax.sharding import PartitionSpec as P
import functools

HD = 128
SPAN = 3
BLOCK = 128
MAXLEN = 768


def shifted(value, axis, steps):
    count = lax.axis_size(axis)
    pairs = [(source, (source + steps) % count) for source in range(count)]
    return lax.ppermute(value, axis, pairs)


def exchange(value, axis, mask):
    count = lax.axis_size(axis)
    return lax.ppermute(value, axis, [(source, source ^ mask) for source in range(count)])


def pick(value, bit, axis):
    return (
        lax.dynamic_index_in_dim(value, bit, axis, keepdims=False),
        lax.dynamic_index_in_dim(value, 1 - bit, axis, keepdims=False),
    )


def reduce_kernel(groups, spread, part_ref, out_ref, sent, landed, dp_landed, send_a, recv_a, send_b, recv_b):
    count = lax.axis_size("ctx")
    me = lax.axis_index("ctx")
    group = lax.axis_index("dp")
    core = me % 2
    slot = me // 2
    barrier = pltpu.get_barrier_semaphore()
    for step in range(1, groups):
        peer = 2 * ((slot + step) % groups) + core
        pl.semaphore_signal(barrier, inc=1, device_id=(group, peer), device_id_type=pl.DeviceIdType.MESH)
    for step in range(1, spread):
        pl.semaphore_signal(
            barrier, inc=1, device_id=((group + step) % spread, me), device_id_type=pl.DeviceIdType.MESH
        )
    pl.semaphore_wait(barrier, groups - 1 + spread - 1)
    sent[...] = part_ref[...].astype(sent.dtype)
    copies = []
    for step in range(1, groups):
        target = (slot + step) % groups
        copy = pltpu.make_async_remote_copy(
            src_ref=sent.at[target],
            dst_ref=landed.at[slot],
            send_sem=send_a.at[step - 1],
            recv_sem=recv_a.at[step - 1],
            device_id=(group, 2 * target + core),
            device_id_type=pl.DeviceIdType.MESH,
        )
        copy.start()
        copies.append(copy)
    for copy in copies:
        copy.wait()
    total = part_ref[slot]
    for step in range(1, groups):
        total = total + landed[(slot + groups - step) % groups].astype(jnp.float32)
    dp_landed[group] = total
    copies = []
    for step in range(1, spread):
        copy = pltpu.make_async_remote_copy(
            src_ref=dp_landed.at[group],
            dst_ref=dp_landed.at[group],
            send_sem=send_b.at[step - 1],
            recv_sem=recv_b.at[step - 1],
            device_id=((group + step) % spread, me),
            device_id_type=pl.DeviceIdType.MESH,
        )
        copy.start()
        copies.append(copy)
    for copy in copies:
        copy.wait()
    result = dp_landed[0]
    for index in range(1, spread):
        result = result + dp_landed[index]
    out_ref[...] = result


def reduce_blocks(part, spread):
    groups, share, width = part.shape
    vmem = pl.BlockSpec(memory_space=pltpu.VMEM)
    return pl.pallas_call(
        functools.partial(reduce_kernel, groups, spread),
        in_specs=[vmem],
        out_specs=vmem,
        out_shape=jax.ShapeDtypeStruct((share, width), jnp.float32),
        scratch_shapes=[
            pltpu.VMEM((groups, share, width), jnp.bfloat16),
            pltpu.VMEM((groups, share, width), jnp.bfloat16),
            pltpu.VMEM((spread, share, width), jnp.float32),
            pltpu.SemaphoreType.DMA((groups - 1,)),
            pltpu.SemaphoreType.DMA((groups - 1,)),
            pltpu.SemaphoreType.DMA((spread - 1,)),
            pltpu.SemaphoreType.DMA((spread - 1,)),
        ],
        compiler_params=pltpu.CompilerParams(collective_id=1, has_side_effects=True),
    )(part)


def reduce_rows(local, partner_events, joined, myself, cycle_size):
    width = local.shape[1]
    share = width // cycle_size
    core = myself % 2
    partner_joined = exchange(joined, "ctx", 1)
    both_events = jnp.concatenate([local, partner_events], axis=0)
    both_joined = jnp.concatenate([joined, partner_joined], axis=0)
    halves = both_events.reshape(both_events.shape[0], width // (2 * share), 2, share)
    kept = lax.dynamic_index_in_dim(halves, core, 2, keepdims=False).reshape(both_events.shape[0], width // 2)
    acc = jnp.dot(kept.T, both_joined, preferred_element_type=jnp.float32)
    acc = acc.reshape(width // (2 * share), share, joined.shape[1])
    acc = reduce_blocks(acc, lax.axis_size("dp"))
    return acc


def tiles_kernel(span, alpha, scale, infoc, infor, *refs):
    count = 2 * span + 2
    qs = refs[0:count:2]
    gs = refs[1:count:2]
    ks = refs[count:2 * count:2]
    vs = refs[count + 1:2 * count:2]
    out_ref, dq_ref, dk_ref, dv_ref = refs[2 * count:]
    lanes = 2 * span + 1

    def valid(qa, ka):
        qpos = infoc[:, qa:qa + 1]
        quser = infoc[:, lanes + qa:lanes + qa + 1]
        kpos = infor[ka:ka + 1, :]
        kuser = infor[lanes + ka:lanes + ka + 1, :]
        kkept = infor[2 * lanes + ka:2 * lanes + ka + 1, :]
        return (quser == kuser) & (kpos <= qpos) & (kkept > 0)

    def terms(q, g, k, v, ok):
        z = lax.dot_general(q, k, (((1,), (1,)), ((), ())), preferred_element_type=jnp.float32) * alpha
        sig = 1.0 / (1.0 + jnp.exp(-z))
        weight = jnp.where(ok, scale, 0.0)
        att = (z * sig * weight).astype(jnp.bfloat16)
        dprod = lax.dot_general(g, v, (((1,), (1,)), ((), ())), preferred_element_type=jnp.float32)
        dsc = (dprod * sig * (1.0 + z * (1.0 - sig)) * weight * alpha).astype(jnp.bfloat16)
        return att, dsc

    def back(att, dsc, q, g):
        dk = lax.dot_general(dsc, q, (((0,), (0,)), ((), ())), preferred_element_type=jnp.float32)
        dv = lax.dot_general(att, g, (((0,), (0,)), ((), ())), preferred_element_type=jnp.float32)
        return dk, dv

    q0, g0, k0, v0 = qs[0][...], gs[0][...], ks[0][...], vs[0][...]
    att, dsc = terms(q0, g0, k0, v0, valid(span, span))
    out = jnp.dot(att, v0, preferred_element_type=jnp.float32)
    dq = jnp.dot(dsc, k0, preferred_element_type=jnp.float32)
    dk, dv = back(att, dsc, q0, g0)
    for step in range(1, span + 1):
        k, v = ks[step][...], vs[step][...]
        att, dsc = terms(q0, g0, k, v, valid(span, span - step))
        out = out + jnp.dot(att, v, preferred_element_type=jnp.float32)
        dq = dq + jnp.dot(dsc, k, preferred_element_type=jnp.float32)
        q, g = qs[step][...], gs[step][...]
        att, dsc = terms(q, g, k0, v0, valid(span + step, span))
        b, c = back(att, dsc, q, g)
        dk = dk + b
        dv = dv + c
    out_ref[...] = out.astype(out_ref.dtype)
    dq_ref[...] = dq.astype(dq_ref.dtype)
    dk_ref[...] = dk.astype(dk_ref.dtype)
    dv_ref[...] = dv.astype(dv_ref.dtype)


def attention_tiles(qg_list, kv_list, infoc, infor, nheads, alpha, scale):
    rows = qg_list[0].shape[0]
    span = len(qg_list) - 1
    blk = lambda offset: pl.BlockSpec((rows, HD), lambda h: (0, h + offset))
    full = lambda arr: pl.BlockSpec(arr.shape, lambda h: (0, 0))
    operands, specs = [infoc, infor], [full(infoc), full(infor)]
    for group in (qg_list, kv_list):
        for packed in group:
            operands += [packed, packed]
            specs += [blk(0), blk(nheads)]
    shape = jax.ShapeDtypeStruct((rows, nheads * HD), jnp.bfloat16)
    tile = rows * rows * HD * 2
    return pl.pallas_call(
        functools.partial(tiles_kernel, span, alpha, scale),
        grid=(nheads,),
        in_specs=specs,
        out_specs=[blk(0)] * 4,
        out_shape=[shape] * 4,
        cost_estimate=pl.CostEstimate(
            flops=nheads * (2 * span + 1) * 5 * tile,
            transcendentals=nheads * (2 * span + 1) * rows * rows,
            bytes_accessed=(2 * span + 2) * 2 * rows * nheads * HD * 2 * 2 + 4 * rows * nheads * HD * 2,
        ),
    )(*operands)


def scores(query, key, valid, scale, alpha):
    z = jnp.einsum("qhd,khd->hqk", query, key, preferred_element_type=jnp.float32) * alpha
    sig = jax.nn.sigmoid(z)
    weight = valid[None, :, :].astype(jnp.float32) * scale
    return z, sig, weight


def forward_terms(query, grad, key, value, valid, scale, alpha):
    z, sig, weight = scores(query, key, valid, scale, alpha)
    att = (z * sig * weight).astype(jnp.bfloat16)
    out = jnp.einsum("hqk,khd->qhd", att, value, preferred_element_type=jnp.float32)
    dprod = jnp.einsum("qhd,khd->hqk", grad, value, preferred_element_type=jnp.float32)
    dsc = (dprod * sig * (1.0 + z * (1.0 - sig)) * weight * alpha).astype(jnp.bfloat16)
    dquery = jnp.einsum("hqk,khd->qhd", dsc, key, preferred_element_type=jnp.float32)
    return out, dquery, att, dsc


def backward_terms(query, grad, key, value, valid, scale, alpha):
    z, sig, weight = scores(query, key, valid, scale, alpha)
    att = (z * sig * weight).astype(jnp.bfloat16)
    dprod = jnp.einsum("qhd,khd->hqk", grad, value, preferred_element_type=jnp.float32)
    dsc = (dprod * sig * (1.0 + z * (1.0 - sig)) * weight * alpha).astype(jnp.bfloat16)
    dkey = jnp.einsum("hqk,qhd->khd", dsc, query, preferred_element_type=jnp.float32)
    dvalue = jnp.einsum("hqk,qhd->khd", att, grad, preferred_element_type=jnp.float32)
    return dkey, dvalue


def body(events, w_query, w_key, values, grad_out, lengths, stream_shift, block_keep):
    rows = events.shape[1]
    features = w_query.shape[1]
    nheads = features // HD
    alpha = 1.0 / HD**0.5
    scale = 1.0 / MAXLEN**0.5
    local = events[0]
    queries = jnp.dot(local, w_query, preferred_element_type=jnp.float32).astype(jnp.bfloat16)
    keys = jnp.dot(local, w_key, preferred_element_type=jnp.float32).astype(jnp.bfloat16)
    cycle_size = lax.axis_size("ctx")
    myself = lax.axis_index("ctx")
    total = rows * cycle_size
    ends = jnp.cumsum(lengths[0])
    offset = stream_shift[0]
    keep = block_keep[0]
    blocks_all = jnp.arange(keep.shape[0], dtype=jnp.int32)
    within = jnp.arange(rows, dtype=jnp.int32)

    def describe(anchor):
        anchor = jnp.remainder(anchor, cycle_size)
        position = jnp.remainder(anchor * rows + within - offset, total)
        owner = jnp.sum((position[:, None] >= ends[None, :]).astype(jnp.int32), axis=1)
        which = position // BLOCK
        kept = (
            jnp.sum(jnp.where(which[:, None] == blocks_all[None, :], keep[None, :], 0), axis=1) > 0
        )
        return (position, owner, kept)

    def mask(qinfo, kinfo):
        return (
            (qinfo[1][:, None] == kinfo[1][None, :])
            & (kinfo[0][None, :] <= qinfo[0][:, None])
            & kinfo[2][None, :]
        )

    def split(packed):
        return (
            packed[:, :features].reshape(rows, nheads, HD),
            packed[:, features:].reshape(rows, nheads, HD),
        )

    partner_events = exchange(local, "ctx", 1)
    kv = jnp.concatenate([keys, values[0]], axis=1)
    qg = jnp.concatenate([queries, grad_out[0]], axis=1)
    kv_from = [None] + [shifted(kv, "ctx", step) for step in range(1, SPAN + 1)]
    qg_from = [None] + [shifted(qg, "ctx", -step) for step in range(1, SPAN + 1)]

    offsets = range(-SPAN, SPAN + 1)
    described = [describe(myself + offset) for offset in offsets]
    infor = jnp.stack(
        [d[0] for d in described] + [d[1] for d in described] + [d[2].astype(jnp.int32) for d in described]
    ).astype(jnp.int32)
    infoc = infor.T
    out_b, dq_b, dk_b, dv_b = attention_tiles(
        [qg] + qg_from[1:], [kv] + kv_from[1:], infoc, infor, nheads, alpha, scale
    )
    attended = out_b.reshape(1, rows, features)
    grad_values = dv_b.reshape(1, rows, features)
    joined = jnp.concatenate([dq_b, dk_b], axis=1)
    mine = reduce_rows(local, partner_events, joined, myself, cycle_size)
    grad_wq = mine[:, :features].astype(jnp.bfloat16)
    grad_wk = mine[:, features:].astype(jnp.bfloat16)
    return (attended, grad_values, grad_wq, grad_wk)


def solution(mesh):
    placed = (
        P("dp", "ctx", None),
        P(),
        P(),
        P("dp", "ctx", None),
        P("dp", "ctx", None),
        P("dp", None),
        P("dp"),
        P("dp", None),
    )
    return jax.shard_map(
        body,
        mesh=mesh,
        in_specs=placed,
        out_specs=(P("dp", "ctx", None), P("dp", "ctx", None), P("ctx", None), P("ctx", None)),
        check_vma=False,
    )
```

```python
import jax
import jax.numpy as jnp
from jax import lax
from jax.experimental import pallas as pl
from jax.experimental.pallas import tpu as pltpu
from jax.sharding import PartitionSpec as P
import functools

HD = 128
SPAN = 3
BLOCK = 128
MAXLEN = 768


def shifted(value, axis, steps):
    count = lax.axis_size(axis)
    pairs = [(source, (source + steps) % count) for source in range(count)]
    return lax.ppermute(value, axis, pairs)


def exchange(value, axis, mask):
    count = lax.axis_size(axis)
    return lax.ppermute(value, axis, [(source, source ^ mask) for source in range(count)])


def pick(value, bit, axis):
    return (
        lax.dynamic_index_in_dim(value, bit, axis, keepdims=False),
        lax.dynamic_index_in_dim(value, 1 - bit, axis, keepdims=False),
    )


def reduce_kernel(groups, spread, part_ref, out_ref, sent, landed, sums, mixed, finals, sems):
    me = lax.axis_index("ctx")
    group = lax.axis_index("dp")
    core = me % 2
    slot = me // 2
    mesh_id = pl.DeviceIdType.MESH
    barrier = pltpu.get_barrier_semaphore()
    for step in range(1, groups):
        peer = 2 * ((slot + step) % groups) + core
        pl.semaphore_signal(barrier, inc=1, device_id=(group, peer), device_id_type=mesh_id)
    for step in range(1, spread):
        pl.semaphore_signal(barrier, inc=1, device_id=((group + step) % spread, me), device_id_type=mesh_id)
    pl.semaphore_wait(barrier, groups - 1 + spread - 1)
    sent[...] = part_ref[...].astype(sent.dtype)
    copies = []
    for step in range(1, spread):
        target = (group + step) % spread
        copy = pltpu.make_async_remote_copy(
            src_ref=sent.at[target],
            dst_ref=landed.at[group],
            send_sem=sems.at[0, step - 1],
            recv_sem=sems.at[1, step - 1],
            device_id=(target, me),
            device_id_type=mesh_id,
        )
        copy.start()
        copies.append(copy)
    for copy in copies:
        copy.wait()
    total = part_ref[group]
    for step in range(1, spread):
        total = total + landed[(group + spread - step) % spread].astype(jnp.float32)
    sums[...] = total.astype(sums.dtype)
    copies = []
    for step in range(1, groups):
        target = (slot + step) % groups
        copy = pltpu.make_async_remote_copy(
            src_ref=sums.at[target],
            dst_ref=mixed.at[slot],
            send_sem=sems.at[2, step - 1],
            recv_sem=sems.at[3, step - 1],
            device_id=(group, 2 * target + core),
            device_id_type=mesh_id,
        )
        copy.start()
        copies.append(copy)
    for copy in copies:
        copy.wait()
    result = part_ref[group, slot]
    for step in range(1, spread):
        result = result + landed[(group + spread - step) % spread, slot].astype(jnp.float32)
    for step in range(1, groups):
        result = result + mixed[(slot + groups - step) % groups].astype(jnp.float32)
    finals[group] = result
    copies = []
    for step in range(1, spread):
        target = (group + step) % spread
        copy = pltpu.make_async_remote_copy(
            src_ref=finals.at[group],
            dst_ref=finals.at[group],
            send_sem=sems.at[4, step - 1],
            recv_sem=sems.at[5, step - 1],
            device_id=(target, me),
            device_id_type=mesh_id,
        )
        copy.start()
        copies.append(copy)
    for copy in copies:
        copy.wait()
    out_ref[...] = finals[...]


def reduce_blocks(part, spread):
    groups, share, width = part.shape
    lanes = width // spread
    part = part.reshape(groups, share, spread, lanes).transpose(2, 0, 1, 3)
    vmem = pl.BlockSpec(memory_space=pltpu.VMEM)
    finals = pl.pallas_call(
        functools.partial(reduce_kernel, groups, spread),
        in_specs=[vmem],
        out_specs=vmem,
        out_shape=jax.ShapeDtypeStruct((spread, share, lanes), jnp.float32),
        scratch_shapes=[
            pltpu.VMEM((spread, groups, share, lanes), jnp.bfloat16),
            pltpu.VMEM((spread, groups, share, lanes), jnp.bfloat16),
            pltpu.VMEM((groups, share, lanes), jnp.bfloat16),
            pltpu.VMEM((groups, share, lanes), jnp.bfloat16),
            pltpu.VMEM((spread, share, lanes), jnp.float32),
            pltpu.SemaphoreType.DMA((6, max(groups, spread))),
        ],
        compiler_params=pltpu.CompilerParams(collective_id=1, has_side_effects=True),
    )(part)
    return finals.transpose(1, 0, 2).reshape(share, width)


def reduce_rows(local, partner_events, joined, myself, cycle_size):
    width = local.shape[1]
    share = width // cycle_size
    core = myself % 2
    partner_joined = exchange(joined, "ctx", 1)
    both_events = jnp.concatenate([local, partner_events], axis=0)
    both_joined = jnp.concatenate([joined, partner_joined], axis=0)
    halves = both_events.reshape(both_events.shape[0], width // (2 * share), 2, share)
    kept = lax.dynamic_index_in_dim(halves, core, 2, keepdims=False).reshape(both_events.shape[0], width // 2)
    acc = jnp.dot(kept.T, both_joined, preferred_element_type=jnp.float32)
    acc = acc.reshape(width // (2 * share), share, joined.shape[1])
    acc = reduce_blocks(acc, lax.axis_size("dp"))
    return acc


def tiles_kernel(span, alpha, scale, infoc, infor, *refs):
    count = 2 * span + 2
    qs = refs[0:count:2]
    gs = refs[1:count:2]
    ks = refs[count:2 * count:2]
    vs = refs[count + 1:2 * count:2]
    out_ref, dq_ref, dk_ref, dv_ref = refs[2 * count:]
    lanes = 2 * span + 1

    def valid(qa, ka):
        qpos = infoc[:, qa:qa + 1]
        quser = infoc[:, lanes + qa:lanes + qa + 1]
        kpos = infor[ka:ka + 1, :]
        kuser = infor[lanes + ka:lanes + ka + 1, :]
        kkept = infor[2 * lanes + ka:2 * lanes + ka + 1, :]
        return (quser == kuser) & (kpos <= qpos) & (kkept > 0)

    def terms(q, g, k, v, ok):
        z = lax.dot_general(q, k, (((1,), (1,)), ((), ())), preferred_element_type=jnp.float32) * alpha
        sig = 1.0 / (1.0 + jnp.exp(-z))
        weight = jnp.where(ok, scale, 0.0)
        att = (z * sig * weight).astype(jnp.bfloat16)
        dprod = lax.dot_general(g, v, (((1,), (1,)), ((), ())), preferred_element_type=jnp.float32)
        dsc = (dprod * sig * (1.0 + z * (1.0 - sig)) * weight * alpha).astype(jnp.bfloat16)
        return att, dsc

    def back(att, dsc, q, g):
        dk = lax.dot_general(dsc, q, (((0,), (0,)), ((), ())), preferred_element_type=jnp.float32)
        dv = lax.dot_general(att, g, (((0,), (0,)), ((), ())), preferred_element_type=jnp.float32)
        return dk, dv

    q0, g0, k0, v0 = qs[0][...], gs[0][...], ks[0][...], vs[0][...]
    att, dsc = terms(q0, g0, k0, v0, valid(span, span))
    out = jnp.dot(att, v0, preferred_element_type=jnp.float32)
    dq = jnp.dot(dsc, k0, preferred_element_type=jnp.float32)
    dk, dv = back(att, dsc, q0, g0)
    for step in range(1, span + 1):
        k, v = ks[step][...], vs[step][...]
        att, dsc = terms(q0, g0, k, v, valid(span, span - step))
        out = out + jnp.dot(att, v, preferred_element_type=jnp.float32)
        dq = dq + jnp.dot(dsc, k, preferred_element_type=jnp.float32)
        q, g = qs[step][...], gs[step][...]
        att, dsc = terms(q, g, k0, v0, valid(span + step, span))
        b, c = back(att, dsc, q, g)
        dk = dk + b
        dv = dv + c
    out_ref[...] = out.astype(out_ref.dtype)
    dq_ref[...] = dq.astype(dq_ref.dtype)
    dk_ref[...] = dk.astype(dk_ref.dtype)
    dv_ref[...] = dv.astype(dv_ref.dtype)


def attention_tiles(qg_list, kv_list, infoc, infor, nheads, alpha, scale):
    rows = qg_list[0].shape[0]
    span = len(qg_list) - 1
    blk = lambda offset: pl.BlockSpec((rows, HD), lambda h: (0, h + offset))
    full = lambda arr: pl.BlockSpec(arr.shape, lambda h: (0, 0))
    operands, specs = [infoc, infor], [full(infoc), full(infor)]
    for group in (qg_list, kv_list):
        for packed in group:
            operands += [packed, packed]
            specs += [blk(0), blk(nheads)]
    shape = jax.ShapeDtypeStruct((rows, nheads * HD), jnp.bfloat16)
    tile = rows * rows * HD * 2
    return pl.pallas_call(
        functools.partial(tiles_kernel, span, alpha, scale),
        grid=(nheads,),
        in_specs=specs,
        out_specs=[blk(0)] * 4,
        out_shape=[shape] * 4,
        cost_estimate=pl.CostEstimate(
            flops=nheads * (2 * span + 1) * 5 * tile,
            transcendentals=nheads * (2 * span + 1) * rows * rows,
            bytes_accessed=(2 * span + 2) * 2 * rows * nheads * HD * 2 * 2 + 4 * rows * nheads * HD * 2,
        ),
    )(*operands)


def scores(query, key, valid, scale, alpha):
    z = jnp.einsum("qhd,khd->hqk", query, key, preferred_element_type=jnp.float32) * alpha
    sig = jax.nn.sigmoid(z)
    weight = valid[None, :, :].astype(jnp.float32) * scale
    return z, sig, weight


def forward_terms(query, grad, key, value, valid, scale, alpha):
    z, sig, weight = scores(query, key, valid, scale, alpha)
    att = (z * sig * weight).astype(jnp.bfloat16)
    out = jnp.einsum("hqk,khd->qhd", att, value, preferred_element_type=jnp.float32)
    dprod = jnp.einsum("qhd,khd->hqk", grad, value, preferred_element_type=jnp.float32)
    dsc = (dprod * sig * (1.0 + z * (1.0 - sig)) * weight * alpha).astype(jnp.bfloat16)
    dquery = jnp.einsum("hqk,khd->qhd", dsc, key, preferred_element_type=jnp.float32)
    return out, dquery, att, dsc


def backward_terms(query, grad, key, value, valid, scale, alpha):
    z, sig, weight = scores(query, key, valid, scale, alpha)
    att = (z * sig * weight).astype(jnp.bfloat16)
    dprod = jnp.einsum("qhd,khd->hqk", grad, value, preferred_element_type=jnp.float32)
    dsc = (dprod * sig * (1.0 + z * (1.0 - sig)) * weight * alpha).astype(jnp.bfloat16)
    dkey = jnp.einsum("hqk,qhd->khd", dsc, query, preferred_element_type=jnp.float32)
    dvalue = jnp.einsum("hqk,qhd->khd", att, grad, preferred_element_type=jnp.float32)
    return dkey, dvalue


def body(events, w_query, w_key, values, grad_out, lengths, stream_shift, block_keep):
    rows = events.shape[1]
    features = w_query.shape[1]
    nheads = features // HD
    alpha = 1.0 / HD**0.5
    scale = 1.0 / MAXLEN**0.5
    local = events[0]
    queries = jnp.dot(local, w_query, preferred_element_type=jnp.float32).astype(jnp.bfloat16)
    keys = jnp.dot(local, w_key, preferred_element_type=jnp.float32).astype(jnp.bfloat16)
    cycle_size = lax.axis_size("ctx")
    myself = lax.axis_index("ctx")
    total = rows * cycle_size
    ends = jnp.cumsum(lengths[0])
    offset = stream_shift[0]
    keep = block_keep[0]
    blocks_all = jnp.arange(keep.shape[0], dtype=jnp.int32)
    within = jnp.arange(rows, dtype=jnp.int32)

    def describe(anchor):
        anchor = jnp.remainder(anchor, cycle_size)
        position = jnp.remainder(anchor * rows + within - offset, total)
        owner = jnp.sum((position[:, None] >= ends[None, :]).astype(jnp.int32), axis=1)
        which = position // BLOCK
        kept = (
            jnp.sum(jnp.where(which[:, None] == blocks_all[None, :], keep[None, :], 0), axis=1) > 0
        )
        return (position, owner, kept)

    def mask(qinfo, kinfo):
        return (
            (qinfo[1][:, None] == kinfo[1][None, :])
            & (kinfo[0][None, :] <= qinfo[0][:, None])
            & kinfo[2][None, :]
        )

    def split(packed):
        return (
            packed[:, :features].reshape(rows, nheads, HD),
            packed[:, features:].reshape(rows, nheads, HD),
        )

    partner_events = exchange(local, "ctx", 1)
    kv = jnp.concatenate([keys, values[0]], axis=1)
    qg = jnp.concatenate([queries, grad_out[0]], axis=1)
    kv_from = [None] + [shifted(kv, "ctx", step) for step in range(1, SPAN + 1)]
    qg_from = [None] + [shifted(qg, "ctx", -step) for step in range(1, SPAN + 1)]

    offsets = range(-SPAN, SPAN + 1)
    described = [describe(myself + offset) for offset in offsets]
    infor = jnp.stack(
        [d[0] for d in described] + [d[1] for d in described] + [d[2].astype(jnp.int32) for d in described]
    ).astype(jnp.int32)
    infoc = infor.T
    out_b, dq_b, dk_b, dv_b = attention_tiles(
        [qg] + qg_from[1:], [kv] + kv_from[1:], infoc, infor, nheads, alpha, scale
    )
    attended = out_b.reshape(1, rows, features)
    grad_values = dv_b.reshape(1, rows, features)
    joined = jnp.concatenate([dq_b, dk_b], axis=1)
    mine = reduce_rows(local, partner_events, joined, myself, cycle_size)
    grad_wq = mine[:, :features].astype(jnp.bfloat16)
    grad_wk = mine[:, features:].astype(jnp.bfloat16)
    return (attended, grad_values, grad_wq, grad_wk)


def solution(mesh):
    placed = (
        P("dp", "ctx", None),
        P(),
        P(),
        P("dp", "ctx", None),
        P("dp", "ctx", None),
        P("dp", None),
        P("dp"),
        P("dp", None),
    )
    return jax.shard_map(
        body,
        mesh=mesh,
        in_specs=placed,
        out_specs=(P("dp", "ctx", None), P("dp", "ctx", None), P("ctx", None), P("ctx", None)),
        check_vma=False,
    )
```

```python
import jax
import jax.numpy as jnp
from jax import lax
from jax.experimental import pallas as pl
from jax.experimental.pallas import tpu as pltpu
from jax.sharding import PartitionSpec as P
import functools

HD = 128
SPAN = 3
BLOCK = 128
MAXLEN = 768


def shifted(value, axis, steps):
    count = lax.axis_size(axis)
    pairs = [(source, (source + steps) % count) for source in range(count)]
    return lax.ppermute(value, axis, pairs)


def exchange(value, axis, mask):
    count = lax.axis_size(axis)
    return lax.ppermute(value, axis, [(source, source ^ mask) for source in range(count)])


def relayed(value, myself, sign):
    count = lax.axis_size("ctx")
    odd = myself % 2
    pairs = []
    for source in range(count):
        step = 3 if (source % 2 == 1) == (sign > 0) else 1
        pairs.append((source, (source + sign * step) % count))
    far = shifted(value, "ctx", 2 * sign)
    mixed = lax.ppermute(value, "ctx", pairs)
    swapped = exchange(far, "ctx", 1)
    lead = odd if sign > 0 else 1 - odd
    mixed_anchor = myself - sign * (3 - 2 * lead)
    swapped_anchor = myself - sign * (1 + 2 * lead)
    return [None, far, mixed, swapped], [myself - 2 * sign, mixed_anchor, swapped_anchor]


def pick(value, bit, axis):
    return (
        lax.dynamic_index_in_dim(value, bit, axis, keepdims=False),
        lax.dynamic_index_in_dim(value, 1 - bit, axis, keepdims=False),
    )


def reduce_kernel(groups, spread, part_ref, out_ref, sent, landed, sums, mixed, finals, sems):
    me = lax.axis_index("ctx")
    group = lax.axis_index("dp")
    core = me % 2
    slot = me // 2
    mesh_id = pl.DeviceIdType.MESH
    barrier = pltpu.get_barrier_semaphore()
    for step in range(1, groups):
        peer = 2 * ((slot + step) % groups) + core
        pl.semaphore_signal(barrier, inc=1, device_id=(group, peer), device_id_type=mesh_id)
    for step in range(1, spread):
        pl.semaphore_signal(barrier, inc=1, device_id=((group + step) % spread, me), device_id_type=mesh_id)
    pl.semaphore_wait(barrier, groups - 1 + spread - 1)
    sent[...] = part_ref[...].astype(sent.dtype)
    copies = []
    for step in range(1, spread):
        target = (group + step) % spread
        copy = pltpu.make_async_remote_copy(
            src_ref=sent.at[target],
            dst_ref=landed.at[group],
            send_sem=sems.at[0, step - 1],
            recv_sem=sems.at[1, step - 1],
            device_id=(target, me),
            device_id_type=mesh_id,
        )
        copy.start()
        copies.append(copy)
    for copy in copies:
        copy.wait()
    total = part_ref[group]
    for step in range(1, spread):
        total = total + landed[(group + spread - step) % spread].astype(jnp.float32)
    sums[...] = total.astype(sums.dtype)
    copies = []
    for step in range(1, groups):
        target = (slot + step) % groups
        copy = pltpu.make_async_remote_copy(
            src_ref=sums.at[target],
            dst_ref=mixed.at[slot],
            send_sem=sems.at[2, step - 1],
            recv_sem=sems.at[3, step - 1],
            device_id=(group, 2 * target + core),
            device_id_type=mesh_id,
        )
        copy.start()
        copies.append(copy)
    for copy in copies:
        copy.wait()
    result = part_ref[group, slot]
    for step in range(1, spread):
        result = result + landed[(group + spread - step) % spread, slot].astype(jnp.float32)
    for step in range(1, groups):
        result = result + mixed[(slot + groups - step) % groups].astype(jnp.float32)
    finals[group] = result
    copies = []
    for step in range(1, spread):
        target = (group + step) % spread
        copy = pltpu.make_async_remote_copy(
            src_ref=finals.at[group],
            dst_ref=finals.at[group],
            send_sem=sems.at[4, step - 1],
            recv_sem=sems.at[5, step - 1],
            device_id=(target, me),
            device_id_type=mesh_id,
        )
        copy.start()
        copies.append(copy)
    for copy in copies:
        copy.wait()
    out_ref[...] = finals[...]


def reduce_blocks(part, spread):
    groups, share, width = part.shape
    lanes = width // spread
    part = part.reshape(groups, share, spread, lanes).transpose(2, 0, 1, 3)
    vmem = pl.BlockSpec(memory_space=pltpu.VMEM)
    finals = pl.pallas_call(
        functools.partial(reduce_kernel, groups, spread),
        in_specs=[vmem],
        out_specs=vmem,
        out_shape=jax.ShapeDtypeStruct((spread, share, lanes), jnp.float32),
        scratch_shapes=[
            pltpu.VMEM((spread, groups, share, lanes), jnp.bfloat16),
            pltpu.VMEM((spread, groups, share, lanes), jnp.bfloat16),
            pltpu.VMEM((groups, share, lanes), jnp.bfloat16),
            pltpu.VMEM((groups, share, lanes), jnp.bfloat16),
            pltpu.VMEM((spread, share, lanes), jnp.float32),
            pltpu.SemaphoreType.DMA((6, max(groups, spread))),
        ],
        compiler_params=pltpu.CompilerParams(collective_id=1, has_side_effects=True),
    )(part)
    return finals.transpose(1, 0, 2).reshape(share, width)


def reduce_rows(local, partner_events, joined, myself, cycle_size):
    width = local.shape[1]
    share = width // cycle_size
    core = myself % 2
    partner_joined = exchange(joined, "ctx", 1)
    both_events = jnp.concatenate([local, partner_events], axis=0)
    both_joined = jnp.concatenate([joined, partner_joined], axis=0)
    halves = both_events.reshape(both_events.shape[0], width // (2 * share), 2, share)
    kept = lax.dynamic_index_in_dim(halves, core, 2, keepdims=False).reshape(both_events.shape[0], width // 2)
    acc = jnp.dot(kept.T, both_joined, preferred_element_type=jnp.float32)
    acc = acc.reshape(width // (2 * share), share, joined.shape[1])
    acc = reduce_blocks(acc, lax.axis_size("dp"))
    return acc


def tiles_kernel(span, alpha, scale, infoc, infor, *refs):
    count = 2 * span + 2
    qs = refs[0:count:2]
    gs = refs[1:count:2]
    ks = refs[count:2 * count:2]
    vs = refs[count + 1:2 * count:2]
    out_ref, dq_ref, dk_ref, dv_ref = refs[2 * count:]
    lanes = 2 * span + 1

    def valid(qa, ka):
        qpos = infoc[:, qa:qa + 1]
        quser = infoc[:, lanes + qa:lanes + qa + 1]
        kpos = infor[ka:ka + 1, :]
        kuser = infor[lanes + ka:lanes + ka + 1, :]
        kkept = infor[2 * lanes + ka:2 * lanes + ka + 1, :]
        return (quser == kuser) & (kpos <= qpos) & (kkept > 0)

    def terms(q, g, k, v, ok):
        z = lax.dot_general(q, k, (((1,), (1,)), ((), ())), preferred_element_type=jnp.float32) * alpha
        sig = 1.0 / (1.0 + jnp.exp(-z))
        weight = jnp.where(ok, scale, 0.0)
        att = (z * sig * weight).astype(jnp.bfloat16)
        dprod = lax.dot_general(g, v, (((1,), (1,)), ((), ())), preferred_element_type=jnp.float32)
        dsc = (dprod * sig * (1.0 + z * (1.0 - sig)) * weight * alpha).astype(jnp.bfloat16)
        return att, dsc

    def back(att, dsc, q, g):
        dk = lax.dot_general(dsc, q, (((0,), (0,)), ((), ())), preferred_element_type=jnp.float32)
        dv = lax.dot_general(att, g, (((0,), (0,)), ((), ())), preferred_element_type=jnp.float32)
        return dk, dv

    q0, g0, k0, v0 = qs[0][...], gs[0][...], ks[0][...], vs[0][...]
    att, dsc = terms(q0, g0, k0, v0, valid(0, 0))
    out = jnp.dot(att, v0, preferred_element_type=jnp.float32)
    dq = jnp.dot(dsc, k0, preferred_element_type=jnp.float32)
    dk, dv = back(att, dsc, q0, g0)
    for step in range(1, span + 1):
        k, v = ks[step][...], vs[step][...]
        att, dsc = terms(q0, g0, k, v, valid(0, step))
        out = out + jnp.dot(att, v, preferred_element_type=jnp.float32)
        dq = dq + jnp.dot(dsc, k, preferred_element_type=jnp.float32)
        q, g = qs[step][...], gs[step][...]
        att, dsc = terms(q, g, k0, v0, valid(span + step, 0))
        b, c = back(att, dsc, q, g)
        dk = dk + b
        dv = dv + c
    out_ref[...] = out.astype(out_ref.dtype)
    dq_ref[...] = dq.astype(dq_ref.dtype)
    dk_ref[...] = dk.astype(dk_ref.dtype)
    dv_ref[...] = dv.astype(dv_ref.dtype)


def attention_tiles(qg_list, kv_list, infoc, infor, nheads, alpha, scale):
    rows = qg_list[0].shape[0]
    span = len(qg_list) - 1
    blk = lambda offset: pl.BlockSpec((rows, HD), lambda h: (0, h + offset))
    full = lambda arr: pl.BlockSpec(arr.shape, lambda h: (0, 0))
    operands, specs = [infoc, infor], [full(infoc), full(infor)]
    for group in (qg_list, kv_list):
        for packed in group:
            operands += [packed, packed]
            specs += [blk(0), blk(nheads)]
    shape = jax.ShapeDtypeStruct((rows, nheads * HD), jnp.bfloat16)
    tile = rows * rows * HD * 2
    return pl.pallas_call(
        functools.partial(tiles_kernel, span, alpha, scale),
        grid=(nheads,),
        in_specs=specs,
        out_specs=[blk(0)] * 4,
        out_shape=[shape] * 4,
        cost_estimate=pl.CostEstimate(
            flops=nheads * (2 * span + 1) * 5 * tile,
            transcendentals=nheads * (2 * span + 1) * rows * rows,
            bytes_accessed=(2 * span + 2) * 2 * rows * nheads * HD * 2 * 2 + 4 * rows * nheads * HD * 2,
        ),
    )(*operands)


def scores(query, key, valid, scale, alpha):
    z = jnp.einsum("qhd,khd->hqk", query, key, preferred_element_type=jnp.float32) * alpha
    sig = jax.nn.sigmoid(z)
    weight = valid[None, :, :].astype(jnp.float32) * scale
    return z, sig, weight


def forward_terms(query, grad, key, value, valid, scale, alpha):
    z, sig, weight = scores(query, key, valid, scale, alpha)
    att = (z * sig * weight).astype(jnp.bfloat16)
    out = jnp.einsum("hqk,khd->qhd", att, value, preferred_element_type=jnp.float32)
    dprod = jnp.einsum("qhd,khd->hqk", grad, value, preferred_element_type=jnp.float32)
    dsc = (dprod * sig * (1.0 + z * (1.0 - sig)) * weight * alpha).astype(jnp.bfloat16)
    dquery = jnp.einsum("hqk,khd->qhd", dsc, key, preferred_element_type=jnp.float32)
    return out, dquery, att, dsc


def backward_terms(query, grad, key, value, valid, scale, alpha):
    z, sig, weight = scores(query, key, valid, scale, alpha)
    att = (z * sig * weight).astype(jnp.bfloat16)
    dprod = jnp.einsum("qhd,khd->hqk", grad, value, preferred_element_type=jnp.float32)
    dsc = (dprod * sig * (1.0 + z * (1.0 - sig)) * weight * alpha).astype(jnp.bfloat16)
    dkey = jnp.einsum("hqk,qhd->khd", dsc, query, preferred_element_type=jnp.float32)
    dvalue = jnp.einsum("hqk,qhd->khd", att, grad, preferred_element_type=jnp.float32)
    return dkey, dvalue


def body(events, w_query, w_key, values, grad_out, lengths, stream_shift, block_keep):
    rows = events.shape[1]
    features = w_query.shape[1]
    nheads = features // HD
    alpha = 1.0 / HD**0.5
    scale = 1.0 / MAXLEN**0.5
    local = events[0]
    queries = jnp.dot(local, w_query, preferred_element_type=jnp.float32).astype(jnp.bfloat16)
    keys = jnp.dot(local, w_key, preferred_element_type=jnp.float32).astype(jnp.bfloat16)
    cycle_size = lax.axis_size("ctx")
    myself = lax.axis_index("ctx")
    total = rows * cycle_size
    ends = jnp.cumsum(lengths[0])
    offset = stream_shift[0]
    keep = block_keep[0]
    blocks_all = jnp.arange(keep.shape[0], dtype=jnp.int32)
    within = jnp.arange(rows, dtype=jnp.int32)

    def describe(anchor):
        anchor = jnp.remainder(anchor, cycle_size)
        position = jnp.remainder(anchor * rows + within - offset, total)
        owner = jnp.sum((position[:, None] >= ends[None, :]).astype(jnp.int32), axis=1)
        which = position // BLOCK
        kept = (
            jnp.sum(jnp.where(which[:, None] == blocks_all[None, :], keep[None, :], 0), axis=1) > 0
        )
        return (position, owner, kept)

    def mask(qinfo, kinfo):
        return (
            (qinfo[1][:, None] == kinfo[1][None, :])
            & (kinfo[0][None, :] <= qinfo[0][:, None])
            & kinfo[2][None, :]
        )

    def split(packed):
        return (
            packed[:, :features].reshape(rows, nheads, HD),
            packed[:, features:].reshape(rows, nheads, HD),
        )

    partner_events = exchange(local, "ctx", 1)
    kv = jnp.concatenate([keys, values[0]], axis=1)
    qg = jnp.concatenate([queries, grad_out[0]], axis=1)
    kv_from, kv_anchor = relayed(kv, myself, 1)
    qg_from, qg_anchor = relayed(qg, myself, -1)

    described = [describe(anchor) for anchor in [myself] + kv_anchor + qg_anchor]
    infor = jnp.stack(
        [d[0] for d in described] + [d[1] for d in described] + [d[2].astype(jnp.int32) for d in described]
    ).astype(jnp.int32)
    infoc = infor.T
    out_b, dq_b, dk_b, dv_b = attention_tiles(
        [qg] + qg_from[1:], [kv] + kv_from[1:], infoc, infor, nheads, alpha, scale
    )
    attended = out_b.reshape(1, rows, features)
    grad_values = dv_b.reshape(1, rows, features)
    joined = jnp.concatenate([dq_b, dk_b], axis=1)
    mine = reduce_rows(local, partner_events, joined, myself, cycle_size)
    grad_wq = mine[:, :features].astype(jnp.bfloat16)
    grad_wk = mine[:, features:].astype(jnp.bfloat16)
    return (attended, grad_values, grad_wq, grad_wk)


def solution(mesh):
    placed = (
        P("dp", "ctx", None),
        P(),
        P(),
        P("dp", "ctx", None),
        P("dp", "ctx", None),
        P("dp", None),
        P("dp"),
        P("dp", None),
    )
    return jax.shard_map(
        body,
        mesh=mesh,
        in_specs=placed,
        out_specs=(P("dp", "ctx", None), P("dp", "ctx", None), P("ctx", None), P("ctx", None)),
        check_vma=False,
    )
```

```python
import jax
import jax.numpy as jnp
from jax import lax
from jax.experimental import pallas as pl
from jax.experimental.pallas import tpu as pltpu
from jax.sharding import PartitionSpec as P
import functools

HD = 128
SPAN = 3
BLOCK = 128
MAXLEN = 768


def shifted(value, axis, steps):
    count = lax.axis_size(axis)
    pairs = [(source, (source + steps) % count) for source in range(count)]
    return lax.ppermute(value, axis, pairs)


def exchange(value, axis, mask):
    count = lax.axis_size(axis)
    return lax.ppermute(value, axis, [(source, source ^ mask) for source in range(count)])


def relayed(value, myself, sign):
    count = lax.axis_size("ctx")
    odd = myself % 2
    pairs = []
    for source in range(count):
        step = 3 if (source % 2 == 1) == (sign > 0) else 1
        pairs.append((source, (source + sign * step) % count))
    far = shifted(value, "ctx", 2 * sign)
    mixed = lax.ppermute(value, "ctx", pairs)
    swapped = exchange(far, "ctx", 1)
    lead = odd if sign > 0 else 1 - odd
    mixed_anchor = myself - sign * (3 - 2 * lead)
    swapped_anchor = myself - sign * (1 + 2 * lead)
    return [None, far, mixed, swapped], [myself - 2 * sign, mixed_anchor, swapped_anchor]


def pick(value, bit, axis):
    return (
        lax.dynamic_index_in_dim(value, bit, axis, keepdims=False),
        lax.dynamic_index_in_dim(value, 1 - bit, axis, keepdims=False),
    )


def reduce_kernel(groups, spread, xsel_ref, joined_ref, out_ref, joined_land, part_ref, sent, landed, sums, mixed, finals, sems):
    me = lax.axis_index("ctx")
    group = lax.axis_index("dp")
    core = me % 2
    slot = me // 2
    mesh_id = pl.DeviceIdType.MESH
    barrier = pltpu.get_barrier_semaphore()
    for step in range(1, groups):
        peer = 2 * ((slot + step) % groups) + core
        pl.semaphore_signal(barrier, inc=1, device_id=(group, peer), device_id_type=mesh_id)
    for step in range(1, spread):
        pl.semaphore_signal(barrier, inc=1, device_id=((group + step) % spread, me), device_id_type=mesh_id)
    partner = me + 1 - 2 * core
    pl.semaphore_signal(barrier, inc=1, device_id=(group, partner), device_id_type=mesh_id)
    pl.semaphore_wait(barrier, groups - 1 + spread - 1 + 1)
    pair = pltpu.make_async_remote_copy(
        src_ref=joined_ref,
        dst_ref=joined_land,
        send_sem=sems.at[6, 0],
        recv_sem=sems.at[6, 1],
        device_id=(group, partner),
        device_id_type=mesh_id,
    )
    pair.start()
    rows = joined_ref.shape[0]
    contract = (((0,), (0,)), ((), ()))
    acc = lax.dot_general(xsel_ref[:rows], joined_ref[...], contract, preferred_element_type=jnp.float32)
    pair.wait()
    acc = acc + lax.dot_general(xsel_ref[rows:], joined_land[...], contract, preferred_element_type=jnp.float32)
    _, _, share, lanes = part_ref.shape
    for index in range(spread):
        part_ref[index] = acc[:, index * lanes:(index + 1) * lanes].reshape(groups, share, lanes)
    sent[...] = part_ref[...].astype(sent.dtype)
    copies = []
    for step in range(1, spread):
        target = (group + step) % spread
        copy = pltpu.make_async_remote_copy(
            src_ref=sent.at[target],
            dst_ref=landed.at[group],
            send_sem=sems.at[0, step - 1],
            recv_sem=sems.at[1, step - 1],
            device_id=(target, me),
            device_id_type=mesh_id,
        )
        copy.start()
        copies.append(copy)
    for copy in copies:
        copy.wait()
    total = part_ref[group]
    for step in range(1, spread):
        total = total + landed[(group + spread - step) % spread].astype(jnp.float32)
    sums[...] = total.astype(sums.dtype)
    copies = []
    for step in range(1, groups):
        target = (slot + step) % groups
        copy = pltpu.make_async_remote_copy(
            src_ref=sums.at[target],
            dst_ref=mixed.at[slot],
            send_sem=sems.at[2, step - 1],
            recv_sem=sems.at[3, step - 1],
            device_id=(group, 2 * target + core),
            device_id_type=mesh_id,
        )
        copy.start()
        copies.append(copy)
    for copy in copies:
        copy.wait()
    result = part_ref[group, slot]
    for step in range(1, spread):
        result = result + landed[(group + spread - step) % spread, slot].astype(jnp.float32)
    for step in range(1, groups):
        result = result + mixed[(slot + groups - step) % groups].astype(jnp.float32)
    finals[group] = result
    copies = []
    for step in range(1, spread):
        target = (group + step) % spread
        copy = pltpu.make_async_remote_copy(
            src_ref=finals.at[group],
            dst_ref=finals.at[group],
            send_sem=sems.at[4, step - 1],
            recv_sem=sems.at[5, step - 1],
            device_id=(target, me),
            device_id_type=mesh_id,
        )
        copy.start()
        copies.append(copy)
    for copy in copies:
        copy.wait()
    out_ref[...] = finals[...]


def reduce_blocks(xsel, joined, share, spread):
    rows, width = joined.shape
    groups = xsel.shape[1] // share
    lanes = width // spread
    vmem = pl.BlockSpec(memory_space=pltpu.VMEM)
    finals = pl.pallas_call(
        functools.partial(reduce_kernel, groups, spread),
        in_specs=[vmem, vmem],
        out_specs=vmem,
        out_shape=jax.ShapeDtypeStruct((spread, share, lanes), jnp.float32),
        scratch_shapes=[
            pltpu.VMEM((rows, width), jnp.bfloat16),
            pltpu.VMEM((spread, groups, share, lanes), jnp.float32),
            pltpu.VMEM((spread, groups, share, lanes), jnp.bfloat16),
            pltpu.VMEM((spread, groups, share, lanes), jnp.bfloat16),
            pltpu.VMEM((groups, share, lanes), jnp.bfloat16),
            pltpu.VMEM((groups, share, lanes), jnp.bfloat16),
            pltpu.VMEM((spread, share, lanes), jnp.float32),
            pltpu.SemaphoreType.DMA((7, max(groups, spread))),
        ],
        compiler_params=pltpu.CompilerParams(collective_id=1, has_side_effects=True),
    )(xsel, joined)
    return finals.transpose(1, 0, 2).reshape(share, width)


def reduce_rows(local, partner_events, joined, myself, cycle_size):
    width = local.shape[1]
    share = width // cycle_size
    core = myself % 2
    both_events = jnp.concatenate([local, partner_events], axis=0)
    halves = both_events.reshape(both_events.shape[0], width // (2 * share), 2, share)
    kept = lax.dynamic_index_in_dim(halves, core, 2, keepdims=False).reshape(both_events.shape[0], width // 2)
    acc = reduce_blocks(kept, joined, share, lax.axis_size("dp"))
    return acc


def tiles_kernel(span, alpha, scale, infoc, infor, *refs):
    count = 2 * span + 2
    qs = refs[0:count:2]
    gs = refs[1:count:2]
    ks = refs[count:2 * count:2]
    vs = refs[count + 1:2 * count:2]
    out_ref, dq_ref, dk_ref, dv_ref = refs[2 * count:]
    lanes = 2 * span + 1

    def valid(qa, ka):
        qpos = infoc[:, qa:qa + 1]
        quser = infoc[:, lanes + qa:lanes + qa + 1]
        kpos = infor[ka:ka + 1, :]
        kuser = infor[lanes + ka:lanes + ka + 1, :]
        kkept = infor[2 * lanes + ka:2 * lanes + ka + 1, :]
        return (quser == kuser) & (kpos <= qpos) & (kkept > 0)

    def terms(q, g, k, v, ok):
        z = lax.dot_general(q, k, (((1,), (1,)), ((), ())), preferred_element_type=jnp.float32) * alpha
        sig = 1.0 / (1.0 + jnp.exp(-z))
        weight = jnp.where(ok, scale, 0.0)
        att = (z * sig * weight).astype(jnp.bfloat16)
        dprod = lax.dot_general(g, v, (((1,), (1,)), ((), ())), preferred_element_type=jnp.float32)
        dsc = (dprod * sig * (1.0 + z * (1.0 - sig)) * weight * alpha).astype(jnp.bfloat16)
        return att, dsc

    def back(att, dsc, q, g):
        dk = lax.dot_general(dsc, q, (((0,), (0,)), ((), ())), preferred_element_type=jnp.float32)
        dv = lax.dot_general(att, g, (((0,), (0,)), ((), ())), preferred_element_type=jnp.float32)
        return dk, dv

    q0, g0, k0, v0 = qs[0][...], gs[0][...], ks[0][...], vs[0][...]
    att, dsc = terms(q0, g0, k0, v0, valid(0, 0))
    out = jnp.dot(att, v0, preferred_element_type=jnp.float32)
    dq = jnp.dot(dsc, k0, preferred_element_type=jnp.float32)
    dk, dv = back(att, dsc, q0, g0)
    for step in range(1, span + 1):
        k, v = ks[step][...], vs[step][...]
        att, dsc = terms(q0, g0, k, v, valid(0, step))
        out = out + jnp.dot(att, v, preferred_element_type=jnp.float32)
        dq = dq + jnp.dot(dsc, k, preferred_element_type=jnp.float32)
        q, g = qs[step][...], gs[step][...]
        att, dsc = terms(q, g, k0, v0, valid(span + step, 0))
        b, c = back(att, dsc, q, g)
        dk = dk + b
        dv = dv + c
    out_ref[...] = out.astype(out_ref.dtype)
    dq_ref[...] = dq.astype(dq_ref.dtype)
    dk_ref[...] = dk.astype(dk_ref.dtype)
    dv_ref[...] = dv.astype(dv_ref.dtype)


def attention_tiles(qg_list, kv_list, infoc, infor, nheads, alpha, scale):
    rows = qg_list[0].shape[0]
    span = len(qg_list) - 1
    blk = lambda offset: pl.BlockSpec((rows, HD), lambda h: (0, h + offset))
    full = lambda arr: pl.BlockSpec(arr.shape, lambda h: (0, 0))
    operands, specs = [infoc, infor], [full(infoc), full(infor)]
    for group in (qg_list, kv_list):
        for packed in group:
            operands += [packed, packed]
            specs += [blk(0), blk(nheads)]
    shape = jax.ShapeDtypeStruct((rows, nheads * HD), jnp.bfloat16)
    tile = rows * rows * HD * 2
    return pl.pallas_call(
        functools.partial(tiles_kernel, span, alpha, scale),
        grid=(nheads,),
        in_specs=specs,
        out_specs=[blk(0)] * 4,
        out_shape=[shape] * 4,
        cost_estimate=pl.CostEstimate(
            flops=nheads * (2 * span + 1) * 5 * tile,
            transcendentals=nheads * (2 * span + 1) * rows * rows,
            bytes_accessed=(2 * span + 2) * 2 * rows * nheads * HD * 2 * 2 + 4 * rows * nheads * HD * 2,
        ),
    )(*operands)


def scores(query, key, valid, scale, alpha):
    z = jnp.einsum("qhd,khd->hqk", query, key, preferred_element_type=jnp.float32) * alpha
    sig = jax.nn.sigmoid(z)
    weight = valid[None, :, :].astype(jnp.float32) * scale
    return z, sig, weight


def forward_terms(query, grad, key, value, valid, scale, alpha):
    z, sig, weight = scores(query, key, valid, scale, alpha)
    att = (z * sig * weight).astype(jnp.bfloat16)
    out = jnp.einsum("hqk,khd->qhd", att, value, preferred_element_type=jnp.float32)
    dprod = jnp.einsum("qhd,khd->hqk", grad, value, preferred_element_type=jnp.float32)
    dsc = (dprod * sig * (1.0 + z * (1.0 - sig)) * weight * alpha).astype(jnp.bfloat16)
    dquery = jnp.einsum("hqk,khd->qhd", dsc, key, preferred_element_type=jnp.float32)
    return out, dquery, att, dsc


def backward_terms(query, grad, key, value, valid, scale, alpha):
    z, sig, weight = scores(query, key, valid, scale, alpha)
    att = (z * sig * weight).astype(jnp.bfloat16)
    dprod = jnp.einsum("qhd,khd->hqk", grad, value, preferred_element_type=jnp.float32)
    dsc = (dprod * sig * (1.0 + z * (1.0 - sig)) * weight * alpha).astype(jnp.bfloat16)
    dkey = jnp.einsum("hqk,qhd->khd", dsc, query, preferred_element_type=jnp.float32)
    dvalue = jnp.einsum("hqk,qhd->khd", att, grad, preferred_element_type=jnp.float32)
    return dkey, dvalue


def body(events, w_query, w_key, values, grad_out, lengths, stream_shift, block_keep):
    rows = events.shape[1]
    features = w_query.shape[1]
    nheads = features // HD
    alpha = 1.0 / HD**0.5
    scale = 1.0 / MAXLEN**0.5
    local = events[0]
    queries = jnp.dot(local, w_query, preferred_element_type=jnp.float32).astype(jnp.bfloat16)
    keys = jnp.dot(local, w_key, preferred_element_type=jnp.float32).astype(jnp.bfloat16)
    cycle_size = lax.axis_size("ctx")
    myself = lax.axis_index("ctx")
    total = rows * cycle_size
    ends = jnp.cumsum(lengths[0])
    offset = stream_shift[0]
    keep = block_keep[0]
    blocks_all = jnp.arange(keep.shape[0], dtype=jnp.int32)
    within = jnp.arange(rows, dtype=jnp.int32)

    def describe(anchor):
        anchor = jnp.remainder(anchor, cycle_size)
        position = jnp.remainder(anchor * rows + within - offset, total)
        owner = jnp.sum((position[:, None] >= ends[None, :]).astype(jnp.int32), axis=1)
        which = position // BLOCK
        kept = (
            jnp.sum(jnp.where(which[:, None] == blocks_all[None, :], keep[None, :], 0), axis=1) > 0
        )
        return (position, owner, kept)

    def mask(qinfo, kinfo):
        return (
            (qinfo[1][:, None] == kinfo[1][None, :])
            & (kinfo[0][None, :] <= qinfo[0][:, None])
            & kinfo[2][None, :]
        )

    def split(packed):
        return (
            packed[:, :features].reshape(rows, nheads, HD),
            packed[:, features:].reshape(rows, nheads, HD),
        )

    partner_events = exchange(local, "ctx", 1)
    kv = jnp.concatenate([keys, values[0]], axis=1)
    qg = jnp.concatenate([queries, grad_out[0]], axis=1)
    kv_from, kv_anchor = relayed(kv, myself, 1)
    qg_from, qg_anchor = relayed(qg, myself, -1)

    described = [describe(anchor) for anchor in [myself] + kv_anchor + qg_anchor]
    infor = jnp.stack(
        [d[0] for d in described] + [d[1] for d in described] + [d[2].astype(jnp.int32) for d in described]
    ).astype(jnp.int32)
    infoc = infor.T
    out_b, dq_b, dk_b, dv_b = attention_tiles(
        [qg] + qg_from[1:], [kv] + kv_from[1:], infoc, infor, nheads, alpha, scale
    )
    attended = out_b.reshape(1, rows, features)
    grad_values = dv_b.reshape(1, rows, features)
    joined = jnp.concatenate([dq_b, dk_b], axis=1)
    mine = reduce_rows(local, partner_events, joined, myself, cycle_size)
    grad_wq = mine[:, :features].astype(jnp.bfloat16)
    grad_wk = mine[:, features:].astype(jnp.bfloat16)
    return (attended, grad_values, grad_wq, grad_wk)


def solution(mesh):
    placed = (
        P("dp", "ctx", None),
        P(),
        P(),
        P("dp", "ctx", None),
        P("dp", "ctx", None),
        P("dp", None),
        P("dp"),
        P("dp", None),
    )
    return jax.shard_map(
        body,
        mesh=mesh,
        in_specs=placed,
        out_specs=(P("dp", "ctx", None), P("dp", "ctx", None), P("ctx", None), P("ctx", None)),
        check_vma=False,
    )
```

```python
import jax
import jax.numpy as jnp
from jax import lax
from jax.experimental import pallas as pl
from jax.experimental.pallas import tpu as pltpu
from jax.sharding import PartitionSpec as P
import functools

HD = 128
SPAN = 3
BLOCK = 128
MAXLEN = 768


def shifted(value, axis, steps):
    count = lax.axis_size(axis)
    pairs = [(source, (source + steps) % count) for source in range(count)]
    return lax.ppermute(value, axis, pairs)


def exchange(value, axis, mask):
    count = lax.axis_size(axis)
    return lax.ppermute(value, axis, [(source, source ^ mask) for source in range(count)])


def relayed(value, myself, sign):
    count = lax.axis_size("ctx")
    odd = myself % 2
    pairs = []
    for source in range(count):
        step = 3 if (source % 2 == 1) == (sign > 0) else 1
        pairs.append((source, (source + sign * step) % count))
    far = shifted(value, "ctx", 2 * sign)
    mixed = lax.ppermute(value, "ctx", pairs)
    swapped = exchange(far, "ctx", 1)
    lead = odd if sign > 0 else 1 - odd
    mixed_anchor = myself - sign * (3 - 2 * lead)
    swapped_anchor = myself - sign * (1 + 2 * lead)
    return [None, far, mixed, swapped], [myself - 2 * sign, mixed_anchor, swapped_anchor]


def pick(value, bit, axis):
    return (
        lax.dynamic_index_in_dim(value, bit, axis, keepdims=False),
        lax.dynamic_index_in_dim(value, 1 - bit, axis, keepdims=False),
    )


def reduce_kernel(groups, spread, xsel_ref, joined_ref, out_ref, joined_land, part_ref, sent, landed, sums, mixed, finals, sems):
    me = lax.axis_index("ctx")
    group = lax.axis_index("dp")
    core = me % 2
    slot = me // 2
    mesh_id = pl.DeviceIdType.MESH
    barrier = pltpu.get_barrier_semaphore()
    for step in range(1, groups):
        peer = 2 * ((slot + step) % groups) + core
        pl.semaphore_signal(barrier, inc=1, device_id=(group, peer), device_id_type=mesh_id)
    for step in range(1, spread):
        pl.semaphore_signal(barrier, inc=1, device_id=((group + step) % spread, me), device_id_type=mesh_id)
    partner = me + 1 - 2 * core
    pl.semaphore_signal(barrier, inc=1, device_id=(group, partner), device_id_type=mesh_id)
    pl.semaphore_wait(barrier, groups - 1 + spread - 1 + 1)
    pair = pltpu.make_async_remote_copy(
        src_ref=joined_ref,
        dst_ref=joined_land,
        send_sem=sems.at[6, 0],
        recv_sem=sems.at[6, 1],
        device_id=(group, partner),
        device_id_type=mesh_id,
    )
    pair.start()
    rows = joined_ref.shape[0]
    contract = (((0,), (0,)), ((), ()))
    acc = lax.dot_general(xsel_ref[:rows], joined_ref[...], contract, preferred_element_type=jnp.float32)
    pair.wait()
    acc = acc + lax.dot_general(xsel_ref[rows:], joined_land[...], contract, preferred_element_type=jnp.float32)
    _, _, share, lanes = part_ref.shape
    for index in range(spread):
        part_ref[index] = acc[:, index * lanes:(index + 1) * lanes].reshape(groups, share, lanes)
    sent[...] = part_ref[...].astype(sent.dtype)
    copies = []
    for step in range(1, spread):
        target = (group + step) % spread
        copy = pltpu.make_async_remote_copy(
            src_ref=sent.at[target],
            dst_ref=landed.at[group],
            send_sem=sems.at[0, step - 1],
            recv_sem=sems.at[1, step - 1],
            device_id=(target, me),
            device_id_type=mesh_id,
        )
        copy.start()
        copies.append(copy)
    for copy in copies:
        copy.wait()
    total = part_ref[group]
    for step in range(1, spread):
        total = total + landed[(group + spread - step) % spread].astype(jnp.float32)
    sums[...] = total.astype(sums.dtype)
    copies = []
    for step in range(1, groups):
        target = (slot + step) % groups
        copy = pltpu.make_async_remote_copy(
            src_ref=sums.at[target],
            dst_ref=mixed.at[slot],
            send_sem=sems.at[2, step - 1],
            recv_sem=sems.at[3, step - 1],
            device_id=(group, 2 * target + core),
            device_id_type=mesh_id,
        )
        copy.start()
        copies.append(copy)
    for copy in copies:
        copy.wait()
    result = part_ref[group, slot]
    for step in range(1, spread):
        result = result + landed[(group + spread - step) % spread, slot].astype(jnp.float32)
    for step in range(1, groups):
        result = result + mixed[(slot + groups - step) % groups].astype(jnp.float32)
    finals[group] = result
    copies = []
    for step in range(1, spread):
        target = (group + step) % spread
        copy = pltpu.make_async_remote_copy(
            src_ref=finals.at[group],
            dst_ref=finals.at[group],
            send_sem=sems.at[4, step - 1],
            recv_sem=sems.at[5, step - 1],
            device_id=(target, me),
            device_id_type=mesh_id,
        )
        copy.start()
        copies.append(copy)
    for copy in copies:
        copy.wait()
    out_ref[...] = finals[...]


def reduce_blocks(xsel, joined, share, spread):
    rows, width = joined.shape
    groups = xsel.shape[1] // share
    lanes = width // spread
    vmem = pl.BlockSpec(memory_space=pltpu.VMEM)
    finals = pl.pallas_call(
        functools.partial(reduce_kernel, groups, spread),
        in_specs=[vmem, vmem],
        out_specs=vmem,
        out_shape=jax.ShapeDtypeStruct((spread, share, lanes), jnp.float32),
        scratch_shapes=[
            pltpu.VMEM((rows, width), jnp.bfloat16),
            pltpu.VMEM((spread, groups, share, lanes), jnp.float32),
            pltpu.VMEM((spread, groups, share, lanes), jnp.bfloat16),
            pltpu.VMEM((spread, groups, share, lanes), jnp.bfloat16),
            pltpu.VMEM((groups, share, lanes), jnp.bfloat16),
            pltpu.VMEM((groups, share, lanes), jnp.bfloat16),
            pltpu.VMEM((spread, share, lanes), jnp.float32),
            pltpu.SemaphoreType.DMA((7, max(groups, spread))),
        ],
        compiler_params=pltpu.CompilerParams(collective_id=1, has_side_effects=True),
    )(xsel, joined)
    return finals.transpose(1, 0, 2).reshape(share, width)


def reduce_rows(local, partner_events, joined, myself, cycle_size):
    width = local.shape[1]
    share = width // cycle_size
    core = myself % 2
    both_events = jnp.concatenate([local, partner_events], axis=0)
    halves = both_events.reshape(both_events.shape[0], width // (2 * share), 2, share)
    kept = lax.dynamic_index_in_dim(halves, core, 2, keepdims=False).reshape(both_events.shape[0], width // 2)
    acc = reduce_blocks(kept, joined, share, lax.axis_size("dp"))
    return acc


def tiles_kernel(span, alpha, scale, infoc, infor, *refs):
    count = 2 * span + 2
    qs = refs[0:count:2]
    gs = refs[1:count:2]
    ks = refs[count:2 * count:2]
    vs = refs[count + 1:2 * count:2]
    out_ref, dq_ref, dk_ref, dv_ref = refs[2 * count:]
    lanes = 2 * span + 1

    def valid(qa, ka):
        qpos = infoc[:, qa:qa + 1]
        quser = infoc[:, lanes + qa:lanes + qa + 1]
        kpos = infor[ka:ka + 1, :]
        kuser = infor[lanes + ka:lanes + ka + 1, :]
        kkept = infor[2 * lanes + ka:2 * lanes + ka + 1, :]
        return (quser == kuser) & (kpos <= qpos) & (kkept > 0)

    def terms(q, g, k, v, ok):
        z = lax.dot_general(q, k, (((1,), (1,)), ((), ())), preferred_element_type=jnp.float32) * alpha
        sig = 1.0 / (1.0 + jnp.exp(-z))
        weight = jnp.where(ok, scale, 0.0)
        att = (z * sig * weight).astype(jnp.bfloat16)
        dprod = lax.dot_general(g, v, (((1,), (1,)), ((), ())), preferred_element_type=jnp.float32)
        dsc = (dprod * sig * (1.0 + z * (1.0 - sig)) * weight * alpha).astype(jnp.bfloat16)
        return att, dsc

    def back(att, dsc, q, g):
        dk = lax.dot_general(dsc, q, (((0,), (0,)), ((), ())), preferred_element_type=jnp.float32)
        dv = lax.dot_general(att, g, (((0,), (0,)), ((), ())), preferred_element_type=jnp.float32)
        return dk, dv

    q0, g0, k0, v0 = qs[0][...], gs[0][...], ks[0][...], vs[0][...]
    att, dsc = terms(q0, g0, k0, v0, valid(0, 0))
    out = jnp.dot(att, v0, preferred_element_type=jnp.float32)
    dq = jnp.dot(dsc, k0, preferred_element_type=jnp.float32)
    dk, dv = back(att, dsc, q0, g0)
    for step in range(1, span + 1):
        k, v = ks[step][...], vs[step][...]
        att, dsc = terms(q0, g0, k, v, valid(0, step))
        out = out + jnp.dot(att, v, preferred_element_type=jnp.float32)
        dq = dq + jnp.dot(dsc, k, preferred_element_type=jnp.float32)
        q, g = qs[step][...], gs[step][...]
        att, dsc = terms(q, g, k0, v0, valid(span + step, 0))
        b, c = back(att, dsc, q, g)
        dk = dk + b
        dv = dv + c
    out_ref[...] = out.astype(out_ref.dtype)
    dq_ref[...] = dq.astype(dq_ref.dtype)
    dk_ref[...] = dk.astype(dk_ref.dtype)
    dv_ref[...] = dv.astype(dv_ref.dtype)


def attention_tiles(qg_list, kv_list, infoc, infor, nheads, alpha, scale):
    rows = qg_list[0].shape[0]
    span = len(qg_list) - 1
    blk = lambda offset: pl.BlockSpec((rows, HD), lambda h: (0, h + offset))
    full = lambda arr: pl.BlockSpec(arr.shape, lambda h: (0, 0))
    operands, specs = [infoc, infor], [full(infoc), full(infor)]
    for group in (qg_list, kv_list):
        for packed in group:
            operands += [packed, packed]
            specs += [blk(0), blk(nheads)]
    shape = jax.ShapeDtypeStruct((rows, nheads * HD), jnp.bfloat16)
    tile = rows * rows * HD * 2
    return pl.pallas_call(
        functools.partial(tiles_kernel, span, alpha, scale),
        grid=(nheads,),
        in_specs=specs,
        out_specs=[blk(0)] * 4,
        out_shape=[shape] * 4,
        cost_estimate=pl.CostEstimate(
            flops=nheads * (2 * span + 1) * 5 * tile,
            transcendentals=nheads * (2 * span + 1) * rows * rows,
            bytes_accessed=(2 * span + 2) * 2 * rows * nheads * HD * 2 * 2 + 4 * rows * nheads * HD * 2,
        ),
    )(*operands)


def scores(query, key, valid, scale, alpha):
    z = jnp.einsum("qhd,khd->hqk", query, key, preferred_element_type=jnp.float32) * alpha
    sig = jax.nn.sigmoid(z)
    weight = valid[None, :, :].astype(jnp.float32) * scale
    return z, sig, weight


def forward_terms(query, grad, key, value, valid, scale, alpha):
    z, sig, weight = scores(query, key, valid, scale, alpha)
    att = (z * sig * weight).astype(jnp.bfloat16)
    out = jnp.einsum("hqk,khd->qhd", att, value, preferred_element_type=jnp.float32)
    dprod = jnp.einsum("qhd,khd->hqk", grad, value, preferred_element_type=jnp.float32)
    dsc = (dprod * sig * (1.0 + z * (1.0 - sig)) * weight * alpha).astype(jnp.bfloat16)
    dquery = jnp.einsum("hqk,khd->qhd", dsc, key, preferred_element_type=jnp.float32)
    return out, dquery, att, dsc


def backward_terms(query, grad, key, value, valid, scale, alpha):
    z, sig, weight = scores(query, key, valid, scale, alpha)
    att = (z * sig * weight).astype(jnp.bfloat16)
    dprod = jnp.einsum("qhd,khd->hqk", grad, value, preferred_element_type=jnp.float32)
    dsc = (dprod * sig * (1.0 + z * (1.0 - sig)) * weight * alpha).astype(jnp.bfloat16)
    dkey = jnp.einsum("hqk,qhd->khd", dsc, query, preferred_element_type=jnp.float32)
    dvalue = jnp.einsum("hqk,qhd->khd", att, grad, preferred_element_type=jnp.float32)
    return dkey, dvalue


def fused_kernel(span, alpha, scale, nheads, groups, spread, infoc, infor, *refs):
    count = span + 1
    qgs = refs[:count]
    kvs = refs[count:2 * count]
    xsel_ref = refs[2 * count]
    out_ref, dv_ref, fin_ref = refs[2 * count + 1:2 * count + 4]
    weights, joined, joined_land, part, sent, landed, sums, mixed, finals, sems = refs[2 * count + 4:]
    me = lax.axis_index("ctx")
    group = lax.axis_index("dp")
    core = me % 2
    slot = me // 2
    partner = me + 1 - 2 * core
    mesh_id = pl.DeviceIdType.MESH
    lanes = 2 * span + 1
    rows = joined.shape[1]
    share = part.shape[2]
    landed[group] = jnp.zeros(landed.shape[1:], landed.dtype)

    def valid(qa, ka):
        qpos = infoc[:, qa:qa + 1]
        quser = infoc[:, lanes + qa:lanes + qa + 1]
        kpos = infor[ka:ka + 1, :]
        kuser = infor[lanes + ka:lanes + ka + 1, :]
        kkept = infor[2 * lanes + ka:2 * lanes + ka + 1, :]
        return (quser == kuser) & (kpos <= qpos) & (kkept > 0)

    pairs = [(0, 0)] + [(0, step) for step in range(1, span + 1)] + [(span + step, 0) for step in range(1, span + 1)]
    for index, (qa, ka) in enumerate(pairs):
        weights[index] = jnp.where(valid(qa, ka), scale, 0.0)

    barrier = pltpu.get_barrier_semaphore()
    for step in range(1, groups):
        peer = 2 * ((slot + step) % groups) + core
        pl.semaphore_signal(barrier, inc=1, device_id=(group, peer), device_id_type=mesh_id)
    for step in range(1, spread):
        pl.semaphore_signal(barrier, inc=1, device_id=((group + step) % spread, me), device_id_type=mesh_id)
    pl.semaphore_signal(barrier, inc=1, device_id=(group, partner), device_id_type=mesh_id)
    pl.semaphore_wait(barrier, groups - 1 + spread - 1 + 1)

    def terms(q, g, k, v, w):
        z = lax.dot_general(q, k, (((1,), (1,)), ((), ())), preferred_element_type=jnp.float32) * alpha
        sig = 1.0 / (1.0 + jnp.exp(-z))
        att = (z * sig * w).astype(jnp.bfloat16)
        dprod = lax.dot_general(g, v, (((1,), (1,)), ((), ())), preferred_element_type=jnp.float32)
        dsc = (dprod * sig * (1.0 + z * (1.0 - sig)) * w * alpha).astype(jnp.bfloat16)
        return att, dsc

    contract = (((0,), (0,)), ((), ()))

    def pair_copy(block):
        return pltpu.make_async_remote_copy(
            src_ref=joined.at[block],
            dst_ref=joined_land.at[block],
            send_sem=sems.at[0, block],
            recv_sem=sems.at[1, block],
            device_id=(group, partner),
            device_id_type=mesh_id,
        )

    def spread_copy(block, source):
        return pltpu.make_async_remote_copy(
            src_ref=sent.at[block],
            dst_ref=landed.at[source],
            send_sem=sems.at[2, block],
            recv_sem=sems.at[3, source],
            device_id=(block, me),
            device_id_type=mesh_id,
        )

    def handle(block):
        pair_copy(block).wait()
        acc = lax.dot_general(xsel_ref[:rows], joined[block], contract, preferred_element_type=jnp.float32)
        acc = acc + lax.dot_general(xsel_ref[rows:], joined_land[block], contract, preferred_element_type=jnp.float32)
        part[block] = acc.reshape(part.shape[1:])
        sent[block] = part[block].astype(sent.dtype)

        @pl.when(group != block)
        def _():
            spread_copy(block, group).start()

    for head in range(nheads):
        cq = slice(head * HD, (head + 1) * HD)
        cg = slice((nheads + head) * HD, (nheads + head + 1) * HD)
        q0, g0 = qgs[0][:, cq], qgs[0][:, cg]
        k0, v0 = kvs[0][:, cq], kvs[0][:, cg]
        att, dsc = terms(q0, g0, k0, v0, weights[0])
        out = jnp.dot(att, v0, preferred_element_type=jnp.float32)
        dq = jnp.dot(dsc, k0, preferred_element_type=jnp.float32)
        dk = lax.dot_general(dsc, q0, contract, preferred_element_type=jnp.float32)
        dv = lax.dot_general(att, g0, contract, preferred_element_type=jnp.float32)
        for step in range(1, span + 1):
            k, v = kvs[step][:, cq], kvs[step][:, cg]
            att, dsc = terms(q0, g0, k, v, weights[step])
            out = out + jnp.dot(att, v, preferred_element_type=jnp.float32)
            dq = dq + jnp.dot(dsc, k, preferred_element_type=jnp.float32)
            q, g = qgs[step][:, cq], qgs[step][:, cg]
            att, dsc = terms(q, g, k0, v0, weights[span + step])
            dk = dk + lax.dot_general(dsc, q, contract, preferred_element_type=jnp.float32)
            dv = dv + lax.dot_general(att, g, contract, preferred_element_type=jnp.float32)
        out_ref[:, cq] = out.astype(out_ref.dtype)
        dv_ref[:, cq] = dv.astype(dv_ref.dtype)
        joined[head] = dq.astype(joined.dtype)
        joined[nheads + head] = dk.astype(joined.dtype)
        pair_copy(head).start()
        pair_copy(nheads + head).start()
        if head > 0:
            handle(head - 1)
            handle(nheads + head - 1)
    handle(nheads - 1)
    handle(2 * nheads - 1)

    for block in range(spread):
        @pl.when(group != block)
        def _():
            spread_copy(block, group).wait_send()
            spread_copy(block, block).wait_recv()

    total = part[group]
    for source in range(spread):
        total = total + landed[source].astype(jnp.float32)
    sums[...] = total.astype(sums.dtype)
    copies = []
    for step in range(1, groups):
        target = (slot + step) % groups
        copy = pltpu.make_async_remote_copy(
            src_ref=sums.at[target],
            dst_ref=mixed.at[slot],
            send_sem=sems.at[4, step - 1],
            recv_sem=sems.at[5, step - 1],
            device_id=(group, 2 * target + core),
            device_id_type=mesh_id,
        )
        copy.start()
        copies.append(copy)
    for copy in copies:
        copy.wait()
    result = part[group, slot]
    for source in range(spread):
        result = result + landed[source, slot].astype(jnp.float32)
    for step in range(1, groups):
        result = result + mixed[(slot + groups - step) % groups].astype(jnp.float32)
    finals[group] = result
    copies = []
    for step in range(1, spread):
        target = (group + step) % spread
        copy = pltpu.make_async_remote_copy(
            src_ref=finals.at[group],
            dst_ref=finals.at[group],
            send_sem=sems.at[6, step - 1],
            recv_sem=sems.at[7, step - 1],
            device_id=(target, me),
            device_id_type=mesh_id,
        )
        copy.start()
        copies.append(copy)
    for copy in copies:
        copy.wait()
    fin_ref[...] = finals[...]


def fused_call(qg_list, kv_list, infoc, infor, xsel, nheads, alpha, scale, spread, share):
    rows, width = qg_list[0].shape
    span = len(qg_list) - 1
    groups = xsel.shape[1] // share
    lanes = HD
    vmem = pl.BlockSpec(memory_space=pltpu.VMEM)
    operands = [infoc, infor] + list(qg_list) + list(kv_list) + [xsel]
    half = jax.ShapeDtypeStruct((rows, nheads * HD), jnp.bfloat16)
    out, dv, finals = pl.pallas_call(
        functools.partial(fused_kernel, span, alpha, scale, nheads, groups, spread),
        in_specs=[vmem] * len(operands),
        out_specs=[vmem] * 3,
        out_shape=[half, half, jax.ShapeDtypeStruct((spread, share, lanes), jnp.float32)],
        scratch_shapes=[
            pltpu.VMEM((2 * span + 1, rows, rows), jnp.float32),
            pltpu.VMEM((2 * nheads, rows, HD), jnp.bfloat16),
            pltpu.VMEM((2 * nheads, rows, HD), jnp.bfloat16),
            pltpu.VMEM((spread, groups, share, lanes), jnp.float32),
            pltpu.VMEM((spread, groups, share, lanes), jnp.bfloat16),
            pltpu.VMEM((spread, groups, share, lanes), jnp.bfloat16),
            pltpu.VMEM((groups, share, lanes), jnp.bfloat16),
            pltpu.VMEM((groups, share, lanes), jnp.bfloat16),
            pltpu.VMEM((spread, share, lanes), jnp.float32),
            pltpu.SemaphoreType.DMA((8, max(groups, spread, 2 * nheads))),
        ],
        compiler_params=pltpu.CompilerParams(collective_id=1, has_side_effects=True),
    )(*operands)
    return out, dv, finals.transpose(1, 0, 2).reshape(share, spread * lanes)


def body(events, w_query, w_key, values, grad_out, lengths, stream_shift, block_keep):
    rows = events.shape[1]
    features = w_query.shape[1]
    nheads = features // HD
    alpha = 1.0 / HD**0.5
    scale = 1.0 / MAXLEN**0.5
    local = events[0]
    queries = jnp.dot(local, w_query, preferred_element_type=jnp.float32).astype(jnp.bfloat16)
    keys = jnp.dot(local, w_key, preferred_element_type=jnp.float32).astype(jnp.bfloat16)
    cycle_size = lax.axis_size("ctx")
    myself = lax.axis_index("ctx")
    total = rows * cycle_size
    ends = jnp.cumsum(lengths[0])
    offset = stream_shift[0]
    keep = block_keep[0]
    blocks_all = jnp.arange(keep.shape[0], dtype=jnp.int32)
    within = jnp.arange(rows, dtype=jnp.int32)

    def describe(anchor):
        anchor = jnp.remainder(anchor, cycle_size)
        position = jnp.remainder(anchor * rows + within - offset, total)
        owner = jnp.sum((position[:, None] >= ends[None, :]).astype(jnp.int32), axis=1)
        which = position // BLOCK
        kept = (
            jnp.sum(jnp.where(which[:, None] == blocks_all[None, :], keep[None, :], 0), axis=1) > 0
        )
        return (position, owner, kept)

    def mask(qinfo, kinfo):
        return (
            (qinfo[1][:, None] == kinfo[1][None, :])
            & (kinfo[0][None, :] <= qinfo[0][:, None])
            & kinfo[2][None, :]
        )

    def split(packed):
        return (
            packed[:, :features].reshape(rows, nheads, HD),
            packed[:, features:].reshape(rows, nheads, HD),
        )

    partner_events = exchange(local, "ctx", 1)
    kv = jnp.concatenate([keys, values[0]], axis=1)
    qg = jnp.concatenate([queries, grad_out[0]], axis=1)
    kv_from, kv_anchor = relayed(kv, myself, 1)
    qg_from, qg_anchor = relayed(qg, myself, -1)

    described = [describe(anchor) for anchor in [myself] + kv_anchor + qg_anchor]
    infor = jnp.stack(
        [d[0] for d in described] + [d[1] for d in described] + [d[2].astype(jnp.int32) for d in described]
    ).astype(jnp.int32)
    infoc = infor.T
    share = local.shape[1] // cycle_size
    both_events = jnp.concatenate([local, partner_events], axis=0)
    halves = both_events.reshape(both_events.shape[0], local.shape[1] // (2 * share), 2, share)
    xsel = lax.dynamic_index_in_dim(halves, myself % 2, 2, keepdims=False).reshape(both_events.shape[0], local.shape[1] // 2)
    out_b, dv_b, mine = fused_call(
        [qg] + qg_from[1:], [kv] + kv_from[1:], infoc, infor, xsel, nheads, alpha, scale, lax.axis_size("dp"), share
    )
    attended = out_b.reshape(1, rows, features)
    grad_values = dv_b.reshape(1, rows, features)
    grad_wq = mine[:, :features].astype(jnp.bfloat16)
    grad_wk = mine[:, features:].astype(jnp.bfloat16)
    return (attended, grad_values, grad_wq, grad_wk)


def solution(mesh):
    placed = (
        P("dp", "ctx", None),
        P(),
        P(),
        P("dp", "ctx", None),
        P("dp", "ctx", None),
        P("dp", None),
        P("dp"),
        P("dp", None),
    )
    return jax.shard_map(
        body,
        mesh=mesh,
        in_specs=placed,
        out_specs=(P("dp", "ctx", None), P("dp", "ctx", None), P("ctx", None), P("ctx", None)),
        check_vma=False,
    )
```

```python
import jax
import jax.numpy as jnp
from jax import lax
from jax.experimental import pallas as pl
from jax.experimental.pallas import tpu as pltpu
from jax.sharding import PartitionSpec as P
import functools

HD = 128
SPAN = 3
BLOCK = 128
MAXLEN = 768


def shifted(value, axis, steps):
    count = lax.axis_size(axis)
    pairs = [(source, (source + steps) % count) for source in range(count)]
    return lax.ppermute(value, axis, pairs)


def exchange(value, axis, mask):
    count = lax.axis_size(axis)
    return lax.ppermute(value, axis, [(source, source ^ mask) for source in range(count)])


def relayed(value, myself, sign):
    count = lax.axis_size("ctx")
    odd = myself % 2
    pairs = []
    for source in range(count):
        step = 3 if (source % 2 == 1) == (sign > 0) else 1
        pairs.append((source, (source + sign * step) % count))
    far = shifted(value, "ctx", 2 * sign)
    mixed = lax.ppermute(value, "ctx", pairs)
    swapped = exchange(far, "ctx", 1)
    lead = odd if sign > 0 else 1 - odd
    mixed_anchor = myself - sign * (3 - 2 * lead)
    swapped_anchor = myself - sign * (1 + 2 * lead)
    return [None, far, mixed, swapped], [myself - 2 * sign, mixed_anchor, swapped_anchor]


def pick(value, bit, axis):
    return (
        lax.dynamic_index_in_dim(value, bit, axis, keepdims=False),
        lax.dynamic_index_in_dim(value, 1 - bit, axis, keepdims=False),
    )


def reduce_kernel(groups, spread, xsel_ref, joined_ref, out_ref, joined_land, part_ref, sent, landed, sums, mixed, finals, sems):
    me = lax.axis_index("ctx")
    group = lax.axis_index("dp")
    core = me % 2
    slot = me // 2
    mesh_id = pl.DeviceIdType.MESH
    barrier = pltpu.get_barrier_semaphore()
    for step in range(1, groups):
        peer = 2 * ((slot + step) % groups) + core
        pl.semaphore_signal(barrier, inc=1, device_id=(group, peer), device_id_type=mesh_id)
    for step in range(1, spread):
        pl.semaphore_signal(barrier, inc=1, device_id=((group + step) % spread, me), device_id_type=mesh_id)
    partner = me + 1 - 2 * core
    pl.semaphore_signal(barrier, inc=1, device_id=(group, partner), device_id_type=mesh_id)
    pl.semaphore_wait(barrier, groups - 1 + spread - 1 + 1)
    pair = pltpu.make_async_remote_copy(
        src_ref=joined_ref,
        dst_ref=joined_land,
        send_sem=sems.at[6, 0],
        recv_sem=sems.at[6, 1],
        device_id=(group, partner),
        device_id_type=mesh_id,
    )
    pair.start()
    rows = joined_ref.shape[0]
    contract = (((0,), (0,)), ((), ()))
    acc = lax.dot_general(xsel_ref[:rows], joined_ref[...], contract, preferred_element_type=jnp.float32)
    pair.wait()
    acc = acc + lax.dot_general(xsel_ref[rows:], joined_land[...], contract, preferred_element_type=jnp.float32)
    _, _, share, lanes = part_ref.shape
    for index in range(spread):
        part_ref[index] = acc[:, index * lanes:(index + 1) * lanes].reshape(groups, share, lanes)
    sent[...] = part_ref[...].astype(sent.dtype)
    copies = []
    for step in range(1, spread):
        target = (group + step) % spread
        copy = pltpu.make_async_remote_copy(
            src_ref=sent.at[target],
            dst_ref=landed.at[group],
            send_sem=sems.at[0, step - 1],
            recv_sem=sems.at[1, step - 1],
            device_id=(target, me),
            device_id_type=mesh_id,
        )
        copy.start()
        copies.append(copy)
    for copy in copies:
        copy.wait()
    total = part_ref[group]
    for step in range(1, spread):
        total = total + landed[(group + spread - step) % spread].astype(jnp.float32)
    sums[...] = total.astype(sums.dtype)
    copies = []
    for step in range(1, groups):
        target = (slot + step) % groups
        copy = pltpu.make_async_remote_copy(
            src_ref=sums.at[target],
            dst_ref=mixed.at[slot],
            send_sem=sems.at[2, step - 1],
            recv_sem=sems.at[3, step - 1],
            device_id=(group, 2 * target + core),
            device_id_type=mesh_id,
        )
        copy.start()
        copies.append(copy)
    for copy in copies:
        copy.wait()
    result = part_ref[group, slot]
    for step in range(1, spread):
        result = result + landed[(group + spread - step) % spread, slot].astype(jnp.float32)
    for step in range(1, groups):
        result = result + mixed[(slot + groups - step) % groups].astype(jnp.float32)
    finals[group] = result
    copies = []
    for step in range(1, spread):
        target = (group + step) % spread
        copy = pltpu.make_async_remote_copy(
            src_ref=finals.at[group],
            dst_ref=finals.at[group],
            send_sem=sems.at[4, step - 1],
            recv_sem=sems.at[5, step - 1],
            device_id=(target, me),
            device_id_type=mesh_id,
        )
        copy.start()
        copies.append(copy)
    for copy in copies:
        copy.wait()
    out_ref[...] = finals[...]


def reduce_blocks(xsel, joined, share, spread):
    rows, width = joined.shape
    groups = xsel.shape[1] // share
    lanes = width // spread
    vmem = pl.BlockSpec(memory_space=pltpu.VMEM)
    finals = pl.pallas_call(
        functools.partial(reduce_kernel, groups, spread),
        in_specs=[vmem, vmem],
        out_specs=vmem,
        out_shape=jax.ShapeDtypeStruct((spread, share, lanes), jnp.float32),
        scratch_shapes=[
            pltpu.VMEM((rows, width), jnp.bfloat16),
            pltpu.VMEM((spread, groups, share, lanes), jnp.float32),
            pltpu.VMEM((spread, groups, share, lanes), jnp.bfloat16),
            pltpu.VMEM((spread, groups, share, lanes), jnp.bfloat16),
            pltpu.VMEM((groups, share, lanes), jnp.bfloat16),
            pltpu.VMEM((groups, share, lanes), jnp.bfloat16),
            pltpu.VMEM((spread, share, lanes), jnp.float32),
            pltpu.SemaphoreType.DMA((7, max(groups, spread))),
        ],
        compiler_params=pltpu.CompilerParams(collective_id=1, has_side_effects=True),
    )(xsel, joined)
    return finals.transpose(1, 0, 2).reshape(share, width)


def reduce_rows(local, partner_events, joined, myself, cycle_size):
    width = local.shape[1]
    share = width // cycle_size
    core = myself % 2
    both_events = jnp.concatenate([local, partner_events], axis=0)
    halves = both_events.reshape(both_events.shape[0], width // (2 * share), 2, share)
    kept = lax.dynamic_index_in_dim(halves, core, 2, keepdims=False).reshape(both_events.shape[0], width // 2)
    acc = reduce_blocks(kept, joined, share, lax.axis_size("dp"))
    return acc


def tiles_kernel(span, alpha, scale, infoc, infor, *refs):
    count = 2 * span + 2
    qs = refs[0:count:2]
    gs = refs[1:count:2]
    ks = refs[count:2 * count:2]
    vs = refs[count + 1:2 * count:2]
    out_ref, dq_ref, dk_ref, dv_ref = refs[2 * count:]
    lanes = 2 * span + 1

    def valid(qa, ka):
        qpos = infoc[:, qa:qa + 1]
        quser = infoc[:, lanes + qa:lanes + qa + 1]
        kpos = infor[ka:ka + 1, :]
        kuser = infor[lanes + ka:lanes + ka + 1, :]
        kkept = infor[2 * lanes + ka:2 * lanes + ka + 1, :]
        return (quser == kuser) & (kpos <= qpos) & (kkept > 0)

    def terms(q, g, k, v, ok):
        z = lax.dot_general(q, k, (((1,), (1,)), ((), ())), preferred_element_type=jnp.float32) * alpha
        sig = 0.5 + 0.5 * jnp.tanh(0.5 * z)
        weight = jnp.where(ok, scale, 0.0)
        att = (z * sig * weight).astype(jnp.bfloat16)
        dprod = lax.dot_general(g, v, (((1,), (1,)), ((), ())), preferred_element_type=jnp.float32)
        dsc = (dprod * sig * (1.0 + z * (1.0 - sig)) * weight * alpha).astype(jnp.bfloat16)
        return att, dsc

    def back(att, dsc, q, g):
        dk = lax.dot_general(dsc, q, (((0,), (0,)), ((), ())), preferred_element_type=jnp.float32)
        dv = lax.dot_general(att, g, (((0,), (0,)), ((), ())), preferred_element_type=jnp.float32)
        return dk, dv

    q0, g0, k0, v0 = qs[0][...], gs[0][...], ks[0][...], vs[0][...]
    att, dsc = terms(q0, g0, k0, v0, valid(0, 0))
    out = jnp.dot(att, v0, preferred_element_type=jnp.float32)
    dq = jnp.dot(dsc, k0, preferred_element_type=jnp.float32)
    dk, dv = back(att, dsc, q0, g0)
    for step in range(1, span + 1):
        k, v = ks[step][...], vs[step][...]
        att, dsc = terms(q0, g0, k, v, valid(0, step))
        out = out + jnp.dot(att, v, preferred_element_type=jnp.float32)
        dq = dq + jnp.dot(dsc, k, preferred_element_type=jnp.float32)
        q, g = qs[step][...], gs[step][...]
        att, dsc = terms(q, g, k0, v0, valid(span + step, 0))
        b, c = back(att, dsc, q, g)
        dk = dk + b
        dv = dv + c
    out_ref[...] = out.astype(out_ref.dtype)
    dq_ref[...] = dq.astype(dq_ref.dtype)
    dk_ref[...] = dk.astype(dk_ref.dtype)
    dv_ref[...] = dv.astype(dv_ref.dtype)


def attention_tiles(qg_list, kv_list, infoc, infor, nheads, alpha, scale):
    rows = qg_list[0].shape[0]
    span = len(qg_list) - 1
    blk = lambda offset: pl.BlockSpec((rows, HD), lambda h: (0, h + offset))
    full = lambda arr: pl.BlockSpec(arr.shape, lambda h: (0, 0))
    operands, specs = [infoc, infor], [full(infoc), full(infor)]
    for group in (qg_list, kv_list):
        for packed in group:
            operands += [packed, packed]
            specs += [blk(0), blk(nheads)]
    shape = jax.ShapeDtypeStruct((rows, nheads * HD), jnp.bfloat16)
    tile = rows * rows * HD * 2
    return pl.pallas_call(
        functools.partial(tiles_kernel, span, alpha, scale),
        grid=(nheads,),
        in_specs=specs,
        out_specs=[blk(0)] * 4,
        out_shape=[shape] * 4,
        cost_estimate=pl.CostEstimate(
            flops=nheads * (2 * span + 1) * 5 * tile,
            transcendentals=nheads * (2 * span + 1) * rows * rows,
            bytes_accessed=(2 * span + 2) * 2 * rows * nheads * HD * 2 * 2 + 4 * rows * nheads * HD * 2,
        ),
    )(*operands)


def scores(query, key, valid, scale, alpha):
    z = jnp.einsum("qhd,khd->hqk", query, key, preferred_element_type=jnp.float32) * alpha
    sig = jax.nn.sigmoid(z)
    weight = valid[None, :, :].astype(jnp.float32) * scale
    return z, sig, weight


def forward_terms(query, grad, key, value, valid, scale, alpha):
    z, sig, weight = scores(query, key, valid, scale, alpha)
    att = (z * sig * weight).astype(jnp.bfloat16)
    out = jnp.einsum("hqk,khd->qhd", att, value, preferred_element_type=jnp.float32)
    dprod = jnp.einsum("qhd,khd->hqk", grad, value, preferred_element_type=jnp.float32)
    dsc = (dprod * sig * (1.0 + z * (1.0 - sig)) * weight * alpha).astype(jnp.bfloat16)
    dquery = jnp.einsum("hqk,khd->qhd", dsc, key, preferred_element_type=jnp.float32)
    return out, dquery, att, dsc


def backward_terms(query, grad, key, value, valid, scale, alpha):
    z, sig, weight = scores(query, key, valid, scale, alpha)
    att = (z * sig * weight).astype(jnp.bfloat16)
    dprod = jnp.einsum("qhd,khd->hqk", grad, value, preferred_element_type=jnp.float32)
    dsc = (dprod * sig * (1.0 + z * (1.0 - sig)) * weight * alpha).astype(jnp.bfloat16)
    dkey = jnp.einsum("hqk,qhd->khd", dsc, query, preferred_element_type=jnp.float32)
    dvalue = jnp.einsum("hqk,qhd->khd", att, grad, preferred_element_type=jnp.float32)
    return dkey, dvalue


def body(events, w_query, w_key, values, grad_out, lengths, stream_shift, block_keep):
    rows = events.shape[1]
    features = w_query.shape[1]
    nheads = features // HD
    alpha = 1.0 / HD**0.5
    scale = 1.0 / MAXLEN**0.5
    local = events[0]
    queries = jnp.dot(local, w_query, preferred_element_type=jnp.float32).astype(jnp.bfloat16)
    keys = jnp.dot(local, w_key, preferred_element_type=jnp.float32).astype(jnp.bfloat16)
    cycle_size = lax.axis_size("ctx")
    myself = lax.axis_index("ctx")
    total = rows * cycle_size
    ends = jnp.cumsum(lengths[0])
    offset = stream_shift[0]
    keep = block_keep[0]
    blocks_all = jnp.arange(keep.shape[0], dtype=jnp.int32)
    within = jnp.arange(rows, dtype=jnp.int32)

    def describe(anchor):
        anchor = jnp.remainder(anchor, cycle_size)
        position = jnp.remainder(anchor * rows + within - offset, total)
        owner = jnp.sum((position[:, None] >= ends[None, :]).astype(jnp.int32), axis=1)
        which = position // BLOCK
        kept = (
            jnp.sum(jnp.where(which[:, None] == blocks_all[None, :], keep[None, :], 0), axis=1) > 0
        )
        return (position, owner, kept)

    def mask(qinfo, kinfo):
        return (
            (qinfo[1][:, None] == kinfo[1][None, :])
            & (kinfo[0][None, :] <= qinfo[0][:, None])
            & kinfo[2][None, :]
        )

    def split(packed):
        return (
            packed[:, :features].reshape(rows, nheads, HD),
            packed[:, features:].reshape(rows, nheads, HD),
        )

    partner_events = exchange(local, "ctx", 1)
    kv = jnp.concatenate([keys, values[0]], axis=1)
    qg = jnp.concatenate([queries, grad_out[0]], axis=1)
    kv_from, kv_anchor = relayed(kv, myself, 1)
    qg_from, qg_anchor = relayed(qg, myself, -1)

    described = [describe(anchor) for anchor in [myself] + kv_anchor + qg_anchor]
    infor = jnp.stack(
        [d[0] for d in described] + [d[1] for d in described] + [d[2].astype(jnp.int32) for d in described]
    ).astype(jnp.int32)
    infoc = infor.T
    out_b, dq_b, dk_b, dv_b = attention_tiles(
        [qg] + qg_from[1:], [kv] + kv_from[1:], infoc, infor, nheads, alpha, scale
    )
    attended = out_b.reshape(1, rows, features)
    grad_values = dv_b.reshape(1, rows, features)
    joined = jnp.concatenate([dq_b, dk_b], axis=1)
    mine = reduce_rows(local, partner_events, joined, myself, cycle_size)
    grad_wq = mine[:, :features].astype(jnp.bfloat16)
    grad_wk = mine[:, features:].astype(jnp.bfloat16)
    return (attended, grad_values, grad_wq, grad_wk)


def solution(mesh):
    placed = (
        P("dp", "ctx", None),
        P(),
        P(),
        P("dp", "ctx", None),
        P("dp", "ctx", None),
        P("dp", None),
        P("dp"),
        P("dp", None),
    )
    return jax.shard_map(
        body,
        mesh=mesh,
        in_specs=placed,
        out_specs=(P("dp", "ctx", None), P("dp", "ctx", None), P("ctx", None), P("ctx", None)),
        check_vma=False,
    )
```

```python
import jax
import jax.numpy as jnp
from jax import lax
from jax.experimental import pallas as pl
from jax.experimental.pallas import tpu as pltpu
from jax.sharding import PartitionSpec as P
import functools

HD = 128
SPAN = 3
BLOCK = 128
MAXLEN = 768


def shifted(value, axis, steps):
    count = lax.axis_size(axis)
    pairs = [(source, (source + steps) % count) for source in range(count)]
    return lax.ppermute(value, axis, pairs)


def exchange(value, axis, mask):
    count = lax.axis_size(axis)
    return lax.ppermute(value, axis, [(source, source ^ mask) for source in range(count)])


def relayed(value, myself, sign):
    count = lax.axis_size("ctx")
    odd = myself % 2
    pairs = []
    for source in range(count):
        step = 3 if (source % 2 == 1) == (sign > 0) else 1
        pairs.append((source, (source + sign * step) % count))
    far = shifted(value, "ctx", 2 * sign)
    mixed = lax.ppermute(value, "ctx", pairs)
    swapped = exchange(far, "ctx", 1)
    lead = odd if sign > 0 else 1 - odd
    mixed_anchor = myself - sign * (3 - 2 * lead)
    swapped_anchor = myself - sign * (1 + 2 * lead)
    return [None, far, mixed, swapped], [myself - 2 * sign, mixed_anchor, swapped_anchor]


def pick(value, bit, axis):
    return (
        lax.dynamic_index_in_dim(value, bit, axis, keepdims=False),
        lax.dynamic_index_in_dim(value, 1 - bit, axis, keepdims=False),
    )


def reduce_kernel(groups, spread, xsel_ref, joined_ref, out_ref, joined_land, part_ref, sent, landed, sums, mixed, finals, sems):
    me = lax.axis_index("ctx")
    group = lax.axis_index("dp")
    core = me % 2
    slot = me // 2
    mesh_id = pl.DeviceIdType.MESH
    barrier = pltpu.get_barrier_semaphore()
    for step in range(1, groups):
        peer = 2 * ((slot + step) % groups) + core
        pl.semaphore_signal(barrier, inc=1, device_id=(group, peer), device_id_type=mesh_id)
    for step in range(1, spread):
        pl.semaphore_signal(barrier, inc=1, device_id=((group + step) % spread, me), device_id_type=mesh_id)
    partner = me + 1 - 2 * core
    pl.semaphore_signal(barrier, inc=1, device_id=(group, partner), device_id_type=mesh_id)
    pl.semaphore_wait(barrier, groups - 1 + spread - 1 + 1)
    pair = pltpu.make_async_remote_copy(
        src_ref=joined_ref,
        dst_ref=joined_land,
        send_sem=sems.at[6, 0],
        recv_sem=sems.at[6, 1],
        device_id=(group, partner),
        device_id_type=mesh_id,
    )
    pair.start()
    rows = joined_ref.shape[0]
    contract = (((0,), (0,)), ((), ()))
    acc = lax.dot_general(xsel_ref[:rows], joined_ref[...], contract, preferred_element_type=jnp.float32)
    pair.wait()
    acc = acc + lax.dot_general(xsel_ref[rows:], joined_land[...], contract, preferred_element_type=jnp.float32)
    _, _, share, lanes = part_ref.shape
    for index in range(spread):
        part_ref[index] = acc[:, index * lanes:(index + 1) * lanes].reshape(groups, share, lanes)
    sent[...] = part_ref[...].astype(sent.dtype)
    copies = []
    for step in range(1, spread):
        target = (group + step) % spread
        copy = pltpu.make_async_remote_copy(
            src_ref=sent.at[target],
            dst_ref=landed.at[group],
            send_sem=sems.at[0, step - 1],
            recv_sem=sems.at[1, step - 1],
            device_id=(target, me),
            device_id_type=mesh_id,
        )
        copy.start()
        copies.append(copy)
    for copy in copies:
        copy.wait()
    total = part_ref[group]
    for step in range(1, spread):
        total = total + landed[(group + spread - step) % spread].astype(jnp.float32)
    sums[...] = total.astype(sums.dtype)
    copies = []
    for step in range(1, groups):
        target = (slot + step) % groups
        copy = pltpu.make_async_remote_copy(
            src_ref=sums.at[target],
            dst_ref=mixed.at[slot],
            send_sem=sems.at[2, step - 1],
            recv_sem=sems.at[3, step - 1],
            device_id=(group, 2 * target + core),
            device_id_type=mesh_id,
        )
        copy.start()
        copies.append(copy)
    for copy in copies:
        copy.wait()
    result = part_ref[group, slot]
    for step in range(1, spread):
        result = result + landed[(group + spread - step) % spread, slot].astype(jnp.float32)
    for step in range(1, groups):
        result = result + mixed[(slot + groups - step) % groups].astype(jnp.float32)
    finals[group] = result
    copies = []
    for step in range(1, spread):
        target = (group + step) % spread
        copy = pltpu.make_async_remote_copy(
            src_ref=finals.at[group],
            dst_ref=finals.at[group],
            send_sem=sems.at[4, step - 1],
            recv_sem=sems.at[5, step - 1],
            device_id=(target, me),
            device_id_type=mesh_id,
        )
        copy.start()
        copies.append(copy)
    for copy in copies:
        copy.wait()
    out_ref[...] = finals[...]


def reduce_blocks(xsel, joined, share, spread):
    rows, width = joined.shape
    groups = xsel.shape[1] // share
    lanes = width // spread
    vmem = pl.BlockSpec(memory_space=pltpu.VMEM)
    finals = pl.pallas_call(
        functools.partial(reduce_kernel, groups, spread),
        in_specs=[vmem, vmem],
        out_specs=vmem,
        out_shape=jax.ShapeDtypeStruct((spread, share, lanes), jnp.float32),
        scratch_shapes=[
            pltpu.VMEM((rows, width), jnp.bfloat16),
            pltpu.VMEM((spread, groups, share, lanes), jnp.float32),
            pltpu.VMEM((spread, groups, share, lanes), jnp.bfloat16),
            pltpu.VMEM((spread, groups, share, lanes), jnp.bfloat16),
            pltpu.VMEM((groups, share, lanes), jnp.bfloat16),
            pltpu.VMEM((groups, share, lanes), jnp.bfloat16),
            pltpu.VMEM((spread, share, lanes), jnp.float32),
            pltpu.SemaphoreType.DMA((7, max(groups, spread))),
        ],
        compiler_params=pltpu.CompilerParams(collective_id=1, has_side_effects=True),
    )(xsel, joined)
    return finals.transpose(1, 0, 2).reshape(share, width)


def reduce_rows(local, partner_events, joined, myself, cycle_size):
    width = local.shape[1]
    share = width // cycle_size
    core = myself % 2
    both_events = jnp.concatenate([local, partner_events], axis=0)
    halves = both_events.reshape(both_events.shape[0], width // (2 * share), 2, share)
    kept = lax.dynamic_index_in_dim(halves, core, 2, keepdims=False).reshape(both_events.shape[0], width // 2)
    acc = reduce_blocks(kept, joined, share, lax.axis_size("dp"))
    return acc


def tiles_kernel(span, steps, diag, alpha, scale, infoc, infor, *refs):
    count = 2 * (len(steps) + 1)
    qs = refs[0:count:2]
    gs = refs[1:count:2]
    ks = refs[count:2 * count:2]
    vs = refs[count + 1:2 * count:2]
    rest = refs[2 * count:]
    partials = None if diag else rest[:4]
    out_ref, dq_ref, dk_ref, dv_ref = rest if diag else rest[4:]
    lanes = 2 * span + 1

    def valid(qa, ka):
        qpos = infoc[:, qa:qa + 1]
        quser = infoc[:, lanes + qa:lanes + qa + 1]
        kpos = infor[ka:ka + 1, :]
        kuser = infor[lanes + ka:lanes + ka + 1, :]
        kkept = infor[2 * lanes + ka:2 * lanes + ka + 1, :]
        return (quser == kuser) & (kpos <= qpos) & (kkept > 0)

    def terms(q, g, k, v, ok):
        z = lax.dot_general(q, k, (((1,), (1,)), ((), ())), preferred_element_type=jnp.float32) * alpha
        sig = 1.0 / (1.0 + jnp.exp(-z))
        weight = jnp.where(ok, scale, 0.0)
        att = (z * sig * weight).astype(jnp.bfloat16)
        dprod = lax.dot_general(g, v, (((1,), (1,)), ((), ())), preferred_element_type=jnp.float32)
        dsc = (dprod * sig * (1.0 + z * (1.0 - sig)) * weight * alpha).astype(jnp.bfloat16)
        return att, dsc

    def back(att, dsc, q, g):
        dk = lax.dot_general(dsc, q, (((0,), (0,)), ((), ())), preferred_element_type=jnp.float32)
        dv = lax.dot_general(att, g, (((0,), (0,)), ((), ())), preferred_element_type=jnp.float32)
        return dk, dv

    q0, g0, k0, v0 = qs[0][...], gs[0][...], ks[0][...], vs[0][...]
    if diag:
        att, dsc = terms(q0, g0, k0, v0, valid(0, 0))
        out = jnp.dot(att, v0, preferred_element_type=jnp.float32)
        dq = jnp.dot(dsc, k0, preferred_element_type=jnp.float32)
        dk, dv = back(att, dsc, q0, g0)
    else:
        out, dq, dk, dv = (ref[...] for ref in partials)
    for index, step in enumerate(steps, 1):
        k, v = ks[index][...], vs[index][...]
        att, dsc = terms(q0, g0, k, v, valid(0, step))
        out = out + jnp.dot(att, v, preferred_element_type=jnp.float32)
        dq = dq + jnp.dot(dsc, k, preferred_element_type=jnp.float32)
        q, g = qs[index][...], gs[index][...]
        att, dsc = terms(q, g, k0, v0, valid(span + step, 0))
        b, c = back(att, dsc, q, g)
        dk = dk + b
        dv = dv + c
    out_ref[...] = out.astype(out_ref.dtype)
    dq_ref[...] = dq.astype(dq_ref.dtype)
    dk_ref[...] = dk.astype(dk_ref.dtype)
    dv_ref[...] = dv.astype(dv_ref.dtype)


def attention_tiles(qg_list, kv_list, infoc, infor, nheads, alpha, scale, steps, partials, out_dtype):
    rows = qg_list[0].shape[0]
    span = len(qg_list) - 1
    diag = partials is None
    blk = lambda offset: pl.BlockSpec((rows, HD), lambda h: (0, h + offset))
    full = lambda arr: pl.BlockSpec(arr.shape, lambda h: (0, 0))
    operands, specs = [infoc, infor], [full(infoc), full(infor)]
    for group in (qg_list, kv_list):
        for packed in [group[0]] + [group[step] for step in steps]:
            operands += [packed, packed]
            specs += [blk(0), blk(nheads)]
    if not diag:
        operands += list(partials)
        specs += [blk(0)] * 4
    shape = jax.ShapeDtypeStruct((rows, nheads * HD), out_dtype)
    tile = rows * rows * HD * 2
    tiles = 2 * len(steps) + (1 if diag else 0)
    return pl.pallas_call(
        functools.partial(tiles_kernel, span, tuple(steps), diag, alpha, scale),
        grid=(nheads,),
        in_specs=specs,
        out_specs=[blk(0)] * 4,
        out_shape=[shape] * 4,
        cost_estimate=pl.CostEstimate(
            flops=nheads * tiles * 5 * tile,
            transcendentals=nheads * tiles * rows * rows,
            bytes_accessed=(len(steps) + 1) * 2 * rows * nheads * HD * 2 * 2 + 8 * rows * nheads * HD * 4,
        ),
    )(*operands)


def scores(query, key, valid, scale, alpha):
    z = jnp.einsum("qhd,khd->hqk", query, key, preferred_element_type=jnp.float32) * alpha
    sig = jax.nn.sigmoid(z)
    weight = valid[None, :, :].astype(jnp.float32) * scale
    return z, sig, weight


def forward_terms(query, grad, key, value, valid, scale, alpha):
    z, sig, weight = scores(query, key, valid, scale, alpha)
    att = (z * sig * weight).astype(jnp.bfloat16)
    out = jnp.einsum("hqk,khd->qhd", att, value, preferred_element_type=jnp.float32)
    dprod = jnp.einsum("qhd,khd->hqk", grad, value, preferred_element_type=jnp.float32)
    dsc = (dprod * sig * (1.0 + z * (1.0 - sig)) * weight * alpha).astype(jnp.bfloat16)
    dquery = jnp.einsum("hqk,khd->qhd", dsc, key, preferred_element_type=jnp.float32)
    return out, dquery, att, dsc


def backward_terms(query, grad, key, value, valid, scale, alpha):
    z, sig, weight = scores(query, key, valid, scale, alpha)
    att = (z * sig * weight).astype(jnp.bfloat16)
    dprod = jnp.einsum("qhd,khd->hqk", grad, value, preferred_element_type=jnp.float32)
    dsc = (dprod * sig * (1.0 + z * (1.0 - sig)) * weight * alpha).astype(jnp.bfloat16)
    dkey = jnp.einsum("hqk,qhd->khd", dsc, query, preferred_element_type=jnp.float32)
    dvalue = jnp.einsum("hqk,qhd->khd", att, grad, preferred_element_type=jnp.float32)
    return dkey, dvalue


def body(events, w_query, w_key, values, grad_out, lengths, stream_shift, block_keep):
    rows = events.shape[1]
    features = w_query.shape[1]
    nheads = features // HD
    alpha = 1.0 / HD**0.5
    scale = 1.0 / MAXLEN**0.5
    local = events[0]
    queries = jnp.dot(local, w_query, preferred_element_type=jnp.float32).astype(jnp.bfloat16)
    keys = jnp.dot(local, w_key, preferred_element_type=jnp.float32).astype(jnp.bfloat16)
    cycle_size = lax.axis_size("ctx")
    myself = lax.axis_index("ctx")
    total = rows * cycle_size
    ends = jnp.cumsum(lengths[0])
    offset = stream_shift[0]
    keep = block_keep[0]
    blocks_all = jnp.arange(keep.shape[0], dtype=jnp.int32)
    within = jnp.arange(rows, dtype=jnp.int32)

    def describe(anchor):
        anchor = jnp.remainder(anchor, cycle_size)
        position = jnp.remainder(anchor * rows + within - offset, total)
        owner = jnp.sum((position[:, None] >= ends[None, :]).astype(jnp.int32), axis=1)
        which = position // BLOCK
        kept = (
            jnp.sum(jnp.where(which[:, None] == blocks_all[None, :], keep[None, :], 0), axis=1) > 0
        )
        return (position, owner, kept)

    def mask(qinfo, kinfo):
        return (
            (qinfo[1][:, None] == kinfo[1][None, :])
            & (kinfo[0][None, :] <= qinfo[0][:, None])
            & kinfo[2][None, :]
        )

    def split(packed):
        return (
            packed[:, :features].reshape(rows, nheads, HD),
            packed[:, features:].reshape(rows, nheads, HD),
        )

    partner_events = exchange(local, "ctx", 1)
    kv = jnp.concatenate([keys, values[0]], axis=1)
    qg = jnp.concatenate([queries, grad_out[0]], axis=1)
    kv_from, kv_anchor = relayed(kv, myself, 1)
    qg_from, qg_anchor = relayed(qg, myself, -1)

    described = [describe(anchor) for anchor in [myself] + kv_anchor + qg_anchor]
    infor = jnp.stack(
        [d[0] for d in described] + [d[1] for d in described] + [d[2].astype(jnp.int32) for d in described]
    ).astype(jnp.int32)
    infoc = infor.T
    qg_list, kv_list = [qg] + qg_from[1:], [kv] + kv_from[1:]
    partials = attention_tiles(
        qg_list, kv_list, infoc, infor, nheads, alpha, scale, (1, 2), None, jnp.float32
    )
    out_b, dq_b, dk_b, dv_b = attention_tiles(
        qg_list, kv_list, infoc, infor, nheads, alpha, scale, (3,), partials, jnp.bfloat16
    )
    attended = out_b.reshape(1, rows, features)
    grad_values = dv_b.reshape(1, rows, features)
    joined = jnp.concatenate([dq_b, dk_b], axis=1)
    mine = reduce_rows(local, partner_events, joined, myself, cycle_size)
    grad_wq = mine[:, :features].astype(jnp.bfloat16)
    grad_wk = mine[:, features:].astype(jnp.bfloat16)
    return (attended, grad_values, grad_wq, grad_wk)


def solution(mesh):
    placed = (
        P("dp", "ctx", None),
        P(),
        P(),
        P("dp", "ctx", None),
        P("dp", "ctx", None),
        P("dp", None),
        P("dp"),
        P("dp", None),
    )
    return jax.shard_map(
        body,
        mesh=mesh,
        in_specs=placed,
        out_specs=(P("dp", "ctx", None), P("dp", "ctx", None), P("ctx", None), P("ctx", None)),
        check_vma=False,
    )
```

```python
import jax
import jax.numpy as jnp
from jax import lax
from jax.experimental import pallas as pl
from jax.experimental.pallas import tpu as pltpu
from jax.sharding import PartitionSpec as P
import functools

HD = 128
SPAN = 3
BLOCK = 128
MAXLEN = 768


def shifted(value, axis, steps):
    count = lax.axis_size(axis)
    pairs = [(source, (source + steps) % count) for source in range(count)]
    return lax.ppermute(value, axis, pairs)


def exchange(value, axis, mask):
    count = lax.axis_size(axis)
    return lax.ppermute(value, axis, [(source, source ^ mask) for source in range(count)])


def relayed(value, myself, sign):
    count = lax.axis_size("ctx")
    odd = myself % 2
    pairs = []
    for source in range(count):
        step = 3 if (source % 2 == 1) == (sign > 0) else 1
        pairs.append((source, (source + sign * step) % count))
    far = shifted(value, "ctx", 2 * sign)
    mixed = lax.ppermute(value, "ctx", pairs)
    swapped = exchange(far, "ctx", 1)
    lead = odd if sign > 0 else 1 - odd
    mixed_anchor = myself - sign * (3 - 2 * lead)
    swapped_anchor = myself - sign * (1 + 2 * lead)
    return [None, far, mixed, swapped], [myself - 2 * sign, mixed_anchor, swapped_anchor]


def pick(value, bit, axis):
    return (
        lax.dynamic_index_in_dim(value, bit, axis, keepdims=False),
        lax.dynamic_index_in_dim(value, 1 - bit, axis, keepdims=False),
    )


def reduce_kernel(groups, spread, own_ref, other_ref, joined_ref, out_ref, joined_land, part_ref, sent, landed, sums, mixed, finals, sems):
    me = lax.axis_index("ctx")
    group = lax.axis_index("dp")
    core = me % 2
    slot = me // 2
    mesh_id = pl.DeviceIdType.MESH
    barrier = pltpu.get_barrier_semaphore()
    for step in range(1, groups):
        peer = 2 * ((slot + step) % groups) + core
        pl.semaphore_signal(barrier, inc=1, device_id=(group, peer), device_id_type=mesh_id)
    for step in range(1, spread):
        pl.semaphore_signal(barrier, inc=1, device_id=((group + step) % spread, me), device_id_type=mesh_id)
    partner = me + 1 - 2 * core
    pl.semaphore_signal(barrier, inc=1, device_id=(group, partner), device_id_type=mesh_id)
    pl.semaphore_wait(barrier, groups - 1 + spread - 1 + 1)
    pair = pltpu.make_async_remote_copy(
        src_ref=joined_ref,
        dst_ref=joined_land,
        send_sem=sems.at[6, 0],
        recv_sem=sems.at[6, 1],
        device_id=(group, partner),
        device_id_type=mesh_id,
    )
    pair.start()
    rows = joined_ref.shape[0]
    contract = (((0,), (0,)), ((), ()))
    acc = lax.dot_general(own_ref[...], joined_ref[...], contract, preferred_element_type=jnp.float32)
    pair.wait()
    acc = acc + lax.dot_general(other_ref[...], joined_land[...], contract, preferred_element_type=jnp.float32)
    _, _, share, lanes = part_ref.shape
    for index in range(spread):
        part_ref[index] = acc[:, index * lanes:(index + 1) * lanes].reshape(groups, share, lanes)
    sent[...] = part_ref[...].astype(sent.dtype)
    copies = []
    for step in range(1, spread):
        target = (group + step) % spread
        copy = pltpu.make_async_remote_copy(
            src_ref=sent.at[target],
            dst_ref=landed.at[group],
            send_sem=sems.at[0, step - 1],
            recv_sem=sems.at[1, step - 1],
            device_id=(target, me),
            device_id_type=mesh_id,
        )
        copy.start()
        copies.append(copy)
    for copy in copies:
        copy.wait()
    total = part_ref[group]
    for step in range(1, spread):
        total = total + landed[(group + spread - step) % spread].astype(jnp.float32)
    sums[...] = total.astype(sums.dtype)
    copies = []
    for step in range(1, groups):
        target = (slot + step) % groups
        copy = pltpu.make_async_remote_copy(
            src_ref=sums.at[target],
            dst_ref=mixed.at[slot],
            send_sem=sems.at[2, step - 1],
            recv_sem=sems.at[3, step - 1],
            device_id=(group, 2 * target + core),
            device_id_type=mesh_id,
        )
        copy.start()
        copies.append(copy)
    for copy in copies:
        copy.wait()
    result = part_ref[group, slot]
    for step in range(1, spread):
        result = result + landed[(group + spread - step) % spread, slot].astype(jnp.float32)
    for step in range(1, groups):
        result = result + mixed[(slot + groups - step) % groups].astype(jnp.float32)
    finals[group] = result
    copies = []
    for step in range(1, spread):
        target = (group + step) % spread
        copy = pltpu.make_async_remote_copy(
            src_ref=finals.at[group],
            dst_ref=finals.at[group],
            send_sem=sems.at[4, step - 1],
            recv_sem=sems.at[5, step - 1],
            device_id=(target, me),
            device_id_type=mesh_id,
        )
        copy.start()
        copies.append(copy)
    for copy in copies:
        copy.wait()
    out_ref[...] = finals[...]


def reduce_blocks(own, other, joined, share, spread):
    rows, width = joined.shape
    groups = own.shape[1] // share
    lanes = width // spread
    vmem = pl.BlockSpec(memory_space=pltpu.VMEM)
    finals = pl.pallas_call(
        functools.partial(reduce_kernel, groups, spread),
        in_specs=[vmem, vmem, vmem],
        out_specs=vmem,
        out_shape=jax.ShapeDtypeStruct((spread, share, lanes), jnp.float32),
        scratch_shapes=[
            pltpu.VMEM((rows, width), jnp.bfloat16),
            pltpu.VMEM((spread, groups, share, lanes), jnp.float32),
            pltpu.VMEM((spread, groups, share, lanes), jnp.bfloat16),
            pltpu.VMEM((spread, groups, share, lanes), jnp.bfloat16),
            pltpu.VMEM((groups, share, lanes), jnp.bfloat16),
            pltpu.VMEM((groups, share, lanes), jnp.bfloat16),
            pltpu.VMEM((spread, share, lanes), jnp.float32),
            pltpu.SemaphoreType.DMA((7, max(groups, spread))),
        ],
        compiler_params=pltpu.CompilerParams(collective_id=1, has_side_effects=True),
    )(own, other, joined)
    return finals.transpose(1, 0, 2).reshape(share, width)


def select_features(events, share, bit):
    width = events.shape[1]
    halves = events.reshape(events.shape[0], width // (2 * share), 2, share)
    return lax.dynamic_index_in_dim(halves, bit, 2, keepdims=False).reshape(events.shape[0], width // 2)


def reduce_rows(own, other, joined, share):
    acc = reduce_blocks(own, other, joined, share, lax.axis_size("dp"))
    return acc


def tiles_kernel(span, alpha, scale, infoc, infor, *refs):
    count = 2 * span + 2
    qs = refs[0:count:2]
    gs = refs[1:count:2]
    ks = refs[count:2 * count:2]
    vs = refs[count + 1:2 * count:2]
    out_ref, dq_ref, dk_ref, dv_ref = refs[2 * count:]
    lanes = 2 * span + 1

    def valid(qa, ka):
        qpos = infoc[:, qa:qa + 1]
        quser = infoc[:, lanes + qa:lanes + qa + 1]
        kpos = infor[ka:ka + 1, :]
        kuser = infor[lanes + ka:lanes + ka + 1, :]
        kkept = infor[2 * lanes + ka:2 * lanes + ka + 1, :]
        return (quser == kuser) & (kpos <= qpos) & (kkept > 0)

    def terms(q, g, k, v, ok):
        z = lax.dot_general(q, k, (((1,), (1,)), ((), ())), preferred_element_type=jnp.float32) * alpha
        sig = 1.0 / (1.0 + jnp.exp(-z))
        weight = jnp.where(ok, scale, 0.0)
        att = (z * sig * weight).astype(jnp.bfloat16)
        dprod = lax.dot_general(g, v, (((1,), (1,)), ((), ())), preferred_element_type=jnp.float32)
        dsc = (dprod * sig * (1.0 + z * (1.0 - sig)) * weight * alpha).astype(jnp.bfloat16)
        return att, dsc

    def back(att, dsc, q, g):
        dk = lax.dot_general(dsc, q, (((0,), (0,)), ((), ())), preferred_element_type=jnp.float32)
        dv = lax.dot_general(att, g, (((0,), (0,)), ((), ())), preferred_element_type=jnp.float32)
        return dk, dv

    q0, g0, k0, v0 = qs[0][...], gs[0][...], ks[0][...], vs[0][...]
    att, dsc = terms(q0, g0, k0, v0, valid(0, 0))
    out = jnp.dot(att, v0, preferred_element_type=jnp.float32)
    dq = jnp.dot(dsc, k0, preferred_element_type=jnp.float32)
    dk, dv = back(att, dsc, q0, g0)
    for step in range(1, span + 1):
        k, v = ks[step][...], vs[step][...]
        att, dsc = terms(q0, g0, k, v, valid(0, step))
        out = out + jnp.dot(att, v, preferred_element_type=jnp.float32)
        dq = dq + jnp.dot(dsc, k, preferred_element_type=jnp.float32)
        q, g = qs[step][...], gs[step][...]
        att, dsc = terms(q, g, k0, v0, valid(span + step, 0))
        b, c = back(att, dsc, q, g)
        dk = dk + b
        dv = dv + c
    out_ref[...] = out.astype(out_ref.dtype)
    dq_ref[...] = dq.astype(dq_ref.dtype)
    dk_ref[...] = dk.astype(dk_ref.dtype)
    dv_ref[...] = dv.astype(dv_ref.dtype)


def attention_tiles(qg_list, kv_list, infoc, infor, nheads, alpha, scale):
    rows = qg_list[0].shape[0]
    span = len(qg_list) - 1
    blk = lambda offset: pl.BlockSpec((rows, HD), lambda h: (0, h + offset))
    full = lambda arr: pl.BlockSpec(arr.shape, lambda h: (0, 0))
    operands, specs = [infoc, infor], [full(infoc), full(infor)]
    for group in (qg_list, kv_list):
        for packed in group:
            operands += [packed, packed]
            specs += [blk(0), blk(nheads)]
    shape = jax.ShapeDtypeStruct((rows, nheads * HD), jnp.bfloat16)
    tile = rows * rows * HD * 2
    return pl.pallas_call(
        functools.partial(tiles_kernel, span, alpha, scale),
        grid=(nheads,),
        in_specs=specs,
        out_specs=[blk(0)] * 4,
        out_shape=[shape] * 4,
        cost_estimate=pl.CostEstimate(
            flops=nheads * (2 * span + 1) * 5 * tile,
            transcendentals=nheads * (2 * span + 1) * rows * rows,
            bytes_accessed=(2 * span + 2) * 2 * rows * nheads * HD * 2 * 2 + 4 * rows * nheads * HD * 2,
        ),
    )(*operands)


def scores(query, key, valid, scale, alpha):
    z = jnp.einsum("qhd,khd->hqk", query, key, preferred_element_type=jnp.float32) * alpha
    sig = jax.nn.sigmoid(z)
    weight = valid[None, :, :].astype(jnp.float32) * scale
    return z, sig, weight


def forward_terms(query, grad, key, value, valid, scale, alpha):
    z, sig, weight = scores(query, key, valid, scale, alpha)
    att = (z * sig * weight).astype(jnp.bfloat16)
    out = jnp.einsum("hqk,khd->qhd", att, value, preferred_element_type=jnp.float32)
    dprod = jnp.einsum("qhd,khd->hqk", grad, value, preferred_element_type=jnp.float32)
    dsc = (dprod * sig * (1.0 + z * (1.0 - sig)) * weight * alpha).astype(jnp.bfloat16)
    dquery = jnp.einsum("hqk,khd->qhd", dsc, key, preferred_element_type=jnp.float32)
    return out, dquery, att, dsc


def backward_terms(query, grad, key, value, valid, scale, alpha):
    z, sig, weight = scores(query, key, valid, scale, alpha)
    att = (z * sig * weight).astype(jnp.bfloat16)
    dprod = jnp.einsum("qhd,khd->hqk", grad, value, preferred_element_type=jnp.float32)
    dsc = (dprod * sig * (1.0 + z * (1.0 - sig)) * weight * alpha).astype(jnp.bfloat16)
    dkey = jnp.einsum("hqk,qhd->khd", dsc, query, preferred_element_type=jnp.float32)
    dvalue = jnp.einsum("hqk,qhd->khd", att, grad, preferred_element_type=jnp.float32)
    return dkey, dvalue


def body(events, w_query, w_key, values, grad_out, lengths, stream_shift, block_keep):
    rows = events.shape[1]
    features = w_query.shape[1]
    nheads = features // HD
    alpha = 1.0 / HD**0.5
    scale = 1.0 / MAXLEN**0.5
    local = events[0]
    queries = jnp.dot(local, w_query, preferred_element_type=jnp.float32).astype(jnp.bfloat16)
    keys = jnp.dot(local, w_key, preferred_element_type=jnp.float32).astype(jnp.bfloat16)
    cycle_size = lax.axis_size("ctx")
    myself = lax.axis_index("ctx")
    total = rows * cycle_size
    ends = jnp.cumsum(lengths[0])
    offset = stream_shift[0]
    keep = block_keep[0]
    blocks_all = jnp.arange(keep.shape[0], dtype=jnp.int32)
    within = jnp.arange(rows, dtype=jnp.int32)

    def describe(anchor):
        anchor = jnp.remainder(anchor, cycle_size)
        position = jnp.remainder(anchor * rows + within - offset, total)
        owner = jnp.sum((position[:, None] >= ends[None, :]).astype(jnp.int32), axis=1)
        which = position // BLOCK
        kept = (
            jnp.sum(jnp.where(which[:, None] == blocks_all[None, :], keep[None, :], 0), axis=1) > 0
        )
        return (position, owner, kept)

    def mask(qinfo, kinfo):
        return (
            (qinfo[1][:, None] == kinfo[1][None, :])
            & (kinfo[0][None, :] <= qinfo[0][:, None])
            & kinfo[2][None, :]
        )

    def split(packed):
        return (
            packed[:, :features].reshape(rows, nheads, HD),
            packed[:, features:].reshape(rows, nheads, HD),
        )

    share = local.shape[1] // cycle_size
    own_events = select_features(local, share, myself % 2)
    other_events = exchange(select_features(local, share, 1 - myself % 2), "ctx", 1)
    kv = jnp.concatenate([keys, values[0]], axis=1)
    qg = jnp.concatenate([queries, grad_out[0]], axis=1)
    kv_from, kv_anchor = relayed(kv, myself, 1)
    qg_from, qg_anchor = relayed(qg, myself, -1)

    described = [describe(anchor) for anchor in [myself] + kv_anchor + qg_anchor]
    infor = jnp.stack(
        [d[0] for d in described] + [d[1] for d in described] + [d[2].astype(jnp.int32) for d in described]
    ).astype(jnp.int32)
    infoc = infor.T
    out_b, dq_b, dk_b, dv_b = attention_tiles(
        [qg] + qg_from[1:], [kv] + kv_from[1:], infoc, infor, nheads, alpha, scale
    )
    attended = out_b.reshape(1, rows, features)
    grad_values = dv_b.reshape(1, rows, features)
    joined = jnp.concatenate([dq_b, dk_b], axis=1)
    mine = reduce_rows(own_events, other_events, joined, share)
    grad_wq = mine[:, :features].astype(jnp.bfloat16)
    grad_wk = mine[:, features:].astype(jnp.bfloat16)
    return (attended, grad_values, grad_wq, grad_wk)


def solution(mesh):
    placed = (
        P("dp", "ctx", None),
        P(),
        P(),
        P("dp", "ctx", None),
        P("dp", "ctx", None),
        P("dp", None),
        P("dp"),
        P("dp", None),
    )
    return jax.shard_map(
        body,
        mesh=mesh,
        in_specs=placed,
        out_specs=(P("dp", "ctx", None), P("dp", "ctx", None), P("ctx", None), P("ctx", None)),
        check_vma=False,
    )
```

```python
import jax
import jax.numpy as jnp
from jax import lax
from jax.experimental import pallas as pl
from jax.experimental.pallas import tpu as pltpu
from jax.sharding import PartitionSpec as P
import functools

HD = 128
SPAN = 3
BLOCK = 128
MAXLEN = 768


def shifted(value, axis, steps):
    count = lax.axis_size(axis)
    pairs = [(source, (source + steps) % count) for source in range(count)]
    return lax.ppermute(value, axis, pairs)


def exchange(value, axis, mask):
    count = lax.axis_size(axis)
    return lax.ppermute(value, axis, [(source, source ^ mask) for source in range(count)])


def relayed(value, myself, sign):
    count = lax.axis_size("ctx")
    odd = myself % 2
    pairs = []
    for source in range(count):
        step = 3 if (source % 2 == 1) == (sign > 0) else 1
        pairs.append((source, (source + sign * step) % count))
    far = shifted(value, "ctx", 2 * sign)
    mixed = lax.ppermute(value, "ctx", pairs)
    swapped = exchange(far, "ctx", 1)
    lead = odd if sign > 0 else 1 - odd
    mixed_anchor = myself - sign * (3 - 2 * lead)
    swapped_anchor = myself - sign * (1 + 2 * lead)
    return [None, far, mixed, swapped], [myself - 2 * sign, mixed_anchor, swapped_anchor]


def pick(value, bit, axis):
    return (
        lax.dynamic_index_in_dim(value, bit, axis, keepdims=False),
        lax.dynamic_index_in_dim(value, 1 - bit, axis, keepdims=False),
    )


def reduce_kernel(groups, spread, own_ref, other_ref, joined_ref, out_ref, joined_land, part_ref, sent, landed, sums, mixed, finals, sems):
    me = lax.axis_index("ctx")
    group = lax.axis_index("dp")
    core = me % 2
    slot = me // 2
    mesh_id = pl.DeviceIdType.MESH
    barrier = pltpu.get_barrier_semaphore()
    for step in range(1, groups):
        peer = 2 * ((slot + step) % groups) + core
        pl.semaphore_signal(barrier, inc=1, device_id=(group, peer), device_id_type=mesh_id)
    for step in range(1, spread):
        pl.semaphore_signal(barrier, inc=1, device_id=((group + step) % spread, me), device_id_type=mesh_id)
    partner = me + 1 - 2 * core
    pl.semaphore_signal(barrier, inc=1, device_id=(group, partner), device_id_type=mesh_id)
    pl.semaphore_wait(barrier, groups - 1 + spread - 1 + 1)
    pair = pltpu.make_async_remote_copy(
        src_ref=joined_ref,
        dst_ref=joined_land,
        send_sem=sems.at[6, 0],
        recv_sem=sems.at[6, 1],
        device_id=(group, partner),
        device_id_type=mesh_id,
    )
    pair.start()
    contract = (((0,), (0,)), ((), ()))
    accs = [
        lax.dot_general(own_ref[...], joined_ref[half], contract, preferred_element_type=jnp.float32)
        for half in range(2)
    ]
    pair.wait()
    accs = [
        accs[half] + lax.dot_general(other_ref[...], joined_land[half], contract, preferred_element_type=jnp.float32)
        for half in range(2)
    ]
    _, _, share, lanes = part_ref.shape
    features = joined_ref.shape[2]
    for index in range(spread):
        half, column = divmod(index * lanes, features)
        part_ref[index] = accs[half][:, column:column + lanes].reshape(groups, share, lanes)
    sent[...] = part_ref[...].astype(sent.dtype)
    copies = []
    for step in range(1, spread):
        target = (group + step) % spread
        copy = pltpu.make_async_remote_copy(
            src_ref=sent.at[target],
            dst_ref=landed.at[group],
            send_sem=sems.at[0, step - 1],
            recv_sem=sems.at[1, step - 1],
            device_id=(target, me),
            device_id_type=mesh_id,
        )
        copy.start()
        copies.append(copy)
    for copy in copies:
        copy.wait()
    total = part_ref[group]
    for step in range(1, spread):
        total = total + landed[(group + spread - step) % spread].astype(jnp.float32)
    sums[...] = total.astype(sums.dtype)
    copies = []
    for step in range(1, groups):
        target = (slot + step) % groups
        copy = pltpu.make_async_remote_copy(
            src_ref=sums.at[target],
            dst_ref=mixed.at[slot],
            send_sem=sems.at[2, step - 1],
            recv_sem=sems.at[3, step - 1],
            device_id=(group, 2 * target + core),
            device_id_type=mesh_id,
        )
        copy.start()
        copies.append(copy)
    for copy in copies:
        copy.wait()
    result = part_ref[group, slot]
    for step in range(1, spread):
        result = result + landed[(group + spread - step) % spread, slot].astype(jnp.float32)
    for step in range(1, groups):
        result = result + mixed[(slot + groups - step) % groups].astype(jnp.float32)
    finals[group] = result
    copies = []
    for step in range(1, spread):
        target = (group + step) % spread
        copy = pltpu.make_async_remote_copy(
            src_ref=finals.at[group],
            dst_ref=finals.at[group],
            send_sem=sems.at[4, step - 1],
            recv_sem=sems.at[5, step - 1],
            device_id=(target, me),
            device_id_type=mesh_id,
        )
        copy.start()
        copies.append(copy)
    for copy in copies:
        copy.wait()
    out_ref[...] = finals[...]


def reduce_blocks(own, other, joined, share, spread):
    _, rows, features = joined.shape
    width = 2 * features
    groups = own.shape[1] // share
    lanes = width // spread
    vmem = pl.BlockSpec(memory_space=pltpu.VMEM)
    finals = pl.pallas_call(
        functools.partial(reduce_kernel, groups, spread),
        in_specs=[vmem, vmem, vmem],
        out_specs=vmem,
        out_shape=jax.ShapeDtypeStruct((spread, share, lanes), jnp.float32),
        scratch_shapes=[
            pltpu.VMEM((2, rows, features), jnp.bfloat16),
            pltpu.VMEM((spread, groups, share, lanes), jnp.float32),
            pltpu.VMEM((spread, groups, share, lanes), jnp.bfloat16),
            pltpu.VMEM((spread, groups, share, lanes), jnp.bfloat16),
            pltpu.VMEM((groups, share, lanes), jnp.bfloat16),
            pltpu.VMEM((groups, share, lanes), jnp.bfloat16),
            pltpu.VMEM((spread, share, lanes), jnp.float32),
            pltpu.SemaphoreType.DMA((7, max(groups, spread))),
        ],
        compiler_params=pltpu.CompilerParams(collective_id=1, has_side_effects=True),
    )(own, other, joined)
    return finals.transpose(1, 0, 2).reshape(share, width)


def select_features(events, share, bit):
    width = events.shape[1]
    halves = events.reshape(events.shape[0], width // (2 * share), 2, share)
    return lax.dynamic_index_in_dim(halves, bit, 2, keepdims=False).reshape(events.shape[0], width // 2)


def reduce_rows(own, other, joined, share):
    acc = reduce_blocks(own, other, joined, share, lax.axis_size("dp"))
    return acc


def tiles_kernel(span, alpha, scale, infoc, infor, *refs):
    count = 2 * span + 2
    qs = refs[0:count:2]
    gs = refs[1:count:2]
    ks = refs[count:2 * count:2]
    vs = refs[count + 1:2 * count:2]
    out_ref, dqk_ref, dv_ref = refs[2 * count:]
    lanes = 2 * span + 1

    def valid(qa, ka):
        qpos = infoc[:, qa:qa + 1]
        quser = infoc[:, lanes + qa:lanes + qa + 1]
        kpos = infor[ka:ka + 1, :]
        kuser = infor[lanes + ka:lanes + ka + 1, :]
        kkept = infor[2 * lanes + ka:2 * lanes + ka + 1, :]
        return (quser == kuser) & (kpos <= qpos) & (kkept > 0)

    def terms(q, g, k, v, ok):
        z = lax.dot_general(q, k, (((1,), (1,)), ((), ())), preferred_element_type=jnp.float32) * alpha
        sig = 1.0 / (1.0 + jnp.exp(-z))
        weight = jnp.where(ok, scale, 0.0)
        att = (z * sig * weight).astype(jnp.bfloat16)
        dprod = lax.dot_general(g, v, (((1,), (1,)), ((), ())), preferred_element_type=jnp.float32)
        dsc = (dprod * sig * (1.0 + z * (1.0 - sig)) * weight * alpha).astype(jnp.bfloat16)
        return att, dsc

    def back(att, dsc, q, g):
        dk = lax.dot_general(dsc, q, (((0,), (0,)), ((), ())), preferred_element_type=jnp.float32)
        dv = lax.dot_general(att, g, (((0,), (0,)), ((), ())), preferred_element_type=jnp.float32)
        return dk, dv

    q0, g0, k0, v0 = qs[0][...], gs[0][...], ks[0][...], vs[0][...]
    att, dsc = terms(q0, g0, k0, v0, valid(0, 0))
    out = jnp.dot(att, v0, preferred_element_type=jnp.float32)
    dq = jnp.dot(dsc, k0, preferred_element_type=jnp.float32)
    dk, dv = back(att, dsc, q0, g0)
    for step in range(1, span + 1):
        k, v = ks[step][...], vs[step][...]
        att, dsc = terms(q0, g0, k, v, valid(0, step))
        out = out + jnp.dot(att, v, preferred_element_type=jnp.float32)
        dq = dq + jnp.dot(dsc, k, preferred_element_type=jnp.float32)
        q, g = qs[step][...], gs[step][...]
        att, dsc = terms(q, g, k0, v0, valid(span + step, 0))
        b, c = back(att, dsc, q, g)
        dk = dk + b
        dv = dv + c
    out_ref[...] = out.astype(out_ref.dtype)
    dqk_ref[0] = dq.astype(dqk_ref.dtype)
    dqk_ref[1] = dk.astype(dqk_ref.dtype)
    dv_ref[...] = dv.astype(dv_ref.dtype)


def attention_tiles(qg_list, kv_list, infoc, infor, nheads, alpha, scale):
    rows = qg_list[0].shape[0]
    span = len(qg_list) - 1
    blk = lambda offset: pl.BlockSpec((rows, HD), lambda h: (0, h + offset))
    full = lambda arr: pl.BlockSpec(arr.shape, lambda h: (0, 0))
    operands, specs = [infoc, infor], [full(infoc), full(infor)]
    for group in (qg_list, kv_list):
        for packed in group:
            operands += [packed, packed]
            specs += [blk(0), blk(nheads)]
    shape = jax.ShapeDtypeStruct((rows, nheads * HD), jnp.bfloat16)
    tile = rows * rows * HD * 2
    return pl.pallas_call(
        functools.partial(tiles_kernel, span, alpha, scale),
        grid=(nheads,),
        in_specs=specs,
        out_specs=[blk(0), pl.BlockSpec((2, rows, HD), lambda h: (0, 0, h)), blk(0)],
        out_shape=[shape, jax.ShapeDtypeStruct((2, rows, nheads * HD), jnp.bfloat16), shape],
        cost_estimate=pl.CostEstimate(
            flops=nheads * (2 * span + 1) * 5 * tile,
            transcendentals=nheads * (2 * span + 1) * rows * rows,
            bytes_accessed=(2 * span + 2) * 2 * rows * nheads * HD * 2 * 2 + 4 * rows * nheads * HD * 2,
        ),
    )(*operands)


def scores(query, key, valid, scale, alpha):
    z = jnp.einsum("qhd,khd->hqk", query, key, preferred_element_type=jnp.float32) * alpha
    sig = jax.nn.sigmoid(z)
    weight = valid[None, :, :].astype(jnp.float32) * scale
    return z, sig, weight


def forward_terms(query, grad, key, value, valid, scale, alpha):
    z, sig, weight = scores(query, key, valid, scale, alpha)
    att = (z * sig * weight).astype(jnp.bfloat16)
    out = jnp.einsum("hqk,khd->qhd", att, value, preferred_element_type=jnp.float32)
    dprod = jnp.einsum("qhd,khd->hqk", grad, value, preferred_element_type=jnp.float32)
    dsc = (dprod * sig * (1.0 + z * (1.0 - sig)) * weight * alpha).astype(jnp.bfloat16)
    dquery = jnp.einsum("hqk,khd->qhd", dsc, key, preferred_element_type=jnp.float32)
    return out, dquery, att, dsc


def backward_terms(query, grad, key, value, valid, scale, alpha):
    z, sig, weight = scores(query, key, valid, scale, alpha)
    att = (z * sig * weight).astype(jnp.bfloat16)
    dprod = jnp.einsum("qhd,khd->hqk", grad, value, preferred_element_type=jnp.float32)
    dsc = (dprod * sig * (1.0 + z * (1.0 - sig)) * weight * alpha).astype(jnp.bfloat16)
    dkey = jnp.einsum("hqk,qhd->khd", dsc, query, preferred_element_type=jnp.float32)
    dvalue = jnp.einsum("hqk,qhd->khd", att, grad, preferred_element_type=jnp.float32)
    return dkey, dvalue


def body(events, w_query, w_key, values, grad_out, lengths, stream_shift, block_keep):
    rows = events.shape[1]
    features = w_query.shape[1]
    nheads = features // HD
    alpha = 1.0 / HD**0.5
    scale = 1.0 / MAXLEN**0.5
    local = events[0]
    queries = jnp.dot(local, w_query, preferred_element_type=jnp.float32).astype(jnp.bfloat16)
    keys = jnp.dot(local, w_key, preferred_element_type=jnp.float32).astype(jnp.bfloat16)
    cycle_size = lax.axis_size("ctx")
    myself = lax.axis_index("ctx")
    total = rows * cycle_size
    ends = jnp.cumsum(lengths[0])
    offset = stream_shift[0]
    keep = block_keep[0]
    blocks_all = jnp.arange(keep.shape[0], dtype=jnp.int32)
    within = jnp.arange(rows, dtype=jnp.int32)

    def describe(anchor):
        anchor = jnp.remainder(anchor, cycle_size)
        position = jnp.remainder(anchor * rows + within - offset, total)
        owner = jnp.sum((position[:, None] >= ends[None, :]).astype(jnp.int32), axis=1)
        which = position // BLOCK
        kept = (
            jnp.sum(jnp.where(which[:, None] == blocks_all[None, :], keep[None, :], 0), axis=1) > 0
        )
        return (position, owner, kept)

    def mask(qinfo, kinfo):
        return (
            (qinfo[1][:, None] == kinfo[1][None, :])
            & (kinfo[0][None, :] <= qinfo[0][:, None])
            & kinfo[2][None, :]
        )

    def split(packed):
        return (
            packed[:, :features].reshape(rows, nheads, HD),
            packed[:, features:].reshape(rows, nheads, HD),
        )

    share = local.shape[1] // cycle_size
    own_events = select_features(local, share, myself % 2)
    other_events = exchange(select_features(local, share, 1 - myself % 2), "ctx", 1)
    kv = jnp.concatenate([keys, values[0]], axis=1)
    qg = jnp.concatenate([queries, grad_out[0]], axis=1)
    kv_from, kv_anchor = relayed(kv, myself, 1)
    qg_from, qg_anchor = relayed(qg, myself, -1)

    described = [describe(anchor) for anchor in [myself] + kv_anchor + qg_anchor]
    infor = jnp.stack(
        [d[0] for d in described] + [d[1] for d in described] + [d[2].astype(jnp.int32) for d in described]
    ).astype(jnp.int32)
    infoc = infor.T
    out_b, joined, dv_b = attention_tiles(
        [qg] + qg_from[1:], [kv] + kv_from[1:], infoc, infor, nheads, alpha, scale
    )
    attended = out_b.reshape(1, rows, features)
    grad_values = dv_b.reshape(1, rows, features)
    mine = reduce_rows(own_events, other_events, joined, share)
    grad_wq = mine[:, :features].astype(jnp.bfloat16)
    grad_wk = mine[:, features:].astype(jnp.bfloat16)
    return (attended, grad_values, grad_wq, grad_wk)


def solution(mesh):
    placed = (
        P("dp", "ctx", None),
        P(),
        P(),
        P("dp", "ctx", None),
        P("dp", "ctx", None),
        P("dp", None),
        P("dp"),
        P("dp", None),
    )
    return jax.shard_map(
        body,
        mesh=mesh,
        in_specs=placed,
        out_specs=(P("dp", "ctx", None), P("dp", "ctx", None), P("ctx", None), P("ctx", None)),
        check_vma=False,
    )
```

```python
import jax
import jax.numpy as jnp
from jax import lax
from jax.experimental import pallas as pl
from jax.experimental.pallas import tpu as pltpu
from jax.sharding import PartitionSpec as P
import functools

HD = 128
SPAN = 3
BLOCK = 128
MAXLEN = 768


def shifted(value, axis, steps):
    count = lax.axis_size(axis)
    pairs = [(source, (source + steps) % count) for source in range(count)]
    return lax.ppermute(value, axis, pairs)


def exchange(value, axis, mask):
    count = lax.axis_size(axis)
    return lax.ppermute(value, axis, [(source, source ^ mask) for source in range(count)])


def relayed(value, myself, sign):
    count = lax.axis_size("ctx")
    odd = myself % 2
    pairs = []
    for source in range(count):
        step = 3 if (source % 2 == 1) == (sign > 0) else 1
        pairs.append((source, (source + sign * step) % count))
    far = shifted(value, "ctx", 2 * sign)
    mixed = lax.ppermute(value, "ctx", pairs)
    swapped = exchange(far, "ctx", 1)
    lead = odd if sign > 0 else 1 - odd
    mixed_anchor = myself - sign * (3 - 2 * lead)
    swapped_anchor = myself - sign * (1 + 2 * lead)
    return [None, far, mixed, swapped], [myself - 2 * sign, mixed_anchor, swapped_anchor]


def pick(value, bit, axis):
    return (
        lax.dynamic_index_in_dim(value, bit, axis, keepdims=False),
        lax.dynamic_index_in_dim(value, 1 - bit, axis, keepdims=False),
    )


def reduce_kernel(groups, spread, own_ref, other_ref, joined_ref, wq_ref, wk_ref, joined_land, part_ref, sent, landed, sums, mixed, finals, sems):
    me = lax.axis_index("ctx")
    group = lax.axis_index("dp")
    core = me % 2
    slot = me // 2
    mesh_id = pl.DeviceIdType.MESH
    barrier = pltpu.get_barrier_semaphore()
    for step in range(1, groups):
        peer = 2 * ((slot + step) % groups) + core
        pl.semaphore_signal(barrier, inc=1, device_id=(group, peer), device_id_type=mesh_id)
    for step in range(1, spread):
        pl.semaphore_signal(barrier, inc=1, device_id=((group + step) % spread, me), device_id_type=mesh_id)
    partner = me + 1 - 2 * core
    pl.semaphore_signal(barrier, inc=1, device_id=(group, partner), device_id_type=mesh_id)
    pl.semaphore_wait(barrier, groups - 1 + spread - 1 + 1)
    pair = pltpu.make_async_remote_copy(
        src_ref=joined_ref,
        dst_ref=joined_land,
        send_sem=sems.at[6, 0],
        recv_sem=sems.at[6, 1],
        device_id=(group, partner),
        device_id_type=mesh_id,
    )
    pair.start()
    contract = (((0,), (0,)), ((), ()))
    accs = [
        lax.dot_general(own_ref[...], joined_ref[half], contract, preferred_element_type=jnp.float32)
        for half in range(2)
    ]
    pair.wait()
    accs = [
        accs[half] + lax.dot_general(other_ref[...], joined_land[half], contract, preferred_element_type=jnp.float32)
        for half in range(2)
    ]
    _, _, share, lanes = part_ref.shape
    features = joined_ref.shape[2]
    for index in range(spread):
        half, column = divmod(index * lanes, features)
        part_ref[index] = accs[half][:, column:column + lanes].reshape(groups, share, lanes)
    sent[...] = part_ref[...].astype(sent.dtype)
    copies = []
    for step in range(1, spread):
        target = (group + step) % spread
        copy = pltpu.make_async_remote_copy(
            src_ref=sent.at[target],
            dst_ref=landed.at[group],
            send_sem=sems.at[0, step - 1],
            recv_sem=sems.at[1, step - 1],
            device_id=(target, me),
            device_id_type=mesh_id,
        )
        copy.start()
        copies.append(copy)
    for copy in copies:
        copy.wait()
    total = part_ref[group]
    for step in range(1, spread):
        total = total + landed[(group + spread - step) % spread].astype(jnp.float32)
    sums[...] = total.astype(sums.dtype)
    copies = []
    for step in range(1, groups):
        target = (slot + step) % groups
        copy = pltpu.make_async_remote_copy(
            src_ref=sums.at[target],
            dst_ref=mixed.at[slot],
            send_sem=sems.at[2, step - 1],
            recv_sem=sems.at[3, step - 1],
            device_id=(group, 2 * target + core),
            device_id_type=mesh_id,
        )
        copy.start()
        copies.append(copy)
    for copy in copies:
        copy.wait()
    result = part_ref[group, slot]
    for step in range(1, spread):
        result = result + landed[(group + spread - step) % spread, slot].astype(jnp.float32)
    for step in range(1, groups):
        result = result + mixed[(slot + groups - step) % groups].astype(jnp.float32)
    finals[group] = result
    copies = []
    for step in range(1, spread):
        target = (group + step) % spread
        copy = pltpu.make_async_remote_copy(
            src_ref=finals.at[group],
            dst_ref=finals.at[group],
            send_sem=sems.at[4, step - 1],
            recv_sem=sems.at[5, step - 1],
            device_id=(target, me),
            device_id_type=mesh_id,
        )
        copy.start()
        copies.append(copy)
    for copy in copies:
        copy.wait()
    for index in range(spread):
        half, column = divmod(index * lanes, features)
        target = (wq_ref, wk_ref)[half]
        target[:, column:column + lanes] = finals[index].astype(target.dtype)


def reduce_blocks(own, other, joined, share, spread):
    _, rows, features = joined.shape
    width = 2 * features
    groups = own.shape[1] // share
    lanes = width // spread
    vmem = pl.BlockSpec(memory_space=pltpu.VMEM)
    return pl.pallas_call(
        functools.partial(reduce_kernel, groups, spread),
        in_specs=[vmem, vmem, vmem],
        out_specs=[vmem, vmem],
        out_shape=[jax.ShapeDtypeStruct((share, features), jnp.bfloat16)] * 2,
        scratch_shapes=[
            pltpu.VMEM((2, rows, features), jnp.bfloat16),
            pltpu.VMEM((spread, groups, share, lanes), jnp.float32),
            pltpu.VMEM((spread, groups, share, lanes), jnp.bfloat16),
            pltpu.VMEM((spread, groups, share, lanes), jnp.bfloat16),
            pltpu.VMEM((groups, share, lanes), jnp.bfloat16),
            pltpu.VMEM((groups, share, lanes), jnp.bfloat16),
            pltpu.VMEM((spread, share, lanes), jnp.float32),
            pltpu.SemaphoreType.DMA((7, max(groups, spread))),
        ],
        compiler_params=pltpu.CompilerParams(collective_id=1, has_side_effects=True),
    )(own, other, joined)


def select_features(events, share, bit):
    width = events.shape[1]
    halves = events.reshape(events.shape[0], width // (2 * share), 2, share)
    return lax.dynamic_index_in_dim(halves, bit, 2, keepdims=False).reshape(events.shape[0], width // 2)


def reduce_rows(own, other, joined, share):
    acc = reduce_blocks(own, other, joined, share, lax.axis_size("dp"))
    return acc


def tiles_kernel(span, alpha, scale, infoc, infor, *refs):
    count = 2 * span + 2
    qs = refs[0:count:2]
    gs = refs[1:count:2]
    ks = refs[count:2 * count:2]
    vs = refs[count + 1:2 * count:2]
    out_ref, dqk_ref, dv_ref = refs[2 * count:]
    lanes = 2 * span + 1

    def valid(qa, ka):
        qpos = infoc[:, qa:qa + 1]
        quser = infoc[:, lanes + qa:lanes + qa + 1]
        kpos = infor[ka:ka + 1, :]
        kuser = infor[lanes + ka:lanes + ka + 1, :]
        kkept = infor[2 * lanes + ka:2 * lanes + ka + 1, :]
        return (quser == kuser) & (kpos <= qpos) & (kkept > 0)

    def terms(q, g, k, v, ok):
        z = lax.dot_general(q, k, (((1,), (1,)), ((), ())), preferred_element_type=jnp.float32) * alpha
        sig = 1.0 / (1.0 + jnp.exp(-z))
        weight = jnp.where(ok, scale, 0.0)
        att = (z * sig * weight).astype(jnp.bfloat16)
        dprod = lax.dot_general(g, v, (((1,), (1,)), ((), ())), preferred_element_type=jnp.float32)
        dsc = (dprod * sig * (1.0 + z * (1.0 - sig)) * weight * alpha).astype(jnp.bfloat16)
        return att, dsc

    def back(att, dsc, q, g):
        dk = lax.dot_general(dsc, q, (((0,), (0,)), ((), ())), preferred_element_type=jnp.float32)
        dv = lax.dot_general(att, g, (((0,), (0,)), ((), ())), preferred_element_type=jnp.float32)
        return dk, dv

    q0, g0, k0, v0 = qs[0][...], gs[0][...], ks[0][...], vs[0][...]
    att, dsc = terms(q0, g0, k0, v0, valid(0, 0))
    out = jnp.dot(att, v0, preferred_element_type=jnp.float32)
    dq = jnp.dot(dsc, k0, preferred_element_type=jnp.float32)
    dk, dv = back(att, dsc, q0, g0)
    for step in range(1, span + 1):
        k, v = ks[step][...], vs[step][...]
        att, dsc = terms(q0, g0, k, v, valid(0, step))
        out = out + jnp.dot(att, v, preferred_element_type=jnp.float32)
        dq = dq + jnp.dot(dsc, k, preferred_element_type=jnp.float32)
        q, g = qs[step][...], gs[step][...]
        att, dsc = terms(q, g, k0, v0, valid(span + step, 0))
        b, c = back(att, dsc, q, g)
        dk = dk + b
        dv = dv + c
    out_ref[...] = out.astype(out_ref.dtype)
    dqk_ref[0] = dq.astype(dqk_ref.dtype)
    dqk_ref[1] = dk.astype(dqk_ref.dtype)
    dv_ref[...] = dv.astype(dv_ref.dtype)


def attention_tiles(qg_list, kv_list, infoc, infor, nheads, alpha, scale):
    rows = qg_list[0].shape[0]
    span = len(qg_list) - 1
    blk = lambda offset: pl.BlockSpec((rows, HD), lambda h: (0, h + offset))
    full = lambda arr: pl.BlockSpec(arr.shape, lambda h: (0, 0))
    operands, specs = [infoc, infor], [full(infoc), full(infor)]
    for group in (qg_list, kv_list):
        for packed in group:
            operands += [packed, packed]
            specs += [blk(0), blk(nheads)]
    shape = jax.ShapeDtypeStruct((rows, nheads * HD), jnp.bfloat16)
    tile = rows * rows * HD * 2
    return pl.pallas_call(
        functools.partial(tiles_kernel, span, alpha, scale),
        grid=(nheads,),
        in_specs=specs,
        out_specs=[blk(0), pl.BlockSpec((2, rows, HD), lambda h: (0, 0, h)), blk(0)],
        out_shape=[shape, jax.ShapeDtypeStruct((2, rows, nheads * HD), jnp.bfloat16), shape],
        cost_estimate=pl.CostEstimate(
            flops=nheads * (2 * span + 1) * 5 * tile,
            transcendentals=nheads * (2 * span + 1) * rows * rows,
            bytes_accessed=(2 * span + 2) * 2 * rows * nheads * HD * 2 * 2 + 4 * rows * nheads * HD * 2,
        ),
    )(*operands)


def scores(query, key, valid, scale, alpha):
    z = jnp.einsum("qhd,khd->hqk", query, key, preferred_element_type=jnp.float32) * alpha
    sig = jax.nn.sigmoid(z)
    weight = valid[None, :, :].astype(jnp.float32) * scale
    return z, sig, weight


def forward_terms(query, grad, key, value, valid, scale, alpha):
    z, sig, weight = scores(query, key, valid, scale, alpha)
    att = (z * sig * weight).astype(jnp.bfloat16)
    out = jnp.einsum("hqk,khd->qhd", att, value, preferred_element_type=jnp.float32)
    dprod = jnp.einsum("qhd,khd->hqk", grad, value, preferred_element_type=jnp.float32)
    dsc = (dprod * sig * (1.0 + z * (1.0 - sig)) * weight * alpha).astype(jnp.bfloat16)
    dquery = jnp.einsum("hqk,khd->qhd", dsc, key, preferred_element_type=jnp.float32)
    return out, dquery, att, dsc


def backward_terms(query, grad, key, value, valid, scale, alpha):
    z, sig, weight = scores(query, key, valid, scale, alpha)
    att = (z * sig * weight).astype(jnp.bfloat16)
    dprod = jnp.einsum("qhd,khd->hqk", grad, value, preferred_element_type=jnp.float32)
    dsc = (dprod * sig * (1.0 + z * (1.0 - sig)) * weight * alpha).astype(jnp.bfloat16)
    dkey = jnp.einsum("hqk,qhd->khd", dsc, query, preferred_element_type=jnp.float32)
    dvalue = jnp.einsum("hqk,qhd->khd", att, grad, preferred_element_type=jnp.float32)
    return dkey, dvalue


def body(events, w_query, w_key, values, grad_out, lengths, stream_shift, block_keep):
    rows = events.shape[1]
    features = w_query.shape[1]
    nheads = features // HD
    alpha = 1.0 / HD**0.5
    scale = 1.0 / MAXLEN**0.5
    local = events[0]
    queries = jnp.dot(local, w_query, preferred_element_type=jnp.float32).astype(jnp.bfloat16)
    keys = jnp.dot(local, w_key, preferred_element_type=jnp.float32).astype(jnp.bfloat16)
    cycle_size = lax.axis_size("ctx")
    myself = lax.axis_index("ctx")
    total = rows * cycle_size
    ends = jnp.cumsum(lengths[0])
    offset = stream_shift[0]
    keep = block_keep[0]
    blocks_all = jnp.arange(keep.shape[0], dtype=jnp.int32)
    within = jnp.arange(rows, dtype=jnp.int32)

    def describe(anchor):
        anchor = jnp.remainder(anchor, cycle_size)
        position = jnp.remainder(anchor * rows + within - offset, total)
        owner = jnp.sum((position[:, None] >= ends[None, :]).astype(jnp.int32), axis=1)
        which = position // BLOCK
        kept = (
            jnp.sum(jnp.where(which[:, None] == blocks_all[None, :], keep[None, :], 0), axis=1) > 0
        )
        return (position, owner, kept)

    def mask(qinfo, kinfo):
        return (
            (qinfo[1][:, None] == kinfo[1][None, :])
            & (kinfo[0][None, :] <= qinfo[0][:, None])
            & kinfo[2][None, :]
        )

    def split(packed):
        return (
            packed[:, :features].reshape(rows, nheads, HD),
            packed[:, features:].reshape(rows, nheads, HD),
        )

    share = local.shape[1] // cycle_size
    own_events = select_features(local, share, myself % 2)
    other_events = exchange(select_features(local, share, 1 - myself % 2), "ctx", 1)
    kv = jnp.concatenate([keys, values[0]], axis=1)
    qg = jnp.concatenate([queries, grad_out[0]], axis=1)
    kv_from, kv_anchor = relayed(kv, myself, 1)
    qg_from, qg_anchor = relayed(qg, myself, -1)

    described = [describe(anchor) for anchor in [myself] + kv_anchor + qg_anchor]
    infor = jnp.stack(
        [d[0] for d in described] + [d[1] for d in described] + [d[2].astype(jnp.int32) for d in described]
    ).astype(jnp.int32)
    infoc = infor.T
    out_b, joined, dv_b = attention_tiles(
        [qg] + qg_from[1:], [kv] + kv_from[1:], infoc, infor, nheads, alpha, scale
    )
    attended = out_b.reshape(1, rows, features)
    grad_values = dv_b.reshape(1, rows, features)
    grad_wq, grad_wk = reduce_rows(own_events, other_events, joined, share)
    return (attended, grad_values, grad_wq, grad_wk)


def solution(mesh):
    placed = (
        P("dp", "ctx", None),
        P(),
        P(),
        P("dp", "ctx", None),
        P("dp", "ctx", None),
        P("dp", None),
        P("dp"),
        P("dp", None),
    )
    return jax.shard_map(
        body,
        mesh=mesh,
        in_specs=placed,
        out_specs=(P("dp", "ctx", None), P("dp", "ctx", None), P("ctx", None), P("ctx", None)),
        check_vma=False,
    )
```

```python
import jax
import jax.numpy as jnp
from jax import lax
from jax.experimental import pallas as pl
from jax.experimental.pallas import tpu as pltpu
from jax.sharding import PartitionSpec as P
import functools

HD = 128
SPAN = 3
BLOCK = 128
MAXLEN = 768


def shifted(value, axis, steps):
    count = lax.axis_size(axis)
    pairs = [(source, (source + steps) % count) for source in range(count)]
    return lax.ppermute(value, axis, pairs)


def exchange(value, axis, mask):
    count = lax.axis_size(axis)
    return lax.ppermute(value, axis, [(source, source ^ mask) for source in range(count)])


def relayed(value, myself, sign):
    count = lax.axis_size("ctx")
    odd = myself % 2
    pairs = []
    for source in range(count):
        step = 3 if (source % 2 == 1) == (sign > 0) else 1
        pairs.append((source, (source + sign * step) % count))
    far = shifted(value, "ctx", 2 * sign)
    mixed = lax.ppermute(value, "ctx", pairs)
    swapped = exchange(far, "ctx", 1)
    lead = odd if sign > 0 else 1 - odd
    mixed_anchor = myself - sign * (3 - 2 * lead)
    swapped_anchor = myself - sign * (1 + 2 * lead)
    return [None, far, mixed, swapped], [myself - 2 * sign, mixed_anchor, swapped_anchor]


def pick(value, bit, axis):
    return (
        lax.dynamic_index_in_dim(value, bit, axis, keepdims=False),
        lax.dynamic_index_in_dim(value, 1 - bit, axis, keepdims=False),
    )


def reduce_kernel(groups, spread, own_ref, other_ref, joined_ref, wq_ref, wk_ref, joined_land, part_ref, sent, landed, sums, mixed, finals, sems):
    me = lax.axis_index("ctx")
    group = lax.axis_index("dp")
    core = me % 2
    slot = me // 2
    mesh_id = pl.DeviceIdType.MESH
    barrier = pltpu.get_barrier_semaphore()
    for step in range(1, groups):
        peer = 2 * ((slot + step) % groups) + core
        pl.semaphore_signal(barrier, inc=1, device_id=(group, peer), device_id_type=mesh_id)
    for step in range(1, spread):
        pl.semaphore_signal(barrier, inc=1, device_id=((group + step) % spread, me), device_id_type=mesh_id)
    partner = me + 1 - 2 * core
    pl.semaphore_signal(barrier, inc=1, device_id=(group, partner), device_id_type=mesh_id)
    pl.semaphore_wait(barrier, groups - 1 + spread - 1 + 1)
    pair = pltpu.make_async_remote_copy(
        src_ref=joined_ref,
        dst_ref=joined_land,
        send_sem=sems.at[6, 0],
        recv_sem=sems.at[6, 1],
        device_id=(group, partner),
        device_id_type=mesh_id,
    )
    pair.start()
    contract = (((0,), (0,)), ((), ()))
    accs = [
        lax.dot_general(own_ref[...], joined_ref[half], contract, preferred_element_type=jnp.float32)
        for half in range(2)
    ]
    pair.wait()
    accs = [
        accs[half] + lax.dot_general(other_ref[...], joined_land[half], contract, preferred_element_type=jnp.float32)
        for half in range(2)
    ]
    _, _, share, lanes = part_ref.shape
    features = joined_ref.shape[2]
    for index in range(spread):
        half, column = divmod(index * lanes, features)
        part_ref[index] = accs[half][:, column:column + lanes].reshape(groups, share, lanes)
    sent[...] = part_ref[...].astype(sent.dtype)
    copies = []
    for step in range(1, spread):
        target = (group + step) % spread
        copy = pltpu.make_async_remote_copy(
            src_ref=sent.at[target],
            dst_ref=landed.at[group],
            send_sem=sems.at[0, step - 1],
            recv_sem=sems.at[1, step - 1],
            device_id=(target, me),
            device_id_type=mesh_id,
        )
        copy.start()
        copies.append(copy)
    for copy in copies:
        copy.wait()
    total = part_ref[group]
    for step in range(1, spread):
        total = total + landed[(group + spread - step) % spread].astype(jnp.float32)
    sums[...] = total.astype(sums.dtype)
    copies = []
    for step in range(1, groups):
        target = (slot + step) % groups
        copy = pltpu.make_async_remote_copy(
            src_ref=sums.at[target],
            dst_ref=mixed.at[slot],
            send_sem=sems.at[2, step - 1],
            recv_sem=sems.at[3, step - 1],
            device_id=(group, 2 * target + core),
            device_id_type=mesh_id,
        )
        copy.start()
        copies.append(copy)
    for copy in copies:
        copy.wait()
    result = part_ref[group, slot]
    for step in range(1, spread):
        result = result + landed[(group + spread - step) % spread, slot].astype(jnp.float32)
    for step in range(1, groups):
        result = result + mixed[(slot + groups - step) % groups].astype(jnp.float32)
    finals[group] = result
    copies = []
    for step in range(1, spread):
        target = (group + step) % spread
        copy = pltpu.make_async_remote_copy(
            src_ref=finals.at[group],
            dst_ref=finals.at[group],
            send_sem=sems.at[4, step - 1],
            recv_sem=sems.at[5, step - 1],
            device_id=(target, me),
            device_id_type=mesh_id,
        )
        copy.start()
        copies.append(copy)
    for copy in copies:
        copy.wait()
    for index in range(spread):
        half, column = divmod(index * lanes, features)
        target = (wq_ref, wk_ref)[half]
        target[:, column:column + lanes] = finals[index].astype(target.dtype)


def reduce_blocks(own, other, joined, share, spread):
    _, rows, features = joined.shape
    width = 2 * features
    groups = own.shape[1] // share
    lanes = width // spread
    vmem = pl.BlockSpec(memory_space=pltpu.VMEM)
    return pl.pallas_call(
        functools.partial(reduce_kernel, groups, spread),
        in_specs=[vmem, vmem, vmem],
        out_specs=[vmem, vmem],
        out_shape=[jax.ShapeDtypeStruct((share, features), jnp.bfloat16)] * 2,
        scratch_shapes=[
            pltpu.VMEM((2, rows, features), jnp.bfloat16),
            pltpu.VMEM((spread, groups, share, lanes), jnp.float32),
            pltpu.VMEM((spread, groups, share, lanes), jnp.bfloat16),
            pltpu.VMEM((spread, groups, share, lanes), jnp.bfloat16),
            pltpu.VMEM((groups, share, lanes), jnp.bfloat16),
            pltpu.VMEM((groups, share, lanes), jnp.bfloat16),
            pltpu.VMEM((spread, share, lanes), jnp.float32),
            pltpu.SemaphoreType.DMA((7, max(groups, spread))),
        ],
        compiler_params=pltpu.CompilerParams(collective_id=1, has_side_effects=True),
    )(own, other, joined)


def select_features(events, share, bit):
    width = events.shape[1]
    halves = events.reshape(events.shape[0], width // (2 * share), 2, share)
    return lax.dynamic_index_in_dim(halves, bit, 2, keepdims=False).reshape(events.shape[0], width // 2)


def reduce_rows(own, other, joined, share):
    acc = reduce_blocks(own, other, joined, share, lax.axis_size("dp"))
    return acc


def tiles_kernel(span, alpha, scale, infoc, infor, *refs):
    count = 2 * span + 2
    qs = refs[0:count:2]
    gs = refs[1:count:2]
    ks = refs[count:2 * count:2]
    vs = refs[count + 1:2 * count:2]
    out_ref, dqk_ref, dv_ref = refs[2 * count:]
    lanes = 2 * span + 1

    def valid(qa, ka):
        qpos = infoc[:, qa:qa + 1]
        quser = infoc[:, lanes + qa:lanes + qa + 1]
        kpos = infor[ka:ka + 1, :]
        kuser = infor[lanes + ka:lanes + ka + 1, :]
        kkept = infor[2 * lanes + ka:2 * lanes + ka + 1, :]
        return (quser == kuser) & (kpos <= qpos) & (kkept > 0)

    def terms(q, g, k, v, ok):
        z = lax.dot_general(q, k, (((1,), (1,)), ((), ())), preferred_element_type=jnp.float32) * alpha
        sig = 1.0 / (1.0 + jnp.exp(-z))
        weight = jnp.where(ok, scale, 0.0)
        att = (z * sig * weight).astype(jnp.bfloat16)
        dprod = lax.dot_general(g, v, (((1,), (1,)), ((), ())), preferred_element_type=jnp.float32)
        dsc = (dprod * sig * (1.0 + z * (1.0 - sig)) * weight * alpha).astype(jnp.bfloat16)
        return att, dsc

    def back(att, dsc, q, g):
        dk = lax.dot_general(dsc, q, (((0,), (0,)), ((), ())), preferred_element_type=jnp.float32)
        dv = lax.dot_general(att, g, (((0,), (0,)), ((), ())), preferred_element_type=jnp.float32)
        return dk, dv

    q0, g0, k0, v0 = qs[0][...], gs[0][...], ks[0][...], vs[0][...]
    att, dsc = terms(q0, g0, k0, v0, valid(0, 0))
    out = jnp.dot(att, v0, preferred_element_type=jnp.float32)
    dq = jnp.dot(dsc, k0, preferred_element_type=jnp.float32)
    dk, dv = back(att, dsc, q0, g0)
    for step in range(1, span + 1):
        k, v = ks[step][...], vs[step][...]
        att, dsc = terms(q0, g0, k, v, valid(0, step))
        out = out + jnp.dot(att, v, preferred_element_type=jnp.float32)
        dq = dq + jnp.dot(dsc, k, preferred_element_type=jnp.float32)
        q, g = qs[step][...], gs[step][...]
        att, dsc = terms(q, g, k0, v0, valid(span + step, 0))
        b, c = back(att, dsc, q, g)
        dk = dk + b
        dv = dv + c
    out_ref[...] = out.astype(out_ref.dtype)
    dqk_ref[0] = dq.astype(dqk_ref.dtype)
    dqk_ref[1] = dk.astype(dqk_ref.dtype)
    dv_ref[...] = dv.astype(dv_ref.dtype)


def attention_tiles(qg_list, kv_list, infoc, infor, nheads, alpha, scale):
    rows = qg_list[0].shape[0]
    span = len(qg_list) - 1
    blk = lambda offset: pl.BlockSpec((rows, HD), lambda h: (0, h + offset))
    full = lambda arr: pl.BlockSpec(arr.shape, lambda h: (0, 0))
    operands, specs = [infoc, infor], [full(infoc), full(infor)]
    for group in (qg_list, kv_list):
        for packed in group:
            operands += [packed, packed]
            specs += [blk(0), blk(nheads)]
    shape = jax.ShapeDtypeStruct((rows, nheads * HD), jnp.bfloat16)
    tile = rows * rows * HD * 2
    return pl.pallas_call(
        functools.partial(tiles_kernel, span, alpha, scale),
        grid=(nheads,),
        in_specs=specs,
        out_specs=[blk(0), pl.BlockSpec((2, rows, HD), lambda h: (0, 0, h)), blk(0)],
        out_shape=[shape, jax.ShapeDtypeStruct((2, rows, nheads * HD), jnp.bfloat16), shape],
        cost_estimate=pl.CostEstimate(
            flops=nheads * (2 * span + 1) * 5 * tile,
            transcendentals=nheads * (2 * span + 1) * rows * rows,
            bytes_accessed=(2 * span + 2) * 2 * rows * nheads * HD * 2 * 2 + 4 * rows * nheads * HD * 2,
        ),
    )(*operands)


def scores(query, key, valid, scale, alpha):
    z = jnp.einsum("qhd,khd->hqk", query, key, preferred_element_type=jnp.float32) * alpha
    sig = jax.nn.sigmoid(z)
    weight = valid[None, :, :].astype(jnp.float32) * scale
    return z, sig, weight


def forward_terms(query, grad, key, value, valid, scale, alpha):
    z, sig, weight = scores(query, key, valid, scale, alpha)
    att = (z * sig * weight).astype(jnp.bfloat16)
    out = jnp.einsum("hqk,khd->qhd", att, value, preferred_element_type=jnp.float32)
    dprod = jnp.einsum("qhd,khd->hqk", grad, value, preferred_element_type=jnp.float32)
    dsc = (dprod * sig * (1.0 + z * (1.0 - sig)) * weight * alpha).astype(jnp.bfloat16)
    dquery = jnp.einsum("hqk,khd->qhd", dsc, key, preferred_element_type=jnp.float32)
    return out, dquery, att, dsc


def backward_terms(query, grad, key, value, valid, scale, alpha):
    z, sig, weight = scores(query, key, valid, scale, alpha)
    att = (z * sig * weight).astype(jnp.bfloat16)
    dprod = jnp.einsum("qhd,khd->hqk", grad, value, preferred_element_type=jnp.float32)
    dsc = (dprod * sig * (1.0 + z * (1.0 - sig)) * weight * alpha).astype(jnp.bfloat16)
    dkey = jnp.einsum("hqk,qhd->khd", dsc, query, preferred_element_type=jnp.float32)
    dvalue = jnp.einsum("hqk,qhd->khd", att, grad, preferred_element_type=jnp.float32)
    return dkey, dvalue


def body(events, w_query, w_key, values, grad_out, lengths, stream_shift, block_keep):
    rows = events.shape[1]
    features = w_query.shape[1]
    nheads = features // HD
    alpha = 1.0 / HD**0.5
    scale = 1.0 / MAXLEN**0.5
    local = events[0]
    queries = jnp.dot(local, w_query, preferred_element_type=jnp.float32).astype(jnp.bfloat16)
    keys = jnp.dot(local, w_key, preferred_element_type=jnp.float32).astype(jnp.bfloat16)
    cycle_size = lax.axis_size("ctx")
    myself = lax.axis_index("ctx")
    total = rows * cycle_size
    ends = jnp.cumsum(lengths[0])
    offset = stream_shift[0]
    keep = block_keep[0]
    blocks_all = jnp.arange(keep.shape[0], dtype=jnp.int32)
    within = jnp.arange(rows, dtype=jnp.int32)

    def describe(anchor):
        anchor = jnp.remainder(anchor, cycle_size)
        position = jnp.remainder(anchor * rows + within - offset, total)
        owner = jnp.sum((position[:, None] >= ends[None, :]).astype(jnp.int32), axis=1)
        which = position // BLOCK
        kept = (
            jnp.sum(jnp.where(which[:, None] == blocks_all[None, :], keep[None, :], 0), axis=1) > 0
        )
        return (position, owner, kept)

    def mask(qinfo, kinfo):
        return (
            (qinfo[1][:, None] == kinfo[1][None, :])
            & (kinfo[0][None, :] <= qinfo[0][:, None])
            & kinfo[2][None, :]
        )

    def split(packed):
        return (
            packed[:, :features].reshape(rows, nheads, HD),
            packed[:, features:].reshape(rows, nheads, HD),
        )

    share = local.shape[1] // cycle_size
    own_events = select_features(local, share, myself % 2)
    other_events = exchange(select_features(local, share, 1 - myself % 2), "ctx", 1)
    kv = jnp.concatenate([keys, values[0]], axis=1)
    qg = jnp.concatenate([queries, grad_out[0]], axis=1)
    kv_from, kv_anchor = relayed(kv, myself, 1)
    qg_from, qg_anchor = relayed(qg, myself, -1)

    described = [describe(anchor) for anchor in [myself] + kv_anchor + qg_anchor]
    columns = [d[0] for d in described] + [d[1] for d in described] + [d[2].astype(jnp.int32) for d in described]
    infor = jnp.stack(columns).astype(jnp.int32)
    infoc = jnp.stack(columns, axis=1).astype(jnp.int32)
    out_b, joined, dv_b = attention_tiles(
        [qg] + qg_from[1:], [kv] + kv_from[1:], infoc, infor, nheads, alpha, scale
    )
    attended = out_b.reshape(1, rows, features)
    grad_values = dv_b.reshape(1, rows, features)
    grad_wq, grad_wk = reduce_rows(own_events, other_events, joined, share)
    return (attended, grad_values, grad_wq, grad_wk)


def solution(mesh):
    placed = (
        P("dp", "ctx", None),
        P(),
        P(),
        P("dp", "ctx", None),
        P("dp", "ctx", None),
        P("dp", None),
        P("dp"),
        P("dp", None),
    )
    return jax.shard_map(
        body,
        mesh=mesh,
        in_specs=placed,
        out_specs=(P("dp", "ctx", None), P("dp", "ctx", None), P("ctx", None), P("ctx", None)),
        check_vma=False,
    )
```
